32 devices in a mesh: grp: 2 (over x), ctx: 8 (over z, y), ch: 2 (over core).
Axes of the slice: x: 2, y: 2, z: 4, core: 2. Of those that a mesh axis runs over, the one named last changes fastest.
Arguments:
- query_in: bfloat16 [2048, 4096], P(('grp', 'ctx'), 'ch'), parts along dimension 0, may hold values from -6 to 6
- key_in: bfloat16 [2048, 4096], P(('grp', 'ctx'), 'ch'), parts along dimension 0, may hold values from -6 to 6
- value_in: bfloat16 [2048, 4096], P(('grp', 'ctx'), 'ch'), parts along dimension 0, may hold values from -6 to 6
- short_filter: float32 [3, 3, 4096], P(None, None, 'ch'), may hold values from -3 to 3
- skip_bias: float32 [4096], P('ch'), may hold values from -4 to 4
- filter_spectrum: float32 [2, 8, 2, 128, 256], P(None, 'ctx', None, None, 'ch'), may hold values from -6 to 6, as said below
Outputs:
- hyena_out: bfloat16 [2048, 4096], P(('grp', 'ctx'), 'ch'), parts along dimension 0
The draws below stay inside these ranges and needn't reach their ends.
There are 2 independent parts, one for each index of `grp`. The reference program is written for one: setup_inputs(seed, part) draws one part's arguments, and reference() takes and returns one part's arrays. A program takes and returns all parts, laid end to end along the dimension named above; an argument that names none is the same for every part. Nothing has to cross between parts.
Inputs may be any that keep to these rules, and one draw needn't show every extreme that they name: `filter_spectrum`: for each group the entries at frequencies f and 2048 - f (f = 0 with itself) have equal real parts and opposite imaginary parts, as the spectrum of a real filter.
All inputs are finite; a program needn't handle non-finite values.
Results may differ from the reference program's by a relative error of at most 0.001.
Values may be sent and summed in bfloat16 or wider, within the bound.
A program may use at most 64 MiB of HBM per device.

```python
import jax
import jax.numpy as jnp
import numpy as np
from jax import lax

C = 4096
SHORT = 3
TOK_DEV = 128
L = 1024
GROUPS = 256
N_CTX = 8


def reversed_bits_drawn(number, digits):
    result = number * 0
    for bit_level in range(digits):
        result = result + (number >> bit_level & 1) * (1 << digits - 1 - bit_level)
    return result


def draw_filter_spectrum(key, part):
    levels = N_CTX.bit_length() - 1
    total = 2 * TOK_DEV * N_CTX
    key_real = jax.random.fold_in(key, 101)
    key_imag = jax.random.fold_in(key, 202)
    base_real = jax.random.truncated_normal(key_real, -4.0, 4.0, (total, GROUPS), jnp.float32)
    base_imag = jax.random.truncated_normal(key_imag, -4.0, 4.0, (total, GROUPS), jnp.float32)
    frequency = jnp.arange(total, dtype=jnp.int32)
    mirror = (total - frequency) % total
    herm_real = (base_real + base_real[mirror]) * 0.70710678
    herm_imag = (base_imag - base_imag[mirror]) * 0.70710678
    block_ids = reversed_bits_drawn(jnp.arange(N_CTX, dtype=jnp.int32), levels)
    position = 2 * (block_ids[:, None, None] + N_CTX * jnp.arange(TOK_DEV, dtype=jnp.int32)[None, None, :]) + jnp.arange(2, dtype=jnp.int32)[None, :, None]
    return jnp.stack((herm_real[position], herm_imag[position]))


def block_levels(key, extent, split, smallest, high):
    def one(axis_at, blocks):
        draws = jax.random.uniform(jax.random.fold_in(jax.random.fold_in(key, 6), axis_at), (blocks,), jnp.float32, smallest / len(split), high / len(split))
        return jnp.repeat(jnp.exp(draws), extent[axis_at] // blocks).reshape((-1,) + (1,) * (len(extent) - axis_at - 1))

    gain = one(*split[0])
    for cut in split[1:]:
        gain = gain * one(*cut)
    return gain


def centred(own_key, extent, width, reach, cuts=(), kind=jnp.bfloat16):
    entries = jax.random.normal(own_key, extent, jnp.float32) * width
    if len(cuts) > 0:
        entries = block_levels(own_key, extent, cuts, -0.22, 0.18) * entries
    return jnp.clip(entries, min=-reach, max=reach).astype(kind)


def setup_inputs(seed: int = 0, part: int = 0) -> dict:
    keys = jax.random.split(jax.random.key(seed), 7)
    own_keys = jax.random.split(jax.random.fold_in(keys[6], part), 7)
    query_in = centred(own_keys[0], (L, C), 1.0, 6.0, ((0, 8), (1, 2)))
    key_in = centred(own_keys[1], (L, C), 1.0, 6.0, ((0, 8), (1, 2)))
    value_in = centred(own_keys[2], (L, C), 1.0, 6.0, ((0, 8), (1, 2)))
    short_filter = centred(keys[3], (3, SHORT, C), 0.6, 3.0, ((2, 2),), jnp.float32)
    skip_bias = centred(keys[4], (C,), 1.0, 4.0, ((0, 2),), jnp.float32)
    filter_spectrum = draw_filter_spectrum(jax.random.fold_in(keys[6], 71), part)
    return dict(query_in=query_in, key_in=key_in, value_in=value_in, short_filter=short_filter, skip_bias=skip_bias, filter_spectrum=filter_spectrum)


def reversed_bits(number, digits):
    result = number * 0
    for bit_level in range(digits):
        result = result + ((number >> bit_level) & 1) * (1 << (digits - 1 - bit_level))
    return result


def reference(query_in, key_in, value_in, short_filter, skip_bias, filter_spectrum):
    seq_length, chan_width = query_in.shape
    tap_count = short_filter.shape[1]
    stacked = jnp.stack((query_in, key_in, value_in)).astype(jnp.float32)
    padded = jnp.pad(stacked, ((0, 0), (tap_count - 1, 0), (0, 0)))
    filtered = short_filter[:, 0, None, :] * padded[:, tap_count - 1:, :]
    for tap_lag in range(1, tap_count):
        start_row = tap_count - 1 - tap_lag
        filtered = filtered + short_filter[:, tap_lag, None, :] * padded[:, start_row:start_row + seq_length, :]
    gated = filtered[1] * filtered[2]
    parties = filter_spectrum.shape[1]
    tok_rows = filter_spectrum.shape[3]
    group_count = filter_spectrum.shape[4]
    levels = parties.bit_length() - 1
    block_ids = reversed_bits(np.arange(parties), levels)
    freq_index = 2 * (block_ids[:, None, None] + parties * np.arange(tok_rows)[None, None, :]) + np.arange(2)[None, :, None]
    flat_index = jnp.asarray(freq_index.reshape(-1), dtype=jnp.int32)
    total = 2 * seq_length
    spec_real = jnp.zeros((total, group_count), jnp.float32).at[flat_index].set(filter_spectrum[0].reshape(-1, group_count))
    spec_imag = jnp.zeros((total, group_count), jnp.float32).at[flat_index].set(filter_spectrum[1].reshape(-1, group_count))
    per_group = chan_width // group_count
    response = lax.complex(jnp.repeat(spec_real, per_group, axis=1), jnp.repeat(spec_imag, per_group, axis=1))
    forward = jnp.fft.fft(gated, n=total, axis=0)
    conv = jnp.real(jnp.fft.ifft(forward * response, axis=0))[:seq_length]
    return (filtered[0] * (conv + skip_bias[None, :] * gated)).astype(jnp.bfloat16)
```

```python
import functools
import math

import jax
import jax.numpy as jnp
import ml_dtypes
import numpy as np
from jax import lax
from jax.experimental import pallas as pl
from jax.experimental.pallas import tpu as pltpu
from jax.sharding import PartitionSpec as P

HIGHEST = lax.Precision.HIGHEST
MESH = pl.DeviceIdType.MESH
POWER = 17
REACH = 2.0 ** (126 / POWER)


def passed_along(value, axis, steps):
    count = lax.axis_size(axis)
    leading, last = (max(0, -steps), min(count, count - steps))
    return lax.ppermute(value, axis, [(source, source + steps) for source in range(leading, last)])


def reversed_bits(number, digits):
    result = number * 0
    for bit_level in range(digits):
        result = result + (number >> bit_level & 1) * (1 << digits - 1 - bit_level)
    return result


def rotate(real_part, imag_part, cosine, sine):
    return (real_part * cosine - imag_part * sine, real_part * sine + imag_part * cosine)


def complex_product(pattern, table_real, table_imag, data_real, data_imag):
    out_real = jnp.einsum(pattern, table_real, data_real, precision=HIGHEST) - jnp.einsum(
        pattern, table_imag, data_imag, precision=HIGHEST
    )
    out_imag = jnp.einsum(pattern, table_real, data_imag, precision=HIGHEST) + jnp.einsum(
        pattern, table_imag, data_real, precision=HIGHEST
    )
    return (out_real, out_imag)


def angle_table(rows, cols, modulus):
    exponent = (
        jnp.arange(rows, dtype=jnp.int32)[:, None]
        * jnp.arange(cols, dtype=jnp.int32)[None, :]
        % modulus
    )
    angle = 2.0 * math.pi / modulus * exponent.astype(jnp.float32)
    return (jnp.cos(angle), jnp.sin(angle))


def whole_convolution(first_real, first_imag, filter_spectrum, parties, levels):
    tok_rows = first_real.shape[0]
    packed = jnp.stack((first_real, first_imag))
    spread = lax.all_to_all(packed, "ctx", split_axis=2, concat_axis=1, tiled=True)
    spectrum = lax.all_to_all(filter_spectrum, "ctx", split_axis=4, concat_axis=1, tiled=True)
    tail = spectrum.shape[2:]
    spectrum = spectrum.reshape(2, *[2] * levels, *tail)
    spectrum = spectrum.transpose(0, *range(levels, 0, -1), *range(levels + 1, levels + 4))
    spectrum = spectrum.reshape(2, parties, *tail)
    size_b = 2 * parties
    total = tok_rows * size_b
    spectrum = spectrum.reshape(2, size_b, tok_rows, spectrum.shape[4])
    columns = spread.shape[2]
    data = spread.reshape(2, size_b // 2, tok_rows, columns)
    outer_cos, outer_sin = angle_table(size_b, size_b // 2, size_b)
    twist_cos, twist_sin = angle_table(size_b, tok_rows, total)
    inner_cos, inner_sin = angle_table(tok_rows, tok_rows, tok_rows)
    section_real, section_imag = complex_product(
        "fn,nac->fac", outer_cos, -outer_sin, data[0], data[1]
    )
    section_real, section_imag = rotate(
        section_real, section_imag, twist_cos[..., None], -twist_sin[..., None]
    )
    freq_real, freq_imag = complex_product(
        "ak,fac->fkc", inner_cos, -inner_sin, section_real, section_imag
    )
    group_local = spectrum.shape[3]
    per_group = columns // group_local
    shaped_real = freq_real.reshape(size_b, tok_rows, group_local, per_group)
    shaped_imag = freq_imag.reshape(size_b, tok_rows, group_local, per_group)
    resp_real = spectrum[0][..., None]
    resp_imag = spectrum[1][..., None]
    prod_real = (shaped_real * resp_real - shaped_imag * resp_imag).reshape(
        size_b, tok_rows, columns
    )
    prod_imag = (shaped_real * resp_imag + shaped_imag * resp_real).reshape(
        size_b, tok_rows, columns
    )
    back_real, back_imag = complex_product(
        "ak,fkc->fac", inner_cos, inner_sin, prod_real, prod_imag
    )
    back_real, back_imag = rotate(back_real, back_imag, twist_cos[..., None], twist_sin[..., None])
    out_real, out_imag = complex_product(
        "nf,fac->nac", outer_cos.T, outer_sin.T, back_real, back_imag
    )
    norm_factor = 1.0 / total
    result = (
        jnp.stack(
            (
                out_real.reshape(size_b // 2 * tok_rows, columns),
                out_imag.reshape(size_b // 2 * tok_rows, columns),
            )
        )
        * norm_factor
    )
    returned = lax.all_to_all(result, "ctx", split_axis=1, concat_axis=2, tiled=True)
    return (returned[0], returned[1])


def on_device(query_in, key_in, value_in, short_filter, skip_bias, filter_spectrum):
    tok_rows, chan_width = query_in.shape
    parties = lax.axis_size("ctx")
    levels = parties.bit_length() - 1
    tap_count = short_filter.shape[1]
    group_count = filter_spectrum.shape[4]
    half_group = chan_width // (2 * group_count)
    packed_width = group_count * half_group
    stacked = jnp.stack((query_in, key_in, value_in))
    earlier = passed_along(stacked[:, tok_rows - (tap_count - 1) :, :], "ctx", 1)
    extended = jnp.concatenate((earlier, stacked), axis=1).astype(jnp.float32)
    filtered = short_filter[:, 0, None, :] * extended[:, tap_count - 1 :, :]
    for tap_lag in range(1, tap_count):
        start_row = tap_count - 1 - tap_lag
        filtered = (
            filtered
            + short_filter[:, tap_lag, None, :] * extended[:, start_row : start_row + tok_rows, :]
        )
    gated = filtered[1] * filtered[2]
    halves = gated.reshape(tok_rows, group_count, 2, half_group)
    first_real = halves[:, :, 0, :].reshape(tok_rows, packed_width)
    first_imag = halves[:, :, 1, :].reshape(tok_rows, packed_width)
    conv_real, conv_imag = whole_convolution(
        first_real, first_imag, filter_spectrum, parties, levels
    )
    conv = jnp.stack(
        (
            conv_real.reshape(tok_rows, group_count, half_group),
            conv_imag.reshape(tok_rows, group_count, half_group),
        ),
        axis=2,
    ).reshape(tok_rows, chan_width)
    return (filtered[0] * (conv + skip_bias[None, :] * gated)).astype(jnp.bfloat16)


def split_terms(value):
    high = value.astype(jnp.bfloat16)
    low = (value - high.astype(jnp.float32)).astype(jnp.bfloat16)
    return high, low


def encode(value):
    peak = jnp.max(jnp.abs(value), axis=0, keepdims=True)
    scale = jnp.maximum(peak * 1.0078125, 2.0**-100).astype(jnp.bfloat16)
    ratio = value * (REACH / scale.astype(jnp.float32))
    square = ratio * ratio
    fourth = square * square
    eighth = fourth * fourth
    code = (ratio * (eighth * eighth)).astype(jnp.bfloat16)
    return jnp.concatenate((code, jnp.broadcast_to(scale, (8, value.shape[1]))), axis=0)


def decode(block):
    rows = block.shape[0] - 8
    code = block[:rows].astype(jnp.float32)
    scale = block[rows:].astype(jnp.float32)[:1, :] * (1.0 / REACH)
    root = jnp.exp(jnp.log(jnp.maximum(jnp.abs(code), 2.0**-126)) * (1.0 / POWER)) * scale
    return jnp.where(code < 0, -root, jnp.where(code > 0, root, jnp.zeros_like(root)))


def place_of(rho, parties):
    if rho % parties == 0:
        return 0, rho // parties
    return (rho, 0) if rho < parties else (2 * parties - rho, 1)


def transform_tables(parties, tok_rows):
    classes, half = 2 * parties, tok_rows // 2
    total = classes * tok_rows
    time = np.arange(tok_rows)
    table = np.zeros((parties, 2, 2, half, 2, tok_rows))
    for rho in range(classes):
        pair, side = place_of(rho, parties)
        angle = 2.0 * np.pi / total * ((classes * np.arange(half)[:, None] + rho) * time % total)
        cosine, sine = np.cos(angle), np.sin(angle)
        if pair == 0:
            table[pair, side, 0, :, side] = cosine
            table[pair, side, 1, :, side] = -sine
        else:
            sign = 1.0 - 2.0 * side
            table[pair, side, 0, :, 0] = cosine
            table[pair, side, 0, :, 1] = sign * sine
            table[pair, side, 1, :, 0] = -sine
            table[pair, side, 1, :, 1] = sign * cosine
    table[0, 0, 1, 0, 0] = 1.0 - 2.0 * (time % 2)
    forward = table.reshape(parties, 2 * tok_rows, 2 * tok_rows)

    def parts(matrix):
        high = matrix.astype(ml_dtypes.bfloat16)
        low = (matrix - high.astype(np.float64)).astype(ml_dtypes.bfloat16)
        return high, low

    return parts(forward) + parts(np.ascontiguousarray(forward.transpose(0, 2, 1)))


def weighted(terms):
    result = None
    for weight, value in terms:
        if abs(weight) < 1e-12:
            continue
        if abs(abs(weight) - 1.0) > 1e-12:
            term = value * abs(weight)
        else:
            term = value
        if result is None:
            result = term if weight > 0 else -term
        else:
            result = result + term if weight > 0 else result - term
    return result


def class_signals(blocks):
    parties = len(blocks)
    middle = parties // 2
    sums = [blocks[i] + blocks[i + middle] for i in range(middle)]
    gaps = [blocks[i] - blocks[i + middle] for i in range(middle)]
    signals = []
    for pair in range(parties):
        if pair == 0:
            even = weighted([(1.0, sums[i]) for i in range(0, middle, 2)])
            odd = weighted([(1.0, sums[i]) for i in range(1, middle, 2)])
            signals.append((even + odd, even - odd))
            continue
        used = blocks if pair % 2 else (sums if pair % 4 == 0 else gaps)
        angles = [math.pi * pair * i / parties for i in range(len(used))]
        real = weighted([(math.cos(a), v) for a, v in zip(angles, used)])
        imag = weighted([(-math.sin(a), v) for a, v in zip(angles, used)])
        signals.append((real, imag))
    return signals


def block_sums(signals):
    parties = len(signals)
    middle = parties // 2
    results = [None] * parties
    for i in range(middle):
        even = {0: [], 2: []}
        for pair in range(0, parties, 2):
            angle = math.pi * pair * i / parties
            real, imag = signals[pair]
            if pair == 0:
                even[0] += [(1.0, real), (1.0 - 2.0 * (i % 2), imag)]
            else:
                even[pair % 4] += [(math.cos(angle), real), (-math.sin(angle), imag)]
        same, flipped = weighted(even[0]), weighted(even[2])
        for place, base in ((i, same + flipped), (i + middle, same - flipped)):
            odd = []
            for pair in range(1, parties, 2):
                angle = math.pi * pair * place / parties
                real, imag = signals[pair]
                odd += [(math.cos(angle), real), (-math.sin(angle), imag)]
            results[place] = base + weighted(odd)
    return results


def hyena_kernel(
    parties,
    query_ref,
    key_ref,
    value_ref,
    taps_ref,
    skip_ref,
    spec_ref,
    fwd_high_hbm,
    fwd_low_hbm,
    bwd_high_hbm,
    bwd_low_hbm,
    out_ref,
    fwd_high,
    fwd_low,
    bwd_high,
    bwd_low,
    halo_out,
    halo_in,
    spec_out,
    spec_in,
    gated,
    data_out,
    data_in,
    data,
    classes,
    response,
    inverse,
    conv,
    conv_out,
    conv_in,
    table_sem,
    halo_send,
    halo_recv,
    spec_send,
    spec_recv,
    data_send,
    data_recv,
    conv_send,
    conv_recv,
):
    me = lax.axis_index("ctx")
    tok_rows, width = query_ref.shape
    owned = width // parties
    chunks, lanes = data_out.shape[0], gated.shape[3]
    group_count = spec_ref.shape[4]
    group_owned = group_count // parties
    group_chunk = group_owned // chunks
    half = tok_rows // 2
    rows = 2 * tok_rows

    tables = [
        pltpu.make_async_copy(source, target, table_sem.at[index])
        for index, (source, target) in enumerate(
            (
                (fwd_high_hbm, fwd_high),
                (fwd_low_hbm, fwd_low),
                (bwd_high_hbm, bwd_high),
                (bwd_low_hbm, bwd_low),
            )
        )
    ]
    for table in tables:
        table.start()

    barrier = pltpu.get_barrier_semaphore()

    @pl.loop(1, parties)
    def _(step):
        pl.semaphore_signal(
            barrier, inc=1, device_id={"ctx": lax.rem(me + step, parties)}, device_id_type=MESH
        )

    for index, ref in enumerate((query_ref, key_ref, value_ref)):
        last = ref[tok_rows - 16 :, :].astype(jnp.float32)
        halo_out[2 * index : 2 * index + 2, :] = last[14:16, :]
    halo_out[6:8, :] = jnp.zeros((2, width), jnp.float32)
    pl.semaphore_wait(barrier, parties - 1)

    halo = pltpu.make_async_remote_copy(
        halo_out,
        halo_in,
        halo_send,
        halo_recv,
        device_id={"ctx": lax.rem(me + 1, parties)},
        device_id_type=MESH,
    )
    halo.start()

    reach = parties // 2
    far, near = (1 - me // reach) * reach, me // reach * reach

    def partner(step):
        if step < reach:
            return far + lax.rem(me + step, reach)
        return near + lax.rem(me + step - reach + 1, reach)

    def spec_copy(target, slot):
        return pltpu.make_async_remote_copy(
            spec_out.at[pl.ds(pl.multiple_of(target * group_owned, group_owned), group_owned), :],
            spec_in.at[slot],
            spec_send.at[target],
            spec_recv.at[slot],
            device_id={"ctx": target},
            device_id_type=MESH,
        )

    def data_copy(chunk, target, slot):
        return pltpu.make_async_remote_copy(
            data_out.at[chunk, target],
            data_in.at[chunk, slot],
            data_send.at[chunk, target],
            data_recv.at[chunk, slot],
            device_id={"ctx": target},
            device_id_type=MESH,
        )

    def conv_copy(chunk, target, slot):
        return pltpu.make_async_remote_copy(
            conv_out.at[chunk, target],
            conv_in.at[chunk, slot],
            conv_send.at[chunk, target],
            conv_recv.at[chunk, slot],
            device_id={"ctx": target},
            device_id_type=MESH,
        )

    packed = jnp.concatenate(
        [spec_ref[part, 0, parity, :half, :] for part in range(2) for parity in range(2)], axis=0
    )
    row_index = lax.broadcasted_iota(jnp.int32, packed.shape, 0)
    highest = spec_ref[0, 0, 0, half : half + 1, :]
    packed = jnp.where((row_index == tok_rows) & (me == 0), highest, packed)
    spec_out[...] = packed.T

    for step in range(parties - 1):
        spec_copy(partner(step), me).start()

    spec_in[me] = spec_out[pl.ds(pl.multiple_of(me * group_owned, group_owned), group_owned), :]

    token = lax.broadcasted_iota(jnp.int32, (tok_rows, lanes), 0)

    def short(ref, index, columns):
        current = ref[:, columns].astype(jnp.float32)
        before = halo_in[2 * index : 2 * index + 2, columns]
        before = jnp.where(me == 0, jnp.zeros_like(before), before)
        shifted = jnp.where(token == 0, before[1:2, :], pltpu.roll(current, 1, 0))
        twice = jnp.where(token == 0, before[0:1, :], pltpu.roll(current, 2, 0))
        twice = jnp.where(token == 1, before[1:2, :], twice)
        taps = taps_ref[index, :, columns]
        return taps[0:1, :] * current + taps[1:2, :] * shifted + taps[2:3, :] * twice

    halo.wait_recv()

    def columns_of(target, chunk):
        return pl.ds(pl.multiple_of(target * owned + chunk * lanes, lanes), lanes)

    def gate(chunk, target):
        columns = columns_of(target, chunk)
        product = short(key_ref, 1, columns) * short(value_ref, 2, columns)
        gated[chunk, target] = product
        return product

    for chunk in range(chunks):

        for step in range(parties - 1):
            target = partner(step)
            data_out[chunk, target] = encode(gate(chunk, target))
            data_copy(chunk, target, me).start()

        data[chunk, me] = gate(chunk, me)

    lane_group = lax.broadcasted_iota(jnp.int32, (3 * group_chunk, lanes), 1) // (
        lanes // group_chunk
    )
    slot_group = lax.broadcasted_iota(jnp.int32, (3 * group_chunk, lanes), 0) % group_chunk
    spread = (lane_group == slot_group).astype(jnp.float32).astype(jnp.bfloat16)

    @pl.loop(1, parties)
    def _(step):
        spec_copy(me, lax.rem(me + step, parties)).wait_recv()

    levels = parties.bit_length() - 1
    row = lax.broadcasted_iota(jnp.int32, (rows, lanes), 0)
    for party in range(parties):
        for chunk in range(chunks):
            exact = spec_in[party, chunk * group_chunk : (chunk + 1) * group_chunk, :]
            high = exact.astype(jnp.bfloat16).astype(jnp.float32)
            middle = (exact - high).astype(jnp.bfloat16).astype(jnp.float32)
            low = exact - high - middle
            terms = jnp.concatenate((high, middle, low), axis=0).astype(jnp.bfloat16)
            wide = lax.dot_general(
                terms, spread, (((0,), (0,)), ((), ())), preferred_element_type=jnp.float32
            )
            if party == 0:
                ends = lax.rem(row, tok_rows) == 0
                wide = wide * jnp.where(ends, 0.5 / (parties * tok_rows), 1.0 / (parties * tok_rows))
            else:
                wide = wide * (1.0 / (parties * tok_rows))
            for parity in range(2):
                pair, side = place_of(2 * reversed_bits(party, levels) + parity, parties)
                for part in range(2):
                    start = part * tok_rows + parity * half
                    response[chunk, pair, side, part] = wide[start : start + half]

    for table in tables:
        table.wait()

    first = lax.broadcasted_iota(jnp.int32, (half, lanes), 0) == 0
    slab = 16

    for chunk in range(chunks):

        @pl.loop(1, parties)
        def _(step, chunk=chunk):
            source = lax.rem(me + step, parties)
            data_copy(chunk, me, source).wait_recv()
            data[chunk, source] = decode(data_in[chunk, source])

        @pl.loop(0, tok_rows // slab)
        def _(step, chunk=chunk):
            here = pl.ds(pl.multiple_of(step * slab, slab), slab)
            blocks = [data[chunk, party, here, :] for party in range(parties)]
            for pair, signals in enumerate(class_signals(blocks)):
                for side, signal in enumerate(signals):
                    classes[chunk, pair, side, here, :] = jnp.concatenate(
                        split_terms(signal), axis=1
                    )

        @pl.loop(0, parties, unroll=4)
        def _(pair, chunk=chunk):
            signal = classes[chunk, pair].reshape(rows, 2 * lanes)
            wide = jnp.dot(fwd_high[pair], signal, preferred_element_type=jnp.float32)
            rest = jnp.dot(fwd_low[pair], signal[:, :lanes], preferred_element_type=jnp.float32)
            spectrum = wide[:, :lanes] + wide[:, lanes:] + rest
            products = []
            for side in range(2):
                data_re = spectrum[side * tok_rows : side * tok_rows + half]
                data_im = spectrum[side * tok_rows + half : (side + 1) * tok_rows]
                resp_re, resp_im = response[chunk, pair, side, 0], response[chunk, pair, side, 1]
                both_re, both_im = data_re * resp_re, data_im * resp_im
                cross = data_re * resp_im + data_im * resp_re
                if side == 0:
                    alone = first & (pair == 0)
                    products.append(both_re - jnp.where(alone, jnp.zeros_like(both_im), both_im))
                    products.append(jnp.where(alone, both_im, cross))
                else:
                    products += [both_re - both_im, cross]
            product = jnp.concatenate(split_terms(jnp.concatenate(products, axis=0)), axis=1)
            wide = jnp.dot(bwd_high[pair], product, preferred_element_type=jnp.float32)
            rest = jnp.dot(bwd_low[pair], product[:, :lanes], preferred_element_type=jnp.float32)
            result = wide[:, :lanes] + wide[:, lanes:] + rest
            inverse[chunk, pair] = result.reshape(2, tok_rows, lanes)

        @pl.loop(0, tok_rows // slab)
        def _(step, chunk=chunk):
            here = pl.ds(pl.multiple_of(step * slab, slab), slab)
            signals = [
                (inverse[chunk, pair, 0, here, :], inverse[chunk, pair, 1, here, :])
                for pair in range(parties)
            ]
            for party, result in enumerate(block_sums(signals)):
                conv[chunk, party, here, :] = result

        for step in range(parties - 1):
            target = partner(step)
            conv_out[chunk, target] = encode(conv[chunk, target])
            conv_copy(chunk, target, me).start()

    def finish(chunk, source, conv):
        columns = columns_of(source, chunk)
        mixed = conv + skip_ref[:, columns] * gated[chunk, source]
        out_ref[:, columns] = (short(query_ref, 0, columns) * mixed).astype(jnp.bfloat16)

    for chunk in range(chunks):
        finish(chunk, me, conv[chunk, me])

        @pl.loop(1, parties)
        def _(step, chunk=chunk):
            source = lax.rem(me + step, parties)
            conv_copy(chunk, me, source).wait_recv()
            finish(chunk, source, decode(conv_in[chunk, source]))

    halo.wait_send()

    @pl.loop(1, parties)
    def _(step):
        target = lax.rem(me + step, parties)
        spec_copy(target, me).wait_send()
        for chunk in range(chunks):
            data_copy(chunk, target, me).wait_send()
            conv_copy(chunk, target, me).wait_send()


def one_kernel(tables, query_in, key_in, value_in, short_filter, skip_bias, filter_spectrum):
    tok_rows, width = query_in.shape
    parties = lax.axis_size("ctx")
    group_count = filter_spectrum.shape[4]
    lanes = 128
    chunks = width // parties // lanes
    vmem = pl.BlockSpec(memory_space=pltpu.VMEM)
    hbm = pl.BlockSpec(memory_space=pltpu.HBM)
    f32, bf16 = jnp.float32, jnp.bfloat16
    dma = pltpu.SemaphoreType.DMA
    return pl.pallas_call(
        functools.partial(hyena_kernel, parties),
        out_shape=pltpu.VMEM((tok_rows, width), bf16),
        in_specs=[vmem] * 6 + [hbm] * 4,
        out_specs=vmem,
        scratch_shapes=[
            *[pltpu.VMEM((parties, 2 * tok_rows, 2 * tok_rows), bf16)] * 4,
            pltpu.VMEM((8, width), f32),
            pltpu.VMEM((8, width), f32),
            pltpu.VMEM((group_count, 2 * tok_rows), f32),
            pltpu.VMEM((parties, group_count // parties, 2 * tok_rows), f32),
            pltpu.VMEM((chunks, parties, tok_rows, lanes), f32),
            pltpu.VMEM((chunks, parties, tok_rows + 8, lanes), bf16),
            pltpu.VMEM((chunks, parties, tok_rows + 8, lanes), bf16),
            pltpu.VMEM((chunks, parties, tok_rows, lanes), f32),
            pltpu.VMEM((chunks, parties, 2, tok_rows, 2 * lanes), bf16),
            pltpu.VMEM((chunks, parties, 2, 2, tok_rows // 2, lanes), f32),
            pltpu.VMEM((chunks, parties, 2, tok_rows, lanes), f32),
            pltpu.VMEM((chunks, parties, tok_rows, lanes), f32),
            pltpu.VMEM((chunks, parties, tok_rows + 8, lanes), bf16),
            pltpu.VMEM((chunks, parties, tok_rows + 8, lanes), bf16),
            dma((4,)),
            dma,
            dma,
            dma((parties,)),
            dma((parties,)),
            dma((chunks, parties)),
            dma((chunks, parties)),
            dma((chunks, parties)),
            dma((chunks, parties)),
        ],
        compiler_params=pltpu.CompilerParams(
            collective_id=0, has_side_effects=True, vmem_limit_bytes=56 * 1024 * 1024
        ),
    )(
        query_in,
        key_in,
        value_in,
        short_filter,
        skip_bias.reshape(1, width),
        filter_spectrum,
        *[jnp.asarray(table) for table in tables],
    )


def solution(mesh):
    parties = mesh.shape["ctx"]

    def per_device(*args):
        tok_rows, width = args[0].shape
        if width // parties % 128 == 0:
            return one_kernel(transform_tables(parties, tok_rows), *args)
        return on_device(*args)

    return jax.shard_map(
        per_device,
        mesh=mesh,
        in_specs=(
            P(("grp", "ctx"), "ch"),
            P(("grp", "ctx"), "ch"),
            P(("grp", "ctx"), "ch"),
            P(None, None, "ch"),
            P("ch"),
            P(None, "ctx", None, None, "ch"),
        ),
        out_specs=P(("grp", "ctx"), "ch"),
        check_vma=False,
    )
```

```python
import functools
import math

import jax
import jax.numpy as jnp
import ml_dtypes
import numpy as np
from jax import lax
from jax.experimental import pallas as pl
from jax.experimental.pallas import tpu as pltpu
from jax.sharding import PartitionSpec as P

HIGHEST = lax.Precision.HIGHEST
MESH = pl.DeviceIdType.MESH
POWER = 17
REACH = 2.0 ** (126 / POWER)


def passed_along(value, axis, steps):
    count = lax.axis_size(axis)
    leading, last = (max(0, -steps), min(count, count - steps))
    return lax.ppermute(value, axis, [(source, source + steps) for source in range(leading, last)])


def reversed_bits(number, digits):
    result = number * 0
    for bit_level in range(digits):
        result = result + (number >> bit_level & 1) * (1 << digits - 1 - bit_level)
    return result


def rotate(real_part, imag_part, cosine, sine):
    return (real_part * cosine - imag_part * sine, real_part * sine + imag_part * cosine)


def complex_product(pattern, table_real, table_imag, data_real, data_imag):
    out_real = jnp.einsum(pattern, table_real, data_real, precision=HIGHEST) - jnp.einsum(
        pattern, table_imag, data_imag, precision=HIGHEST
    )
    out_imag = jnp.einsum(pattern, table_real, data_imag, precision=HIGHEST) + jnp.einsum(
        pattern, table_imag, data_real, precision=HIGHEST
    )
    return (out_real, out_imag)


def angle_table(rows, cols, modulus):
    exponent = (
        jnp.arange(rows, dtype=jnp.int32)[:, None]
        * jnp.arange(cols, dtype=jnp.int32)[None, :]
        % modulus
    )
    angle = 2.0 * math.pi / modulus * exponent.astype(jnp.float32)
    return (jnp.cos(angle), jnp.sin(angle))


def whole_convolution(first_real, first_imag, filter_spectrum, parties, levels):
    tok_rows = first_real.shape[0]
    packed = jnp.stack((first_real, first_imag))
    spread = lax.all_to_all(packed, "ctx", split_axis=2, concat_axis=1, tiled=True)
    spectrum = lax.all_to_all(filter_spectrum, "ctx", split_axis=4, concat_axis=1, tiled=True)
    tail = spectrum.shape[2:]
    spectrum = spectrum.reshape(2, *[2] * levels, *tail)
    spectrum = spectrum.transpose(0, *range(levels, 0, -1), *range(levels + 1, levels + 4))
    spectrum = spectrum.reshape(2, parties, *tail)
    size_b = 2 * parties
    total = tok_rows * size_b
    spectrum = spectrum.reshape(2, size_b, tok_rows, spectrum.shape[4])
    columns = spread.shape[2]
    data = spread.reshape(2, size_b // 2, tok_rows, columns)
    outer_cos, outer_sin = angle_table(size_b, size_b // 2, size_b)
    twist_cos, twist_sin = angle_table(size_b, tok_rows, total)
    inner_cos, inner_sin = angle_table(tok_rows, tok_rows, tok_rows)
    section_real, section_imag = complex_product(
        "fn,nac->fac", outer_cos, -outer_sin, data[0], data[1]
    )
    section_real, section_imag = rotate(
        section_real, section_imag, twist_cos[..., None], -twist_sin[..., None]
    )
    freq_real, freq_imag = complex_product(
        "ak,fac->fkc", inner_cos, -inner_sin, section_real, section_imag
    )
    group_local = spectrum.shape[3]
    per_group = columns // group_local
    shaped_real = freq_real.reshape(size_b, tok_rows, group_local, per_group)
    shaped_imag = freq_imag.reshape(size_b, tok_rows, group_local, per_group)
    resp_real = spectrum[0][..., None]
    resp_imag = spectrum[1][..., None]
    prod_real = (shaped_real * resp_real - shaped_imag * resp_imag).reshape(
        size_b, tok_rows, columns
    )
    prod_imag = (shaped_real * resp_imag + shaped_imag * resp_real).reshape(
        size_b, tok_rows, columns
    )
    back_real, back_imag = complex_product(
        "ak,fkc->fac", inner_cos, inner_sin, prod_real, prod_imag
    )
    back_real, back_imag = rotate(back_real, back_imag, twist_cos[..., None], twist_sin[..., None])
    out_real, out_imag = complex_product(
        "nf,fac->nac", outer_cos.T, outer_sin.T, back_real, back_imag
    )
    norm_factor = 1.0 / total
    result = (
        jnp.stack(
            (
                out_real.reshape(size_b // 2 * tok_rows, columns),
                out_imag.reshape(size_b // 2 * tok_rows, columns),
            )
        )
        * norm_factor
    )
    returned = lax.all_to_all(result, "ctx", split_axis=1, concat_axis=2, tiled=True)
    return (returned[0], returned[1])


def on_device(query_in, key_in, value_in, short_filter, skip_bias, filter_spectrum):
    tok_rows, chan_width = query_in.shape
    parties = lax.axis_size("ctx")
    levels = parties.bit_length() - 1
    tap_count = short_filter.shape[1]
    group_count = filter_spectrum.shape[4]
    half_group = chan_width // (2 * group_count)
    packed_width = group_count * half_group
    stacked = jnp.stack((query_in, key_in, value_in))
    earlier = passed_along(stacked[:, tok_rows - (tap_count - 1) :, :], "ctx", 1)
    extended = jnp.concatenate((earlier, stacked), axis=1).astype(jnp.float32)
    filtered = short_filter[:, 0, None, :] * extended[:, tap_count - 1 :, :]
    for tap_lag in range(1, tap_count):
        start_row = tap_count - 1 - tap_lag
        filtered = (
            filtered
            + short_filter[:, tap_lag, None, :] * extended[:, start_row : start_row + tok_rows, :]
        )
    gated = filtered[1] * filtered[2]
    halves = gated.reshape(tok_rows, group_count, 2, half_group)
    first_real = halves[:, :, 0, :].reshape(tok_rows, packed_width)
    first_imag = halves[:, :, 1, :].reshape(tok_rows, packed_width)
    conv_real, conv_imag = whole_convolution(
        first_real, first_imag, filter_spectrum, parties, levels
    )
    conv = jnp.stack(
        (
            conv_real.reshape(tok_rows, group_count, half_group),
            conv_imag.reshape(tok_rows, group_count, half_group),
        ),
        axis=2,
    ).reshape(tok_rows, chan_width)
    return (filtered[0] * (conv + skip_bias[None, :] * gated)).astype(jnp.bfloat16)


def split_terms(value):
    high = value.astype(jnp.bfloat16)
    low = (value - high.astype(jnp.float32)).astype(jnp.bfloat16)
    return high, low


def scale_of(value):
    peak = jnp.max(jnp.abs(value), axis=0, keepdims=True)
    return jnp.maximum(peak * 1.0078125, 2.0**-100)


def encode(value, scale):
    ratio = value * (REACH / scale)
    square = ratio * ratio
    fourth = square * square
    eighth = fourth * fourth
    return (ratio * (eighth * eighth)).astype(jnp.bfloat16)


def decode(block, scale):
    code = block.astype(jnp.float32)
    root = jnp.exp(jnp.log(jnp.maximum(jnp.abs(code), 2.0**-126)) * (1.0 / POWER))
    root = root * (scale * (1.0 / REACH))
    return jnp.where(code < 0, -root, jnp.where(code > 0, root, jnp.zeros_like(root)))


def place_of(rho, parties):
    if rho % parties == 0:
        return 0, rho // parties
    return (rho, 0) if rho < parties else (2 * parties - rho, 1)


def transform_tables(parties, tok_rows):
    classes, half = 2 * parties, tok_rows // 2
    total = classes * tok_rows
    time = np.arange(tok_rows)
    table = np.zeros((parties, 2, 2, half, 2, tok_rows))
    for rho in range(classes):
        pair, side = place_of(rho, parties)
        angle = 2.0 * np.pi / total * ((classes * np.arange(half)[:, None] + rho) * time % total)
        cosine, sine = np.cos(angle), np.sin(angle)
        if pair == 0:
            table[pair, side, 0, :, side] = cosine
            table[pair, side, 1, :, side] = -sine
        else:
            sign = 1.0 - 2.0 * side
            table[pair, side, 0, :, 0] = cosine
            table[pair, side, 0, :, 1] = sign * sine
            table[pair, side, 1, :, 0] = -sine
            table[pair, side, 1, :, 1] = sign * cosine
    table[0, 0, 1, 0, 0] = 1.0 - 2.0 * (time % 2)
    forward = table.reshape(parties, 2 * tok_rows, 2 * tok_rows)

    def parts(matrix):
        high = matrix.astype(ml_dtypes.bfloat16)
        low = (matrix - high.astype(np.float64)).astype(ml_dtypes.bfloat16)
        return high, low

    return parts(forward) + parts(np.ascontiguousarray(forward.transpose(0, 2, 1)))


def weighted(terms):
    result = None
    for weight, value in terms:
        if abs(weight) < 1e-12:
            continue
        if abs(abs(weight) - 1.0) > 1e-12:
            term = value * abs(weight)
        else:
            term = value
        if result is None:
            result = term if weight > 0 else -term
        else:
            result = result + term if weight > 0 else result - term
    return result


def class_signals(blocks):
    parties = len(blocks)
    middle = parties // 2
    sums = [blocks[i] + blocks[i + middle] for i in range(middle)]
    gaps = [blocks[i] - blocks[i + middle] for i in range(middle)]
    signals = []
    for pair in range(parties):
        if pair == 0:
            even = weighted([(1.0, sums[i]) for i in range(0, middle, 2)])
            odd = weighted([(1.0, sums[i]) for i in range(1, middle, 2)])
            signals.append((even + odd, even - odd))
            continue
        used = blocks if pair % 2 else (sums if pair % 4 == 0 else gaps)
        angles = [math.pi * pair * i / parties for i in range(len(used))]
        real = weighted([(math.cos(a), v) for a, v in zip(angles, used)])
        imag = weighted([(-math.sin(a), v) for a, v in zip(angles, used)])
        signals.append((real, imag))
    return signals


def block_sums(signals):
    parties = len(signals)
    middle = parties // 2
    results = [None] * parties
    for i in range(middle):
        even = {0: [], 2: []}
        for pair in range(0, parties, 2):
            angle = math.pi * pair * i / parties
            real, imag = signals[pair]
            if pair == 0:
                even[0] += [(1.0, real), (1.0 - 2.0 * (i % 2), imag)]
            else:
                even[pair % 4] += [(math.cos(angle), real), (-math.sin(angle), imag)]
        same, flipped = weighted(even[0]), weighted(even[2])
        for place, base in ((i, same + flipped), (i + middle, same - flipped)):
            odd = []
            for pair in range(1, parties, 2):
                angle = math.pi * pair * place / parties
                real, imag = signals[pair]
                odd += [(math.cos(angle), real), (-math.sin(angle), imag)]
            results[place] = base + weighted(odd)
    return results


def hyena_kernel(
    parties,
    query_hbm,
    key_hbm,
    value_hbm,
    taps_hbm,
    skip_hbm,
    spec_hbm,
    fwd_high_hbm,
    fwd_low_hbm,
    bwd_high_hbm,
    bwd_low_hbm,
    out_ref,
    query_ref,
    key_ref,
    value_ref,
    taps_ref,
    skip_ref,
    spec_ref,
    fwd_high,
    fwd_low,
    bwd_high,
    bwd_low,
    halo_out,
    halo_in,
    spec_out,
    spec_in,
    spec_scale_out,
    spec_scale_in,
    gated,
    data_out,
    data_in,
    data_scale_out,
    data_scale_in,
    data,
    classes,
    response,
    inverse,
    conv,
    conv_out,
    conv_in,
    conv_scale_out,
    conv_scale_in,
    input_sem,
    table_sem,
    halo_send,
    halo_recv,
    spec_send,
    spec_recv,
    data_send,
    data_recv,
    conv_send,
    conv_recv,
    spec_scale_send,
    spec_scale_recv,
    data_scale_send,
    data_scale_recv,
    conv_scale_send,
    conv_scale_recv,
):
    me = lax.axis_index("ctx")
    tok_rows, width = query_ref.shape
    owned = width // parties
    chunks, lanes = data_out.shape[0], gated.shape[3]
    group_count = spec_ref.shape[4]
    group_owned = group_count // parties
    group_chunk = group_owned // chunks
    half = tok_rows // 2
    rows = 2 * tok_rows

    inputs = [
        pltpu.make_async_copy(source, target, input_sem.at[index])
        for index, (source, target) in enumerate(
            (
                (spec_hbm, spec_ref),
                (key_hbm, key_ref),
                (value_hbm, value_ref),
                (query_hbm, query_ref),
                (taps_hbm, taps_ref),
                (skip_hbm, skip_ref),
            )
        )
    ]
    for copy in inputs:
        copy.start()

    barrier = pltpu.get_barrier_semaphore()

    @pl.loop(1, parties)
    def _(step):
        pl.semaphore_signal(
            barrier, inc=1, device_id={"ctx": lax.rem(me + step, parties)}, device_id_type=MESH
        )

    inputs[0].wait()
    packed = jnp.concatenate(
        [spec_ref[part, 0, parity, :half, :] for part in range(2) for parity in range(2)], axis=0
    )
    row_index = lax.broadcasted_iota(jnp.int32, packed.shape, 0)
    highest = spec_ref[0, 0, 0, half : half + 1, :]
    packed = jnp.where((row_index == tok_rows) & (me == 0), highest, packed)
    spec_scale = jnp.max(scale_of(packed), axis=1, keepdims=True)
    spec_scale_out[...] = jnp.broadcast_to(spec_scale, (1, lanes))
    codes = packed.T
    spec_out[...] = encode(codes, spec_scale).reshape(spec_out.shape)
    spec_in[me] = spec_out[me]
    spec_scale_in[me] = spec_scale_out[...]

    for copy in inputs[1:]:
        copy.wait()
    tables = [
        pltpu.make_async_copy(source, target, table_sem.at[index])
        for index, (source, target) in enumerate(
            (
                (fwd_high_hbm, fwd_high),
                (fwd_low_hbm, fwd_low),
                (bwd_high_hbm, bwd_high),
                (bwd_low_hbm, bwd_low),
            )
        )
    ]
    for table in tables:
        table.start()


    for index, ref in enumerate((query_ref, key_ref, value_ref)):
        last = ref[tok_rows - 16 :, :].astype(jnp.float32)
        halo_out[2 * index : 2 * index + 2, :] = last[14:16, :]
    halo_out[6:8, :] = jnp.zeros((2, width), jnp.float32)
    pl.semaphore_wait(barrier, parties - 1)

    halo = pltpu.make_async_remote_copy(
        halo_out,
        halo_in,
        halo_send,
        halo_recv,
        device_id={"ctx": lax.rem(me + 1, parties)},
        device_id_type=MESH,
    )
    halo.start()

    reach = parties // 2
    far, near = (1 - me // reach) * reach, me // reach * reach

    def partner(step):
        return lax.rem(me + step + 1, parties)
        crossing = jnp.int32(step < reach)
        return crossing * (far + lax.rem(me + step, reach)) + (1 - crossing) * (
            near + lax.rem(me + step - reach + 1, reach)
        )

    def spec_copy(target, slot):
        return pltpu.make_async_remote_copy(
            spec_out.at[target],
            spec_in.at[slot],
            spec_send.at[target],
            spec_recv.at[slot],
            device_id={"ctx": target},
            device_id_type=MESH,
        )

    def spec_scale_copy(target, slot):
        return pltpu.make_async_remote_copy(
            spec_scale_out,
            spec_scale_in.at[slot],
            spec_scale_send.at[target],
            spec_scale_recv.at[slot],
            device_id={"ctx": target},
            device_id_type=MESH,
        )

    def data_scale_copy(chunk, target, slot):
        return pltpu.make_async_remote_copy(
            data_scale_out.at[chunk, target],
            data_scale_in.at[chunk, slot],
            data_scale_send.at[chunk, target],
            data_scale_recv.at[chunk, slot],
            device_id={"ctx": target},
            device_id_type=MESH,
        )

    def conv_scale_copy(chunk, target, slot):
        return pltpu.make_async_remote_copy(
            conv_scale_out.at[chunk, target],
            conv_scale_in.at[chunk, slot],
            conv_scale_send.at[chunk, target],
            conv_scale_recv.at[chunk, slot],
            device_id={"ctx": target},
            device_id_type=MESH,
        )

    def data_copy(chunk, target, slot):
        return pltpu.make_async_remote_copy(
            data_out.at[chunk, target],
            data_in.at[chunk, slot],
            data_send.at[chunk, target],
            data_recv.at[chunk, slot],
            device_id={"ctx": target},
            device_id_type=MESH,
        )

    def conv_copy(chunk, target, slot):
        return pltpu.make_async_remote_copy(
            conv_out.at[chunk, target],
            conv_in.at[chunk, slot],
            conv_send.at[chunk, target],
            conv_recv.at[chunk, slot],
            device_id={"ctx": target},
            device_id_type=MESH,
        )

    @pl.loop(0, parties - 1)
    def _(step):
        target = partner(step)
        spec_copy(target, me).start()
        spec_scale_copy(target, me).start()

    token = lax.broadcasted_iota(jnp.int32, (tok_rows, lanes), 0)

    def short(ref, index, columns):
        current = ref[:, columns].astype(jnp.float32)
        before = halo_in[2 * index : 2 * index + 2, columns]
        before = jnp.where(me == 0, jnp.zeros_like(before), before)
        shifted = jnp.where(token == 0, before[1:2, :], pltpu.roll(current, 1, 0))
        twice = jnp.where(token == 0, before[0:1, :], pltpu.roll(current, 2, 0))
        twice = jnp.where(token == 1, before[1:2, :], twice)
        taps = taps_ref[index, :, columns]
        return taps[0:1, :] * current + taps[1:2, :] * shifted + taps[2:3, :] * twice

    halo.wait_recv()

    def columns_of(target, chunk):
        return pl.ds(pl.multiple_of(target * owned + chunk * lanes, lanes), lanes)

    def gate(chunk, target):
        columns = columns_of(target, chunk)
        product = short(key_ref, 1, columns) * short(value_ref, 2, columns)
        gated[chunk, target] = product
        return product

    for chunk in range(chunks):

        @pl.loop(0, parties - 1)
        def _(step, chunk=chunk):
            target = partner(step)
            product = gate(chunk, target)
            scale = scale_of(product)
            data_scale_out[chunk, target] = scale
            data_out[chunk, target] = encode(product, scale)
            data_copy(chunk, target, me).start()
            data_scale_copy(chunk, target, me).start()

        data[chunk, me] = gate(chunk, me)

    lane_group = lax.broadcasted_iota(jnp.int32, (3 * group_chunk, lanes), 1) // (
        lanes // group_chunk
    )
    slot_group = lax.broadcasted_iota(jnp.int32, (3 * group_chunk, lanes), 0) % group_chunk
    spread = (lane_group == slot_group).astype(jnp.float32).astype(jnp.bfloat16)

    @pl.loop(1, parties)
    def _(step):
        source = lax.rem(me + step, parties)
        spec_copy(me, source).wait_recv()
        spec_scale_copy(me, source).wait_recv()

    levels = parties.bit_length() - 1
    row = lax.broadcasted_iota(jnp.int32, (rows, lanes), 0)
    for party in range(parties):
        decoded = decode(spec_in[party], spec_scale_in[party, :, :1])
        for chunk in range(chunks):
            exact = decoded[chunk * group_chunk : (chunk + 1) * group_chunk]
            high = exact.astype(jnp.bfloat16).astype(jnp.float32)
            middle = (exact - high).astype(jnp.bfloat16).astype(jnp.float32)
            low = exact - high - middle
            terms = jnp.concatenate((high, middle, low), axis=0).astype(jnp.bfloat16)
            wide = lax.dot_general(
                terms, spread, (((0,), (0,)), ((), ())), preferred_element_type=jnp.float32
            )
            if party == 0:
                ends = lax.rem(row, tok_rows) == 0
                wide = wide * jnp.where(ends, 0.5 / (parties * tok_rows), 1.0 / (parties * tok_rows))
            else:
                wide = wide * (1.0 / (parties * tok_rows))
            for parity in range(2):
                pair, side = place_of(2 * reversed_bits(party, levels) + parity, parties)
                for part in range(2):
                    start = part * tok_rows + parity * half
                    response[chunk, pair, side, part] = wide[start : start + half]

    for table in tables:
        table.wait()

    first = lax.broadcasted_iota(jnp.int32, (half, lanes), 0) == 0
    slab = 16

    for chunk in range(chunks):

        @pl.loop(1, parties)
        def _(step, chunk=chunk):
            source = lax.rem(me + step, parties)
            data_scale_copy(chunk, me, source).wait_recv()
            data_copy(chunk, me, source).wait_recv()
            data[chunk, source] = decode(data_in[chunk, source], data_scale_in[chunk, source])

        @pl.loop(0, tok_rows // slab)
        def _(step, chunk=chunk):
            here = pl.ds(pl.multiple_of(step * slab, slab), slab)
            blocks = [data[chunk, party, here, :] for party in range(parties)]
            for pair, signals in enumerate(class_signals(blocks)):
                for side, signal in enumerate(signals):
                    classes[chunk, pair, side, here, :] = jnp.concatenate(
                        split_terms(signal), axis=1
                    )

        @pl.loop(0, parties, unroll=4)
        def _(pair, chunk=chunk):
            signal = classes[chunk, pair].reshape(rows, 2 * lanes)
            wide = jnp.dot(fwd_high[pair], signal, preferred_element_type=jnp.float32)
            rest = jnp.dot(fwd_low[pair], signal[:, :lanes], preferred_element_type=jnp.float32)
            spectrum = wide[:, :lanes] + wide[:, lanes:] + rest
            products = []
            for side in range(2):
                data_re = spectrum[side * tok_rows : side * tok_rows + half]
                data_im = spectrum[side * tok_rows + half : (side + 1) * tok_rows]
                resp_re, resp_im = response[chunk, pair, side, 0], response[chunk, pair, side, 1]
                both_re, both_im = data_re * resp_re, data_im * resp_im
                cross = data_re * resp_im + data_im * resp_re
                if side == 0:
                    alone = first & (pair == 0)
                    products.append(both_re - jnp.where(alone, jnp.zeros_like(both_im), both_im))
                    products.append(jnp.where(alone, both_im, cross))
                else:
                    products += [both_re - both_im, cross]
            product = jnp.concatenate(split_terms(jnp.concatenate(products, axis=0)), axis=1)
            wide = jnp.dot(bwd_high[pair], product, preferred_element_type=jnp.float32)
            rest = jnp.dot(bwd_low[pair], product[:, :lanes], preferred_element_type=jnp.float32)
            result = wide[:, :lanes] + wide[:, lanes:] + rest
            inverse[chunk, pair] = result.reshape(2, tok_rows, lanes)

        @pl.loop(0, tok_rows // slab)
        def _(step, chunk=chunk):
            here = pl.ds(pl.multiple_of(step * slab, slab), slab)
            signals = [
                (inverse[chunk, pair, 0, here, :], inverse[chunk, pair, 1, here, :])
                for pair in range(parties)
            ]
            for party, result in enumerate(block_sums(signals)):
                conv[chunk, party, here, :] = result

        @pl.loop(0, parties - 1)
        def _(step, chunk=chunk):
            target = partner(step)
            result = conv[chunk, target]
            scale = scale_of(result)
            conv_scale_out[chunk, target] = scale
            conv_out[chunk, target] = encode(result, scale)
            conv_copy(chunk, target, me).start()
            conv_scale_copy(chunk, target, me).start()

    def finish(chunk, source, conv):
        columns = columns_of(source, chunk)
        mixed = conv + skip_ref[:, columns] * gated[chunk, source]
        out_ref[:, columns] = (short(query_ref, 0, columns) * mixed).astype(jnp.bfloat16)

    for chunk in range(chunks):
        finish(chunk, me, conv[chunk, me])

        @pl.loop(1, parties)
        def _(step, chunk=chunk):
            source = lax.rem(me + step, parties)
            conv_scale_copy(chunk, me, source).wait_recv()
            conv_copy(chunk, me, source).wait_recv()
            finish(chunk, source, decode(conv_in[chunk, source], conv_scale_in[chunk, source]))

    halo.wait_send()

    @pl.loop(1, parties)
    def _(step):
        target = lax.rem(me + step, parties)
        spec_copy(target, me).wait_send()
        spec_scale_copy(target, me).wait_send()
        for chunk in range(chunks):
            data_copy(chunk, target, me).wait_send()
            data_scale_copy(chunk, target, me).wait_send()
            conv_copy(chunk, target, me).wait_send()
            conv_scale_copy(chunk, target, me).wait_send()


def one_kernel(tables, query_in, key_in, value_in, short_filter, skip_bias, filter_spectrum):
    tok_rows, width = query_in.shape
    parties = lax.axis_size("ctx")
    group_count = filter_spectrum.shape[4]
    lanes = 128
    chunks = width // parties // lanes
    vmem = pl.BlockSpec(memory_space=pltpu.VMEM)
    hbm = pl.BlockSpec(memory_space=pltpu.HBM)
    f32, bf16 = jnp.float32, jnp.bfloat16
    dma = pltpu.SemaphoreType.DMA
    return pl.pallas_call(
        functools.partial(hyena_kernel, parties),
        out_shape=pltpu.VMEM((tok_rows, width), bf16),
        in_specs=[hbm] * 10,
        out_specs=vmem,
        scratch_shapes=[
            *[pltpu.VMEM((tok_rows, width), bf16)] * 3,
            pltpu.VMEM(short_filter.shape, f32),
            pltpu.VMEM((1, width), f32),
            pltpu.VMEM(filter_spectrum.shape, f32),
            *[pltpu.VMEM((parties, 2 * tok_rows, 2 * tok_rows), bf16)] * 4,
            pltpu.VMEM((8, width), f32),
            pltpu.VMEM((8, width), f32),
            *[pltpu.VMEM((parties, group_count // parties, 2 * tok_rows), bf16)] * 2,
            pltpu.VMEM((1, lanes), f32),
            pltpu.VMEM((parties, 1, lanes), f32),
            pltpu.VMEM((chunks, parties, tok_rows, lanes), f32),
            *[pltpu.VMEM((chunks, parties, tok_rows, lanes), bf16)] * 2,
            *[pltpu.VMEM((chunks, parties, 1, lanes), f32)] * 2,
            pltpu.VMEM((chunks, parties, tok_rows, lanes), f32),
            pltpu.VMEM((chunks, parties, 2, tok_rows, 2 * lanes), bf16),
            pltpu.VMEM((chunks, parties, 2, 2, tok_rows // 2, lanes), f32),
            pltpu.VMEM((chunks, parties, 2, tok_rows, lanes), f32),
            pltpu.VMEM((chunks, parties, tok_rows, lanes), f32),
            *[pltpu.VMEM((chunks, parties, tok_rows, lanes), bf16)] * 2,
            *[pltpu.VMEM((chunks, parties, 1, lanes), f32)] * 2,
            dma((6,)),
            dma((4,)),
            dma,
            dma,
            dma((parties,)),
            dma((parties,)),
            *[dma((chunks, parties))] * 4,
            *[dma((parties,))] * 2,
            *[dma((chunks, parties))] * 4,
        ],
        compiler_params=pltpu.CompilerParams(
            collective_id=0, has_side_effects=True, vmem_limit_bytes=56 * 1024 * 1024
        ),
    )(
        query_in,
        key_in,
        value_in,
        short_filter,
        skip_bias.reshape(1, width),
        filter_spectrum,
        *[jnp.asarray(table) for table in tables],
    )


def solution(mesh):
    parties = mesh.shape["ctx"]

    def per_device(*args):
        tok_rows, width = args[0].shape
        if width // parties % 128 == 0:
            return one_kernel(transform_tables(parties, tok_rows), *args)
        return on_device(*args)

    return jax.shard_map(
        per_device,
        mesh=mesh,
        in_specs=(
            P(("grp", "ctx"), "ch"),
            P(("grp", "ctx"), "ch"),
            P(("grp", "ctx"), "ch"),
            P(None, None, "ch"),
            P("ch"),
            P(None, "ctx", None, None, "ch"),
        ),
        out_specs=P(("grp", "ctx"), "ch"),
        check_vma=False,
    )
```

```python
import functools
import math

import jax
import jax.numpy as jnp
import ml_dtypes
import numpy as np
from jax import lax
from jax.experimental import pallas as pl
from jax.experimental.pallas import tpu as pltpu
from jax.sharding import PartitionSpec as P

HIGHEST = lax.Precision.HIGHEST
MESH = pl.DeviceIdType.MESH
POWER = 17
REACH = 2.0 ** (126 / POWER)


def passed_along(value, axis, steps):
    count = lax.axis_size(axis)
    leading, last = (max(0, -steps), min(count, count - steps))
    return lax.ppermute(value, axis, [(source, source + steps) for source in range(leading, last)])


def reversed_bits(number, digits):
    result = number * 0
    for bit_level in range(digits):
        result = result + (number >> bit_level & 1) * (1 << digits - 1 - bit_level)
    return result


def rotate(real_part, imag_part, cosine, sine):
    return (real_part * cosine - imag_part * sine, real_part * sine + imag_part * cosine)


def complex_product(pattern, table_real, table_imag, data_real, data_imag):
    out_real = jnp.einsum(pattern, table_real, data_real, precision=HIGHEST) - jnp.einsum(
        pattern, table_imag, data_imag, precision=HIGHEST
    )
    out_imag = jnp.einsum(pattern, table_real, data_imag, precision=HIGHEST) + jnp.einsum(
        pattern, table_imag, data_real, precision=HIGHEST
    )
    return (out_real, out_imag)


def angle_table(rows, cols, modulus):
    exponent = (
        jnp.arange(rows, dtype=jnp.int32)[:, None]
        * jnp.arange(cols, dtype=jnp.int32)[None, :]
        % modulus
    )
    angle = 2.0 * math.pi / modulus * exponent.astype(jnp.float32)
    return (jnp.cos(angle), jnp.sin(angle))


def whole_convolution(first_real, first_imag, filter_spectrum, parties, levels):
    tok_rows = first_real.shape[0]
    packed = jnp.stack((first_real, first_imag))
    spread = lax.all_to_all(packed, "ctx", split_axis=2, concat_axis=1, tiled=True)
    spectrum = lax.all_to_all(filter_spectrum, "ctx", split_axis=4, concat_axis=1, tiled=True)
    tail = spectrum.shape[2:]
    spectrum = spectrum.reshape(2, *[2] * levels, *tail)
    spectrum = spectrum.transpose(0, *range(levels, 0, -1), *range(levels + 1, levels + 4))
    spectrum = spectrum.reshape(2, parties, *tail)
    size_b = 2 * parties
    total = tok_rows * size_b
    spectrum = spectrum.reshape(2, size_b, tok_rows, spectrum.shape[4])
    columns = spread.shape[2]
    data = spread.reshape(2, size_b // 2, tok_rows, columns)
    outer_cos, outer_sin = angle_table(size_b, size_b // 2, size_b)
    twist_cos, twist_sin = angle_table(size_b, tok_rows, total)
    inner_cos, inner_sin = angle_table(tok_rows, tok_rows, tok_rows)
    section_real, section_imag = complex_product(
        "fn,nac->fac", outer_cos, -outer_sin, data[0], data[1]
    )
    section_real, section_imag = rotate(
        section_real, section_imag, twist_cos[..., None], -twist_sin[..., None]
    )
    freq_real, freq_imag = complex_product(
        "ak,fac->fkc", inner_cos, -inner_sin, section_real, section_imag
    )
    group_local = spectrum.shape[3]
    per_group = columns // group_local
    shaped_real = freq_real.reshape(size_b, tok_rows, group_local, per_group)
    shaped_imag = freq_imag.reshape(size_b, tok_rows, group_local, per_group)
    resp_real = spectrum[0][..., None]
    resp_imag = spectrum[1][..., None]
    prod_real = (shaped_real * resp_real - shaped_imag * resp_imag).reshape(
        size_b, tok_rows, columns
    )
    prod_imag = (shaped_real * resp_imag + shaped_imag * resp_real).reshape(
        size_b, tok_rows, columns
    )
    back_real, back_imag = complex_product(
        "ak,fkc->fac", inner_cos, inner_sin, prod_real, prod_imag
    )
    back_real, back_imag = rotate(back_real, back_imag, twist_cos[..., None], twist_sin[..., None])
    out_real, out_imag = complex_product(
        "nf,fac->nac", outer_cos.T, outer_sin.T, back_real, back_imag
    )
    norm_factor = 1.0 / total
    result = (
        jnp.stack(
            (
                out_real.reshape(size_b // 2 * tok_rows, columns),
                out_imag.reshape(size_b // 2 * tok_rows, columns),
            )
        )
        * norm_factor
    )
    returned = lax.all_to_all(result, "ctx", split_axis=1, concat_axis=2, tiled=True)
    return (returned[0], returned[1])


def on_device(query_in, key_in, value_in, short_filter, skip_bias, filter_spectrum):
    tok_rows, chan_width = query_in.shape
    parties = lax.axis_size("ctx")
    levels = parties.bit_length() - 1
    tap_count = short_filter.shape[1]
    group_count = filter_spectrum.shape[4]
    half_group = chan_width // (2 * group_count)
    packed_width = group_count * half_group
    stacked = jnp.stack((query_in, key_in, value_in))
    earlier = passed_along(stacked[:, tok_rows - (tap_count - 1) :, :], "ctx", 1)
    extended = jnp.concatenate((earlier, stacked), axis=1).astype(jnp.float32)
    filtered = short_filter[:, 0, None, :] * extended[:, tap_count - 1 :, :]
    for tap_lag in range(1, tap_count):
        start_row = tap_count - 1 - tap_lag
        filtered = (
            filtered
            + short_filter[:, tap_lag, None, :] * extended[:, start_row : start_row + tok_rows, :]
        )
    gated = filtered[1] * filtered[2]
    halves = gated.reshape(tok_rows, group_count, 2, half_group)
    first_real = halves[:, :, 0, :].reshape(tok_rows, packed_width)
    first_imag = halves[:, :, 1, :].reshape(tok_rows, packed_width)
    conv_real, conv_imag = whole_convolution(
        first_real, first_imag, filter_spectrum, parties, levels
    )
    conv = jnp.stack(
        (
            conv_real.reshape(tok_rows, group_count, half_group),
            conv_imag.reshape(tok_rows, group_count, half_group),
        ),
        axis=2,
    ).reshape(tok_rows, chan_width)
    return (filtered[0] * (conv + skip_bias[None, :] * gated)).astype(jnp.bfloat16)


def split_terms(value):
    high = value.astype(jnp.bfloat16)
    low = (value - high.astype(jnp.float32)).astype(jnp.bfloat16)
    return high, low


def scale_of(value):
    peak = jnp.max(jnp.abs(value), axis=0, keepdims=True)
    return jnp.maximum(peak * 1.0078125, 2.0**-100)


def encode(value, scale):
    ratio = value * (REACH / scale)
    square = ratio * ratio
    fourth = square * square
    eighth = fourth * fourth
    return (ratio * (eighth * eighth)).astype(jnp.bfloat16)


def decode(block, scale):
    code = block.astype(jnp.float32)
    root = jnp.exp(jnp.log(jnp.maximum(jnp.abs(code), 2.0**-126)) * (1.0 / POWER))
    root = root * (scale * (1.0 / REACH))
    return jnp.where(code < 0, -root, jnp.where(code > 0, root, jnp.zeros_like(root)))


def place_of(rho, parties):
    if rho % parties == 0:
        return 0, rho // parties
    return (rho, 0) if rho < parties else (2 * parties - rho, 1)


def transform_tables(parties, tok_rows):
    classes, half = 2 * parties, tok_rows // 2
    total = classes * tok_rows
    time = np.arange(tok_rows)
    table = np.zeros((parties, 2, 2, half, 2, tok_rows))
    for rho in range(classes):
        pair, side = place_of(rho, parties)
        angle = 2.0 * np.pi / total * ((classes * np.arange(half)[:, None] + rho) * time % total)
        cosine, sine = np.cos(angle), np.sin(angle)
        if pair == 0:
            table[pair, side, 0, :, side] = cosine
            table[pair, side, 1, :, side] = -sine
        else:
            sign = 1.0 - 2.0 * side
            table[pair, side, 0, :, 0] = cosine
            table[pair, side, 0, :, 1] = sign * sine
            table[pair, side, 1, :, 0] = -sine
            table[pair, side, 1, :, 1] = sign * cosine
    table[0, 0, 1, 0, 0] = 1.0 - 2.0 * (time % 2)
    forward = table.reshape(parties, 2 * tok_rows, 2 * tok_rows)

    def parts(matrix):
        high = matrix.astype(ml_dtypes.bfloat16)
        low = (matrix - high.astype(np.float64)).astype(ml_dtypes.bfloat16)
        return high, low

    return parts(forward) + parts(np.ascontiguousarray(forward.transpose(0, 2, 1)))


def weighted(terms):
    result = None
    for weight, value in terms:
        if abs(weight) < 1e-12:
            continue
        if abs(abs(weight) - 1.0) > 1e-12:
            term = value * abs(weight)
        else:
            term = value
        if result is None:
            result = term if weight > 0 else -term
        else:
            result = result + term if weight > 0 else result - term
    return result


def class_signals(blocks):
    parties = len(blocks)
    middle = parties // 2
    sums = [blocks[i] + blocks[i + middle] for i in range(middle)]
    gaps = [blocks[i] - blocks[i + middle] for i in range(middle)]
    signals = []
    for pair in range(parties):
        if pair == 0:
            even = weighted([(1.0, sums[i]) for i in range(0, middle, 2)])
            odd = weighted([(1.0, sums[i]) for i in range(1, middle, 2)])
            signals.append((even + odd, even - odd))
            continue
        used = blocks if pair % 2 else (sums if pair % 4 == 0 else gaps)
        angles = [math.pi * pair * i / parties for i in range(len(used))]
        real = weighted([(math.cos(a), v) for a, v in zip(angles, used)])
        imag = weighted([(-math.sin(a), v) for a, v in zip(angles, used)])
        signals.append((real, imag))
    return signals


def block_sums(signals):
    parties = len(signals)
    middle = parties // 2
    results = [None] * parties
    for i in range(middle):
        even = {0: [], 2: []}
        for pair in range(0, parties, 2):
            angle = math.pi * pair * i / parties
            real, imag = signals[pair]
            if pair == 0:
                even[0] += [(1.0, real), (1.0 - 2.0 * (i % 2), imag)]
            else:
                even[pair % 4] += [(math.cos(angle), real), (-math.sin(angle), imag)]
        same, flipped = weighted(even[0]), weighted(even[2])
        for place, base in ((i, same + flipped), (i + middle, same - flipped)):
            odd = []
            for pair in range(1, parties, 2):
                angle = math.pi * pair * place / parties
                real, imag = signals[pair]
                odd += [(math.cos(angle), real), (-math.sin(angle), imag)]
            results[place] = base + weighted(odd)
    return results


def hyena_kernel(
    parties,
    query_hbm,
    key_hbm,
    value_hbm,
    taps_hbm,
    skip_hbm,
    spec_hbm,
    fwd_high_hbm,
    fwd_low_hbm,
    bwd_high_hbm,
    bwd_low_hbm,
    out_ref,
    query_ref,
    key_ref,
    value_ref,
    taps_ref,
    skip_ref,
    spec_ref,
    fwd_high,
    fwd_low,
    bwd_high,
    bwd_low,
    edge,
    halo_out,
    halo_query_out,
    halo_in,
    halo_query_in,
    late_out,
    late_in,
    spec_out,
    spec_in,
    spec_scale_out,
    spec_scale_in,
    gated,
    data_out,
    data_in,
    data_scale_out,
    data_scale_in,
    data,
    classes,
    response,
    inverse,
    conv,
    conv_out,
    conv_in,
    conv_scale_out,
    conv_scale_in,
    input_sem,
    table_sem,
    halo_send,
    halo_recv,
    spec_send,
    spec_recv,
    data_send,
    data_recv,
    conv_send,
    conv_recv,
    late_send,
    late_recv,
    spec_scale_send,
    spec_scale_recv,
    data_scale_send,
    data_scale_recv,
    conv_scale_send,
    conv_scale_recv,
):
    me = lax.axis_index("ctx")
    tok_rows, width = query_ref.shape
    owned = width // parties
    chunks, lanes = data_out.shape[0], gated.shape[3]
    group_count = spec_ref.shape[4]
    group_owned = group_count // parties
    group_chunk = group_owned // chunks
    half = tok_rows // 2
    rows = 2 * tok_rows

    barrier = pltpu.get_barrier_semaphore()

    @pl.loop(1, parties)
    def _(step):
        pl.semaphore_signal(
            barrier, inc=1, device_id={"ctx": lax.rem(me + step, parties)}, device_id_type=MESH
        )

    inputs = [
        pltpu.make_async_copy(source, target, input_sem.at[index])
        for index, (source, target) in enumerate(
            (
                (query_hbm.at[tok_rows - 16 :, :], edge.at[0]),
                (key_hbm.at[tok_rows - 16 :, :], edge.at[1]),
                (value_hbm.at[tok_rows - 16 :, :], edge.at[2]),
                (spec_hbm, spec_ref),
                (key_hbm, key_ref),
                (value_hbm, value_ref),
                (taps_hbm, taps_ref),
                (query_hbm, query_ref),
                (skip_hbm, skip_ref),
            )
        )
    ]
    for copy in inputs:
        copy.start()

    for copy in inputs[:3]:
        copy.wait()
    last = edge[...].astype(jnp.float32)[:, 14:16, :]
    halo_out[...] = last[1:].reshape(4, width).astype(jnp.bfloat16)
    halo_query_out[...] = last[0].astype(jnp.bfloat16)
    def halo_copy(source, target, index):
        return pltpu.make_async_remote_copy(
            source,
            target,
            halo_send.at[index],
            halo_recv.at[index],
            device_id={"ctx": lax.rem(me + 1, parties)},
            device_id_type=MESH,
        )

    halo = halo_copy(halo_out, halo_in, 0)
    halo_query = halo_copy(halo_query_out, halo_query_in, 1)

    def spec_copy(target, slot):
        return pltpu.make_async_remote_copy(
            spec_out.at[target],
            spec_in.at[slot],
            spec_send.at[target],
            spec_recv.at[slot],
            device_id={"ctx": target},
            device_id_type=MESH,
        )

    def spec_scale_copy(target, slot):
        return pltpu.make_async_remote_copy(
            spec_scale_out,
            spec_scale_in.at[slot],
            spec_scale_send.at[target],
            spec_scale_recv.at[slot],
            device_id={"ctx": target},
            device_id_type=MESH,
        )

    def data_scale_copy(chunk, target, slot):
        return pltpu.make_async_remote_copy(
            data_scale_out.at[chunk, target],
            data_scale_in.at[chunk, slot],
            data_scale_send.at[chunk, target],
            data_scale_recv.at[chunk, slot],
            device_id={"ctx": target},
            device_id_type=MESH,
        )

    def conv_scale_copy(chunk, target, slot):
        return pltpu.make_async_remote_copy(
            conv_scale_out.at[chunk, target],
            conv_scale_in.at[chunk, slot],
            conv_scale_send.at[chunk, target],
            conv_scale_recv.at[chunk, slot],
            device_id={"ctx": target},
            device_id_type=MESH,
        )

    def data_copy(chunk, target, slot):
        return pltpu.make_async_remote_copy(
            data_out.at[chunk, target],
            data_in.at[chunk, slot],
            data_send.at[chunk, target],
            data_recv.at[chunk, slot],
            device_id={"ctx": target},
            device_id_type=MESH,
        )

    def conv_copy(chunk, target, slot):
        return pltpu.make_async_remote_copy(
            conv_out.at[chunk, target],
            conv_in.at[chunk, slot],
            conv_send.at[chunk, target],
            conv_recv.at[chunk, slot],
            device_id={"ctx": target},
            device_id_type=MESH,
        )

    token = lax.broadcasted_iota(jnp.int32, (tok_rows, lanes), 0)

    def columns_of(target, chunk):
        return pl.ds(pl.multiple_of(target * owned + chunk * lanes, lanes), lanes)

    def rotated(step):
        return lax.rem(me + step + 1, parties)

    def late_copy(target, slot):
        return pltpu.make_async_remote_copy(
            late_out.at[target],
            late_in.at[slot],
            late_send.at[target],
            late_recv.at[slot],
            device_id={"ctx": target},
            device_id_type=MESH,
        )

    def filtered(ref, index, columns, shifted, twice, current):
        taps = taps_ref[index, :, columns]
        return taps[0:1, :] * current + taps[1:2, :] * shifted + taps[2:3, :] * twice

    def inside(ref, index, columns):
        current = ref[:, columns].astype(jnp.float32)
        return filtered(
            ref, index, columns, pltpu.roll(current, 1, 0), pltpu.roll(current, 2, 0), current
        )

    def leading(ref, index, columns, before):
        current = ref[0:16, columns].astype(jnp.float32)[0:2]
        before = before[:, columns].astype(jnp.float32)[2 * index - 2 : 2 * index]
        shifted = jnp.concatenate((before[1:2], current[0:1]), axis=0)
        return filtered(ref, index, columns, shifted, before, current)

    def gate(chunk, target):
        columns = columns_of(target, chunk)
        product = inside(key_ref, 1, columns) * inside(value_ref, 2, columns)
        product = jnp.where(token < 2, jnp.zeros_like(product), product)
        gated[chunk, target] = product
        return product

    for copy in inputs[4:7]:
        copy.wait()

    for chunk in range(chunks):

        @pl.loop(0, parties - 1)
        def _(step, chunk=chunk):
            target = rotated(step)
            product = gate(chunk, target)
            scale = scale_of(product)
            data_scale_out[chunk, target] = scale
            data_out[chunk, target] = encode(product, scale)

        data[chunk, me] = gate(chunk, me)

    inputs[3].wait()
    packed = jnp.concatenate(
        [spec_ref[part, 0, parity, :half, :] for part in range(2) for parity in range(2)], axis=0
    )
    row_index = lax.broadcasted_iota(jnp.int32, packed.shape, 0)
    highest = spec_ref[0, 0, 0, half : half + 1, :]
    packed = jnp.where((row_index == tok_rows) & (me == 0), highest, packed)
    spec_scale = jnp.max(scale_of(packed), axis=1, keepdims=True)
    spec_scale_out[...] = jnp.broadcast_to(spec_scale, (1, lanes))
    codes = packed.T
    spec_out[...] = encode(codes, spec_scale).reshape(spec_out.shape)
    spec_in[me] = spec_out[me]
    spec_scale_in[me] = spec_scale_out[...]

    pl.semaphore_wait(barrier, parties - 1)


    @pl.when(me < parties - 1)
    def _():
        halo.start()
        halo_query.start()

    @pl.loop(0, parties - 1)
    def _(step):
        target = rotated(step)
        spec_copy(target, me).start()
        spec_scale_copy(target, me).start()

    @pl.loop(0, parties - 1)
    def _(step):
        target = rotated(step)
        data_copy(0, target, me).start()
        data_scale_copy(0, target, me).start()

    tables = [
        pltpu.make_async_copy(source, target, table_sem.at[index])
        for index, (source, target) in enumerate(
            (
                (fwd_high_hbm, fwd_high),
                (fwd_low_hbm, fwd_low),
                (bwd_high_hbm, bwd_high),
                (bwd_low_hbm, bwd_low),
            )
        )
    ]
    for table in tables:
        table.start()


    @pl.when(me > 0)
    def _():
        halo.wait_recv()

    @pl.when(me == 0)
    def _():
        halo_in[...] = jnp.zeros_like(halo_in)
        halo_query_in[...] = jnp.zeros_like(halo_query_in)

    def late(chunk, target):
        columns = columns_of(target, chunk)
        rows = leading(key_ref, 1, columns, halo_in) * leading(value_ref, 2, columns, halo_in)
        gated[chunk, target, 0:2, :] = rows
        return rows

    for chunk in range(chunks):
        data[chunk, me, 0:2, :] = late(chunk, me)

    @pl.loop(0, parties - 1)
    def _(step):
        target = rotated(step)
        for chunk in range(chunks):
            late_out[target, chunk] = late(chunk, target)
        late_copy(target, me).start()

    for chunk in range(1, chunks):

        @pl.loop(0, parties - 1)
        def _(step, chunk=chunk):
            target = rotated(step)
            data_copy(chunk, target, me).start()
            data_scale_copy(chunk, target, me).start()

    lane_group = lax.broadcasted_iota(jnp.int32, (3 * group_chunk, lanes), 1) // (
        lanes // group_chunk
    )
    slot_group = lax.broadcasted_iota(jnp.int32, (3 * group_chunk, lanes), 0) % group_chunk
    spread = (lane_group == slot_group).astype(jnp.float32).astype(jnp.bfloat16)

    @pl.loop(1, parties)
    def _(step):
        source = lax.rem(me + step, parties)
        spec_copy(me, source).wait_recv()
        spec_scale_copy(me, source).wait_recv()

    levels = parties.bit_length() - 1
    row = lax.broadcasted_iota(jnp.int32, (rows, lanes), 0)
    for party in range(parties):
        decoded = decode(spec_in[party], spec_scale_in[party, :, :1])
        for chunk in range(chunks):
            exact = decoded[chunk * group_chunk : (chunk + 1) * group_chunk]
            high = exact.astype(jnp.bfloat16).astype(jnp.float32)
            middle = (exact - high).astype(jnp.bfloat16).astype(jnp.float32)
            low = exact - high - middle
            terms = jnp.concatenate((high, middle, low), axis=0).astype(jnp.bfloat16)
            wide = lax.dot_general(
                terms, spread, (((0,), (0,)), ((), ())), preferred_element_type=jnp.float32
            )
            if party == 0:
                ends = lax.rem(row, tok_rows) == 0
                wide = wide * jnp.where(ends, 0.5 / (parties * tok_rows), 1.0 / (parties * tok_rows))
            else:
                wide = wide * (1.0 / (parties * tok_rows))
            for parity in range(2):
                pair, side = place_of(2 * reversed_bits(party, levels) + parity, parties)
                for part in range(2):
                    start = part * tok_rows + parity * half
                    response[chunk, pair, side, part] = wide[start : start + half]

    for table in tables:
        table.wait()

    first = lax.broadcasted_iota(jnp.int32, (half, lanes), 0) == 0
    slab = 16

    for chunk in range(chunks):

        @pl.loop(1, parties)
        def _(step, chunk=chunk):
            source = lax.rem(me + step, parties)
            data_scale_copy(chunk, me, source).wait_recv()
            data_copy(chunk, me, source).wait_recv()
            data[chunk, source] = decode(data_in[chunk, source], data_scale_in[chunk, source])
            if chunk == 0:
                late_copy(me, source).wait_recv()
            data[chunk, source, 0:2, :] = late_in[source, chunk]

        @pl.loop(0, tok_rows // slab)
        def _(step, chunk=chunk):
            here = pl.ds(pl.multiple_of(step * slab, slab), slab)
            blocks = [data[chunk, party, here, :] for party in range(parties)]
            for pair, signals in enumerate(class_signals(blocks)):
                for side, signal in enumerate(signals):
                    classes[chunk, pair, side, here, :] = jnp.concatenate(
                        split_terms(signal), axis=1
                    )

        @pl.loop(0, parties, unroll=4)
        def _(pair, chunk=chunk):
            signal = classes[chunk, pair].reshape(rows, 2 * lanes)
            wide = jnp.dot(fwd_high[pair], signal, preferred_element_type=jnp.float32)
            rest = jnp.dot(fwd_low[pair], signal[:, :lanes], preferred_element_type=jnp.float32)
            spectrum = wide[:, :lanes] + wide[:, lanes:] + rest
            products = []
            for side in range(2):
                data_re = spectrum[side * tok_rows : side * tok_rows + half]
                data_im = spectrum[side * tok_rows + half : (side + 1) * tok_rows]
                resp_re, resp_im = response[chunk, pair, side, 0], response[chunk, pair, side, 1]
                both_re, both_im = data_re * resp_re, data_im * resp_im
                cross = data_re * resp_im + data_im * resp_re
                if side == 0:
                    alone = first & (pair == 0)
                    products.append(both_re - jnp.where(alone, jnp.zeros_like(both_im), both_im))
                    products.append(jnp.where(alone, both_im, cross))
                else:
                    products += [both_re - both_im, cross]
            product = jnp.concatenate(split_terms(jnp.concatenate(products, axis=0)), axis=1)
            wide = jnp.dot(bwd_high[pair], product, preferred_element_type=jnp.float32)
            rest = jnp.dot(bwd_low[pair], product[:, :lanes], preferred_element_type=jnp.float32)
            result = wide[:, :lanes] + wide[:, lanes:] + rest
            inverse[chunk, pair] = result.reshape(2, tok_rows, lanes)

        @pl.loop(0, tok_rows // slab)
        def _(step, chunk=chunk):
            here = pl.ds(pl.multiple_of(step * slab, slab), slab)
            signals = [
                (inverse[chunk, pair, 0, here, :], inverse[chunk, pair, 1, here, :])
                for pair in range(parties)
            ]
            for party, result in enumerate(block_sums(signals)):
                conv[chunk, party, here, :] = result

        @pl.loop(0, parties - 1)
        def _(step, chunk=chunk):
            target = rotated(step)
            result = conv[chunk, target]
            scale = scale_of(result)
            conv_scale_out[chunk, target] = scale
            conv_out[chunk, target] = encode(result, scale)
            conv_copy(chunk, target, me).start()
            conv_scale_copy(chunk, target, me).start()

    @pl.when(me > 0)
    def _():
        halo_query.wait_recv()

    for copy in inputs[7:]:
        copy.wait()

    def short(ref, index, columns):
        current = ref[:, columns].astype(jnp.float32)
        before = halo_query_in[:, columns].astype(jnp.float32)
        shifted = jnp.where(token == 0, before[1:2, :], pltpu.roll(current, 1, 0))
        twice = jnp.where(token == 0, before[0:1, :], pltpu.roll(current, 2, 0))
        twice = jnp.where(token == 1, before[1:2, :], twice)
        taps = taps_ref[index, :, columns]
        return taps[0:1, :] * current + taps[1:2, :] * shifted + taps[2:3, :] * twice

    def finish(chunk, source, conv):
        columns = columns_of(source, chunk)
        mixed = conv + skip_ref[:, columns] * gated[chunk, source]
        out_ref[:, columns] = (short(query_ref, 0, columns) * mixed).astype(jnp.bfloat16)

    for chunk in range(chunks):
        finish(chunk, me, conv[chunk, me])

        @pl.loop(1, parties)
        def _(step, chunk=chunk):
            source = lax.rem(me + step, parties)
            conv_scale_copy(chunk, me, source).wait_recv()
            conv_copy(chunk, me, source).wait_recv()
            finish(chunk, source, decode(conv_in[chunk, source], conv_scale_in[chunk, source]))

    @pl.when(me < parties - 1)
    def _():
        halo.wait_send()
        halo_query.wait_send()

    @pl.loop(1, parties)
    def _(step):
        target = lax.rem(me + step, parties)
        late_copy(target, me).wait_send()
        spec_copy(target, me).wait_send()
        spec_scale_copy(target, me).wait_send()
        for chunk in range(chunks):
            data_copy(chunk, target, me).wait_send()
            data_scale_copy(chunk, target, me).wait_send()
            conv_copy(chunk, target, me).wait_send()
            conv_scale_copy(chunk, target, me).wait_send()


def one_kernel(tables, query_in, key_in, value_in, short_filter, skip_bias, filter_spectrum):
    tok_rows, width = query_in.shape
    parties = lax.axis_size("ctx")
    group_count = filter_spectrum.shape[4]
    lanes = 128
    chunks = width // parties // lanes
    vmem = pl.BlockSpec(memory_space=pltpu.VMEM)
    hbm = pl.BlockSpec(memory_space=pltpu.HBM)
    f32, bf16 = jnp.float32, jnp.bfloat16
    dma = pltpu.SemaphoreType.DMA
    return pl.pallas_call(
        functools.partial(hyena_kernel, parties),
        out_shape=pltpu.VMEM((tok_rows, width), bf16),
        in_specs=[hbm] * 10,
        out_specs=vmem,
        scratch_shapes=[
            *[pltpu.VMEM((tok_rows, width), bf16)] * 3,
            pltpu.VMEM(short_filter.shape, f32),
            pltpu.VMEM((1, width), f32),
            pltpu.VMEM(filter_spectrum.shape, f32),
            *[pltpu.VMEM((parties, 2 * tok_rows, 2 * tok_rows), bf16)] * 4,
            pltpu.VMEM((3, 16, width), bf16),
            pltpu.VMEM((4, width), bf16),
            pltpu.VMEM((2, width), bf16),
            pltpu.VMEM((4, width), bf16),
            pltpu.VMEM((2, width), bf16),
            *[pltpu.VMEM((parties, chunks, 2, lanes), f32)] * 2,
            *[pltpu.VMEM((parties, group_count // parties, 2 * tok_rows), bf16)] * 2,
            pltpu.VMEM((1, lanes), f32),
            pltpu.VMEM((parties, 1, lanes), f32),
            pltpu.VMEM((chunks, parties, tok_rows, lanes), f32),
            *[pltpu.VMEM((chunks, parties, tok_rows, lanes), bf16)] * 2,
            *[pltpu.VMEM((chunks, parties, 1, lanes), f32)] * 2,
            pltpu.VMEM((chunks, parties, tok_rows, lanes), f32),
            pltpu.VMEM((chunks, parties, 2, tok_rows, 2 * lanes), bf16),
            pltpu.VMEM((chunks, parties, 2, 2, tok_rows // 2, lanes), f32),
            pltpu.VMEM((chunks, parties, 2, tok_rows, lanes), f32),
            pltpu.VMEM((chunks, parties, tok_rows, lanes), f32),
            *[pltpu.VMEM((chunks, parties, tok_rows, lanes), bf16)] * 2,
            *[pltpu.VMEM((chunks, parties, 1, lanes), f32)] * 2,
            dma((9,)),
            dma((4,)),
            dma((2,)),
            dma((2,)),
            dma((parties,)),
            dma((parties,)),
            *[dma((chunks, parties))] * 4,
            *[dma((parties,))] * 4,
            *[dma((chunks, parties))] * 4,
        ],
        compiler_params=pltpu.CompilerParams(
            collective_id=0, has_side_effects=True, vmem_limit_bytes=56 * 1024 * 1024
        ),
    )(
        query_in,
        key_in,
        value_in,
        short_filter,
        skip_bias.reshape(1, width),
        filter_spectrum,
        *[jnp.asarray(table) for table in tables],
    )


def solution(mesh):
    parties = mesh.shape["ctx"]

    def per_device(*args):
        tok_rows, width = args[0].shape
        if width // parties % 128 == 0:
            return one_kernel(transform_tables(parties, tok_rows), *args)
        return on_device(*args)

    return jax.shard_map(
        per_device,
        mesh=mesh,
        in_specs=(
            P(("grp", "ctx"), "ch"),
            P(("grp", "ctx"), "ch"),
            P(("grp", "ctx"), "ch"),
            P(None, None, "ch"),
            P("ch"),
            P(None, "ctx", None, None, "ch"),
        ),
        out_specs=P(("grp", "ctx"), "ch"),
        check_vma=False,
    )
```

```python
import functools
import math

import jax
import jax.numpy as jnp
import ml_dtypes
import numpy as np
from jax import lax
from jax.experimental import pallas as pl
from jax.experimental.pallas import tpu as pltpu
from jax.sharding import PartitionSpec as P

HIGHEST = lax.Precision.HIGHEST
MESH = pl.DeviceIdType.MESH
POWER = 17
REACH = 2.0 ** (126 / POWER)


def passed_along(value, axis, steps):
    count = lax.axis_size(axis)
    leading, last = (max(0, -steps), min(count, count - steps))
    return lax.ppermute(value, axis, [(source, source + steps) for source in range(leading, last)])


def reversed_bits(number, digits):
    result = number * 0
    for bit_level in range(digits):
        result = result + (number >> bit_level & 1) * (1 << digits - 1 - bit_level)
    return result


def rotate(real_part, imag_part, cosine, sine):
    return (real_part * cosine - imag_part * sine, real_part * sine + imag_part * cosine)


def complex_product(pattern, table_real, table_imag, data_real, data_imag):
    out_real = jnp.einsum(pattern, table_real, data_real, precision=HIGHEST) - jnp.einsum(
        pattern, table_imag, data_imag, precision=HIGHEST
    )
    out_imag = jnp.einsum(pattern, table_real, data_imag, precision=HIGHEST) + jnp.einsum(
        pattern, table_imag, data_real, precision=HIGHEST
    )
    return (out_real, out_imag)


def angle_table(rows, cols, modulus):
    exponent = (
        jnp.arange(rows, dtype=jnp.int32)[:, None]
        * jnp.arange(cols, dtype=jnp.int32)[None, :]
        % modulus
    )
    angle = 2.0 * math.pi / modulus * exponent.astype(jnp.float32)
    return (jnp.cos(angle), jnp.sin(angle))


def whole_convolution(first_real, first_imag, filter_spectrum, parties, levels):
    tok_rows = first_real.shape[0]
    packed = jnp.stack((first_real, first_imag))
    spread = lax.all_to_all(packed, "ctx", split_axis=2, concat_axis=1, tiled=True)
    spectrum = lax.all_to_all(filter_spectrum, "ctx", split_axis=4, concat_axis=1, tiled=True)
    tail = spectrum.shape[2:]
    spectrum = spectrum.reshape(2, *[2] * levels, *tail)
    spectrum = spectrum.transpose(0, *range(levels, 0, -1), *range(levels + 1, levels + 4))
    spectrum = spectrum.reshape(2, parties, *tail)
    size_b = 2 * parties
    total = tok_rows * size_b
    spectrum = spectrum.reshape(2, size_b, tok_rows, spectrum.shape[4])
    columns = spread.shape[2]
    data = spread.reshape(2, size_b // 2, tok_rows, columns)
    outer_cos, outer_sin = angle_table(size_b, size_b // 2, size_b)
    twist_cos, twist_sin = angle_table(size_b, tok_rows, total)
    inner_cos, inner_sin = angle_table(tok_rows, tok_rows, tok_rows)
    section_real, section_imag = complex_product(
        "fn,nac->fac", outer_cos, -outer_sin, data[0], data[1]
    )
    section_real, section_imag = rotate(
        section_real, section_imag, twist_cos[..., None], -twist_sin[..., None]
    )
    freq_real, freq_imag = complex_product(
        "ak,fac->fkc", inner_cos, -inner_sin, section_real, section_imag
    )
    group_local = spectrum.shape[3]
    per_group = columns // group_local
    shaped_real = freq_real.reshape(size_b, tok_rows, group_local, per_group)
    shaped_imag = freq_imag.reshape(size_b, tok_rows, group_local, per_group)
    resp_real = spectrum[0][..., None]
    resp_imag = spectrum[1][..., None]
    prod_real = (shaped_real * resp_real - shaped_imag * resp_imag).reshape(
        size_b, tok_rows, columns
    )
    prod_imag = (shaped_real * resp_imag + shaped_imag * resp_real).reshape(
        size_b, tok_rows, columns
    )
    back_real, back_imag = complex_product(
        "ak,fkc->fac", inner_cos, inner_sin, prod_real, prod_imag
    )
    back_real, back_imag = rotate(back_real, back_imag, twist_cos[..., None], twist_sin[..., None])
    out_real, out_imag = complex_product(
        "nf,fac->nac", outer_cos.T, outer_sin.T, back_real, back_imag
    )
    norm_factor = 1.0 / total
    result = (
        jnp.stack(
            (
                out_real.reshape(size_b // 2 * tok_rows, columns),
                out_imag.reshape(size_b // 2 * tok_rows, columns),
            )
        )
        * norm_factor
    )
    returned = lax.all_to_all(result, "ctx", split_axis=1, concat_axis=2, tiled=True)
    return (returned[0], returned[1])


def on_device(query_in, key_in, value_in, short_filter, skip_bias, filter_spectrum):
    tok_rows, chan_width = query_in.shape
    parties = lax.axis_size("ctx")
    levels = parties.bit_length() - 1
    tap_count = short_filter.shape[1]
    group_count = filter_spectrum.shape[4]
    half_group = chan_width // (2 * group_count)
    packed_width = group_count * half_group
    stacked = jnp.stack((query_in, key_in, value_in))
    earlier = passed_along(stacked[:, tok_rows - (tap_count - 1) :, :], "ctx", 1)
    extended = jnp.concatenate((earlier, stacked), axis=1).astype(jnp.float32)
    filtered = short_filter[:, 0, None, :] * extended[:, tap_count - 1 :, :]
    for tap_lag in range(1, tap_count):
        start_row = tap_count - 1 - tap_lag
        filtered = (
            filtered
            + short_filter[:, tap_lag, None, :] * extended[:, start_row : start_row + tok_rows, :]
        )
    gated = filtered[1] * filtered[2]
    halves = gated.reshape(tok_rows, group_count, 2, half_group)
    first_real = halves[:, :, 0, :].reshape(tok_rows, packed_width)
    first_imag = halves[:, :, 1, :].reshape(tok_rows, packed_width)
    conv_real, conv_imag = whole_convolution(
        first_real, first_imag, filter_spectrum, parties, levels
    )
    conv = jnp.stack(
        (
            conv_real.reshape(tok_rows, group_count, half_group),
            conv_imag.reshape(tok_rows, group_count, half_group),
        ),
        axis=2,
    ).reshape(tok_rows, chan_width)
    return (filtered[0] * (conv + skip_bias[None, :] * gated)).astype(jnp.bfloat16)


def split_terms(value):
    high = value.astype(jnp.bfloat16)
    low = (value - high.astype(jnp.float32)).astype(jnp.bfloat16)
    return high, low


def scale_of(value):
    peak = jnp.max(jnp.abs(value), axis=0, keepdims=True)
    return jnp.maximum(peak * 1.0078125, 2.0**-100)


def encode(value, scale):
    ratio = value * (REACH / scale)
    square = ratio * ratio
    fourth = square * square
    eighth = fourth * fourth
    return (ratio * (eighth * eighth)).astype(jnp.bfloat16)


def decode(block, scale):
    code = block.astype(jnp.float32)
    root = jnp.exp(jnp.log(jnp.maximum(jnp.abs(code), 2.0**-126)) * (1.0 / POWER))
    root = root * (scale * (1.0 / REACH))
    return jnp.where(code < 0, -root, jnp.where(code > 0, root, jnp.zeros_like(root)))


def place_of(rho, parties):
    if rho % parties == 0:
        return 0, rho // parties
    return (rho, 0) if rho < parties else (2 * parties - rho, 1)


def transform_tables(parties, tok_rows):
    classes, half = 2 * parties, tok_rows // 2
    total = classes * tok_rows
    time = np.arange(tok_rows)
    table = np.zeros((parties, 2, 2, half, 2, tok_rows))
    for rho in range(classes):
        pair, side = place_of(rho, parties)
        angle = 2.0 * np.pi / total * ((classes * np.arange(half)[:, None] + rho) * time % total)
        cosine, sine = np.cos(angle), np.sin(angle)
        if pair == 0:
            table[pair, side, 0, :, side] = cosine
            table[pair, side, 1, :, side] = -sine
        else:
            sign = 1.0 - 2.0 * side
            table[pair, side, 0, :, 0] = cosine
            table[pair, side, 0, :, 1] = sign * sine
            table[pair, side, 1, :, 0] = -sine
            table[pair, side, 1, :, 1] = sign * cosine
    table[0, 0, 1, 0, 0] = 1.0 - 2.0 * (time % 2)
    forward = table.reshape(parties, 2 * tok_rows, 2 * tok_rows)

    def parts(matrix):
        high = matrix.astype(ml_dtypes.bfloat16)
        low = (matrix - high.astype(np.float64)).astype(ml_dtypes.bfloat16)
        return high, low

    return parts(forward) + parts(np.ascontiguousarray(forward.transpose(0, 2, 1)))


def weighted(terms):
    result = None
    for weight, value in terms:
        if abs(weight) < 1e-12:
            continue
        if abs(abs(weight) - 1.0) > 1e-12:
            term = value * abs(weight)
        else:
            term = value
        if result is None:
            result = term if weight > 0 else -term
        else:
            result = result + term if weight > 0 else result - term
    return result


def class_signals(blocks):
    parties = len(blocks)
    middle = parties // 2
    sums = [blocks[i] + blocks[i + middle] for i in range(middle)]
    gaps = [blocks[i] - blocks[i + middle] for i in range(middle)]
    signals = []
    for pair in range(parties):
        if pair == 0:
            even = weighted([(1.0, sums[i]) for i in range(0, middle, 2)])
            odd = weighted([(1.0, sums[i]) for i in range(1, middle, 2)])
            signals.append((even + odd, even - odd))
            continue
        used = blocks if pair % 2 else (sums if pair % 4 == 0 else gaps)
        angles = [math.pi * pair * i / parties for i in range(len(used))]
        real = weighted([(math.cos(a), v) for a, v in zip(angles, used)])
        imag = weighted([(-math.sin(a), v) for a, v in zip(angles, used)])
        signals.append((real, imag))
    return signals


def block_sums(signals):
    parties = len(signals)
    middle = parties // 2
    results = [None] * parties
    for i in range(middle):
        even = {0: [], 2: []}
        for pair in range(0, parties, 2):
            angle = math.pi * pair * i / parties
            real, imag = signals[pair]
            if pair == 0:
                even[0] += [(1.0, real), (1.0 - 2.0 * (i % 2), imag)]
            else:
                even[pair % 4] += [(math.cos(angle), real), (-math.sin(angle), imag)]
        same, flipped = weighted(even[0]), weighted(even[2])
        for place, base in ((i, same + flipped), (i + middle, same - flipped)):
            odd = []
            for pair in range(1, parties, 2):
                angle = math.pi * pair * place / parties
                real, imag = signals[pair]
                odd += [(math.cos(angle), real), (-math.sin(angle), imag)]
            results[place] = base + weighted(odd)
    return results


def hyena_kernel(
    parties,
    query_hbm,
    key_hbm,
    value_hbm,
    taps_hbm,
    skip_hbm,
    spec_hbm,
    fwd_high_hbm,
    fwd_low_hbm,
    bwd_high_hbm,
    bwd_low_hbm,
    out_ref,
    query_ref,
    key_ref,
    value_ref,
    taps_ref,
    skip_ref,
    spec_ref,
    fwd_high,
    fwd_low,
    bwd_high,
    bwd_low,
    edge,
    halo_out,
    halo_query_out,
    halo_in,
    halo_query_in,
    late_out,
    late_in,
    spec_out,
    spec_in,
    spec_scale_out,
    spec_scale_in,
    gated,
    data_out,
    data_in,
    data_scale_out,
    data_scale_in,
    data,
    classes,
    response,
    inverse,
    conv,
    conv_out,
    conv_in,
    conv_scale_out,
    conv_scale_in,
    input_sem,
    table_sem,
    halo_send,
    halo_recv,
    spec_send,
    spec_recv,
    data_send,
    data_recv,
    conv_send,
    conv_recv,
    late_send,
    late_recv,
    relay_send,
    relay_recv,
    spec_scale_send,
    spec_scale_recv,
    data_scale_send,
    data_scale_recv,
    conv_scale_send,
    conv_scale_recv,
):
    me = lax.axis_index("ctx")
    plane = lax.axis_index("grp")
    tok_rows, width = query_ref.shape
    owned = width // parties
    chunks, lanes = data_out.shape[0], gated.shape[3]
    group_count = spec_ref.shape[4]
    group_owned = group_count // parties
    group_chunk = group_owned // chunks
    half = tok_rows // 2
    rows = 2 * tok_rows

    barrier = pltpu.get_barrier_semaphore()

    @pl.loop(1, parties)
    def _(step):
        pl.semaphore_signal(
            barrier, inc=1, device_id={"ctx": lax.rem(me + step, parties)}, device_id_type=MESH
        )

    pl.semaphore_signal(barrier, inc=1, device_id={"grp": 1 - plane}, device_id_type=MESH)

    inputs = [
        pltpu.make_async_copy(source, target, input_sem.at[index])
        for index, (source, target) in enumerate(
            (
                (query_hbm.at[tok_rows - 16 :, :], edge.at[0]),
                (key_hbm.at[tok_rows - 16 :, :], edge.at[1]),
                (value_hbm.at[tok_rows - 16 :, :], edge.at[2]),
                (spec_hbm, spec_ref),
                (key_hbm, key_ref),
                (value_hbm, value_ref),
                (taps_hbm, taps_ref),
                (query_hbm, query_ref),
                (skip_hbm, skip_ref),
            )
        )
    ]
    for copy in inputs:
        copy.start()

    for copy in inputs[:3]:
        copy.wait()
    last = edge[...].astype(jnp.float32)[:, 14:16, :]
    halo_out[...] = last[1:].reshape(4, width).astype(jnp.bfloat16)
    halo_query_out[...] = last[0].astype(jnp.bfloat16)
    def halo_copy(source, target, index):
        return pltpu.make_async_remote_copy(
            source,
            target,
            halo_send.at[index],
            halo_recv.at[index],
            device_id={"ctx": lax.rem(me + 1, parties)},
            device_id_type=MESH,
        )

    halo = halo_copy(halo_out, halo_in, 0)
    halo_query = halo_copy(halo_query_out, halo_query_in, 1)

    def spec_copy(target, slot):
        return pltpu.make_async_remote_copy(
            spec_out.at[plane, target],
            spec_in.at[plane, slot],
            spec_send.at[target],
            spec_recv.at[slot],
            device_id={"ctx": target},
            device_id_type=MESH,
        )

    def relay_copy(part, source):
        return pltpu.make_async_remote_copy(
            spec_in.at[part, source],
            spec_in.at[part, source],
            relay_send.at[source],
            relay_recv.at[source],
            device_id={"grp": 1 - plane},
            device_id_type=MESH,
        )

    def spec_scale_copy(target, slot):
        return pltpu.make_async_remote_copy(
            spec_scale_out,
            spec_scale_in.at[slot],
            spec_scale_send.at[target],
            spec_scale_recv.at[slot],
            device_id={"ctx": target},
            device_id_type=MESH,
        )

    def data_scale_copy(chunk, target, slot):
        return pltpu.make_async_remote_copy(
            data_scale_out.at[chunk, target],
            data_scale_in.at[chunk, slot],
            data_scale_send.at[chunk, target],
            data_scale_recv.at[chunk, slot],
            device_id={"ctx": target},
            device_id_type=MESH,
        )

    def conv_scale_copy(chunk, target, slot):
        return pltpu.make_async_remote_copy(
            conv_scale_out.at[chunk, target],
            conv_scale_in.at[chunk, slot],
            conv_scale_send.at[chunk, target],
            conv_scale_recv.at[chunk, slot],
            device_id={"ctx": target},
            device_id_type=MESH,
        )

    def data_copy(chunk, target, slot):
        return pltpu.make_async_remote_copy(
            data_out.at[chunk, target],
            data_in.at[chunk, slot],
            data_send.at[chunk, target],
            data_recv.at[chunk, slot],
            device_id={"ctx": target},
            device_id_type=MESH,
        )

    def conv_copy(chunk, target, slot):
        return pltpu.make_async_remote_copy(
            conv_out.at[chunk, target],
            conv_in.at[chunk, slot],
            conv_send.at[chunk, target],
            conv_recv.at[chunk, slot],
            device_id={"ctx": target},
            device_id_type=MESH,
        )

    token = lax.broadcasted_iota(jnp.int32, (tok_rows, lanes), 0)

    def columns_of(target, chunk):
        return pl.ds(pl.multiple_of(target * owned + chunk * lanes, lanes), lanes)

    def rotated(step):
        return lax.rem(me + step + 1, parties)

    def late_copy(target, slot):
        return pltpu.make_async_remote_copy(
            late_out.at[target],
            late_in.at[slot],
            late_send.at[target],
            late_recv.at[slot],
            device_id={"ctx": target},
            device_id_type=MESH,
        )

    def filtered(ref, index, columns, shifted, twice, current):
        taps = taps_ref[index, :, columns]
        return taps[0:1, :] * current + taps[1:2, :] * shifted + taps[2:3, :] * twice

    def inside(ref, index, columns):
        current = ref[:, columns].astype(jnp.float32)
        return filtered(
            ref, index, columns, pltpu.roll(current, 1, 0), pltpu.roll(current, 2, 0), current
        )

    def leading(ref, index, columns, before):
        current = ref[0:16, columns].astype(jnp.float32)[0:2]
        before = before[:, columns].astype(jnp.float32)[2 * index - 2 : 2 * index]
        shifted = jnp.concatenate((before[1:2], current[0:1]), axis=0)
        return filtered(ref, index, columns, shifted, before, current)

    def gate(chunk, target):
        columns = columns_of(target, chunk)
        product = inside(key_ref, 1, columns) * inside(value_ref, 2, columns)
        product = jnp.where(token < 2, jnp.zeros_like(product), product)
        gated[chunk, target] = product
        return product

    for copy in inputs[4:7]:
        copy.wait()

    for chunk in range(chunks):

        @pl.loop(0, parties - 1)
        def _(step, chunk=chunk):
            target = rotated(step)
            product = gate(chunk, target)
            scale = scale_of(product)
            data_scale_out[chunk, target] = scale
            data_out[chunk, target] = encode(product, scale)

        data[chunk, me] = gate(chunk, me)

    inputs[3].wait()
    packed = jnp.concatenate(
        [spec_ref[part, 0, parity, :half, :] for part in range(2) for parity in range(2)], axis=0
    )
    row_index = lax.broadcasted_iota(jnp.int32, packed.shape, 0)
    highest = spec_ref[0, 0, 0, half : half + 1, :]
    packed = jnp.where((row_index == tok_rows) & (me == 0), highest, packed)
    spec_scale = jnp.max(scale_of(packed), axis=1, keepdims=True)
    spec_scale_out[...] = jnp.broadcast_to(spec_scale, (1, lanes))
    codes = packed.T
    codes = encode(codes, spec_scale)
    for part in range(2):
        columns = codes[:, part * tok_rows : (part + 1) * tok_rows]
        spec_out[part] = columns.reshape(spec_out.shape[1:])
        spec_in[part, me] = spec_out[part, me]
    spec_scale_in[me] = spec_scale_out[...]

    pl.semaphore_wait(barrier, parties)


    @pl.when(me < parties - 1)
    def _():
        halo.start()
        halo_query.start()

    @pl.loop(0, parties - 1)
    def _(step):
        target = rotated(step)
        spec_copy(target, me).start()
        spec_scale_copy(target, me).start()

    @pl.loop(0, parties - 1)
    def _(step):
        target = rotated(step)
        data_copy(0, target, me).start()
        data_scale_copy(0, target, me).start()

    tables = [
        pltpu.make_async_copy(source, target, table_sem.at[index])
        for index, (source, target) in enumerate(
            (
                (fwd_high_hbm, fwd_high),
                (fwd_low_hbm, fwd_low),
                (bwd_high_hbm, bwd_high),
                (bwd_low_hbm, bwd_low),
            )
        )
    ]
    for table in tables:
        table.start()


    @pl.when(me > 0)
    def _():
        halo.wait_recv()

    @pl.when(me == 0)
    def _():
        halo_in[...] = jnp.zeros_like(halo_in)
        halo_query_in[...] = jnp.zeros_like(halo_query_in)

    def late(chunk, target):
        columns = columns_of(target, chunk)
        rows = leading(key_ref, 1, columns, halo_in) * leading(value_ref, 2, columns, halo_in)
        gated[chunk, target, 0:2, :] = rows
        return rows

    for chunk in range(chunks):
        data[chunk, me, 0:2, :] = late(chunk, me)

    @pl.loop(0, parties - 1)
    def _(step):
        target = rotated(step)
        for chunk in range(chunks):
            late_out[target, chunk] = late(chunk, target)
        late_copy(target, me).start()

    for chunk in range(1, chunks):

        @pl.loop(0, parties - 1)
        def _(step, chunk=chunk):
            target = rotated(step)
            data_copy(chunk, target, me).start()
            data_scale_copy(chunk, target, me).start()

    lane_group = lax.broadcasted_iota(jnp.int32, (3 * group_chunk, lanes), 1) // (
        lanes // group_chunk
    )
    slot_group = lax.broadcasted_iota(jnp.int32, (3 * group_chunk, lanes), 0) % group_chunk
    spread = (lane_group == slot_group).astype(jnp.float32).astype(jnp.bfloat16)

    @pl.loop(1, parties)
    def _(step):
        source = lax.rem(me + parties - step, parties)
        spec_copy(me, source).wait_recv()
        relay_copy(plane, source).start()
        spec_scale_copy(me, source).wait_recv()

    @pl.loop(1, parties)
    def _(step):
        relay_copy(1 - plane, lax.rem(me + parties - step, parties)).wait_recv()

    levels = parties.bit_length() - 1
    row = lax.broadcasted_iota(jnp.int32, (rows, lanes), 0)
    for party in range(parties):
        codes = jnp.concatenate((spec_in[0, party], spec_in[1, party]), axis=1)
        decoded = decode(codes, spec_scale_in[party, :, :1])
        for chunk in range(chunks):
            exact = decoded[chunk * group_chunk : (chunk + 1) * group_chunk]
            high = exact.astype(jnp.bfloat16).astype(jnp.float32)
            middle = (exact - high).astype(jnp.bfloat16).astype(jnp.float32)
            low = exact - high - middle
            terms = jnp.concatenate((high, middle, low), axis=0).astype(jnp.bfloat16)
            wide = lax.dot_general(
                terms, spread, (((0,), (0,)), ((), ())), preferred_element_type=jnp.float32
            )
            if party == 0:
                ends = lax.rem(row, tok_rows) == 0
                wide = wide * jnp.where(ends, 0.5 / (parties * tok_rows), 1.0 / (parties * tok_rows))
            else:
                wide = wide * (1.0 / (parties * tok_rows))
            for parity in range(2):
                pair, side = place_of(2 * reversed_bits(party, levels) + parity, parties)
                for part in range(2):
                    start = part * tok_rows + parity * half
                    response[chunk, pair, side, part] = wide[start : start + half]

    for table in tables:
        table.wait()

    first = lax.broadcasted_iota(jnp.int32, (half, lanes), 0) == 0
    slab = 16

    for chunk in range(chunks):

        @pl.loop(1, parties)
        def _(step, chunk=chunk):
            source = lax.rem(me + step, parties)
            data_scale_copy(chunk, me, source).wait_recv()
            data_copy(chunk, me, source).wait_recv()
            data[chunk, source] = decode(data_in[chunk, source], data_scale_in[chunk, source])
            if chunk == 0:
                late_copy(me, source).wait_recv()
            data[chunk, source, 0:2, :] = late_in[source, chunk]

        @pl.loop(0, tok_rows // slab)
        def _(step, chunk=chunk):
            here = pl.ds(pl.multiple_of(step * slab, slab), slab)
            blocks = [data[chunk, party, here, :] for party in range(parties)]
            for pair, signals in enumerate(class_signals(blocks)):
                for side, signal in enumerate(signals):
                    classes[chunk, pair, side, here, :] = jnp.concatenate(
                        split_terms(signal), axis=1
                    )

        @pl.loop(0, parties, unroll=4)
        def _(pair, chunk=chunk):
            signal = classes[chunk, pair].reshape(rows, 2 * lanes)
            wide = jnp.dot(fwd_high[pair], signal, preferred_element_type=jnp.float32)
            rest = jnp.dot(fwd_low[pair], signal[:, :lanes], preferred_element_type=jnp.float32)
            spectrum = wide[:, :lanes] + wide[:, lanes:] + rest
            products = []
            for side in range(2):
                data_re = spectrum[side * tok_rows : side * tok_rows + half]
                data_im = spectrum[side * tok_rows + half : (side + 1) * tok_rows]
                resp_re, resp_im = response[chunk, pair, side, 0], response[chunk, pair, side, 1]
                both_re, both_im = data_re * resp_re, data_im * resp_im
                cross = data_re * resp_im + data_im * resp_re
                if side == 0:
                    alone = first & (pair == 0)
                    products.append(both_re - jnp.where(alone, jnp.zeros_like(both_im), both_im))
                    products.append(jnp.where(alone, both_im, cross))
                else:
                    products += [both_re - both_im, cross]
            product = jnp.concatenate(split_terms(jnp.concatenate(products, axis=0)), axis=1)
            wide = jnp.dot(bwd_high[pair], product, preferred_element_type=jnp.float32)
            rest = jnp.dot(bwd_low[pair], product[:, :lanes], preferred_element_type=jnp.float32)
            result = wide[:, :lanes] + wide[:, lanes:] + rest
            inverse[chunk, pair] = result.reshape(2, tok_rows, lanes)

        @pl.loop(0, tok_rows // slab)
        def _(step, chunk=chunk):
            here = pl.ds(pl.multiple_of(step * slab, slab), slab)
            signals = [
                (inverse[chunk, pair, 0, here, :], inverse[chunk, pair, 1, here, :])
                for pair in range(parties)
            ]
            for party, result in enumerate(block_sums(signals)):
                conv[chunk, party, here, :] = result

        @pl.loop(0, parties - 1)
        def _(step, chunk=chunk):
            target = rotated(step)
            result = conv[chunk, target]
            scale = scale_of(result)
            conv_scale_out[chunk, target] = scale
            conv_out[chunk, target] = encode(result, scale)
            conv_copy(chunk, target, me).start()
            conv_scale_copy(chunk, target, me).start()

    @pl.when(me > 0)
    def _():
        halo_query.wait_recv()

    for copy in inputs[7:]:
        copy.wait()

    def short(ref, index, columns):
        current = ref[:, columns].astype(jnp.float32)
        before = halo_query_in[:, columns].astype(jnp.float32)
        shifted = jnp.where(token == 0, before[1:2, :], pltpu.roll(current, 1, 0))
        twice = jnp.where(token == 0, before[0:1, :], pltpu.roll(current, 2, 0))
        twice = jnp.where(token == 1, before[1:2, :], twice)
        taps = taps_ref[index, :, columns]
        return taps[0:1, :] * current + taps[1:2, :] * shifted + taps[2:3, :] * twice

    def finish(chunk, source, conv):
        columns = columns_of(source, chunk)
        mixed = conv + skip_ref[:, columns] * gated[chunk, source]
        out_ref[:, columns] = (short(query_ref, 0, columns) * mixed).astype(jnp.bfloat16)

    for chunk in range(chunks):
        finish(chunk, me, conv[chunk, me])

        @pl.loop(1, parties)
        def _(step, chunk=chunk):
            source = lax.rem(me + step, parties)
            conv_scale_copy(chunk, me, source).wait_recv()
            conv_copy(chunk, me, source).wait_recv()
            finish(chunk, source, decode(conv_in[chunk, source], conv_scale_in[chunk, source]))

    @pl.when(me < parties - 1)
    def _():
        halo.wait_send()
        halo_query.wait_send()

    @pl.loop(1, parties)
    def _(step):
        target = lax.rem(me + step, parties)
        late_copy(target, me).wait_send()
        spec_copy(target, me).wait_send()
        relay_copy(plane, target).wait_send()
        spec_scale_copy(target, me).wait_send()
        for chunk in range(chunks):
            data_copy(chunk, target, me).wait_send()
            data_scale_copy(chunk, target, me).wait_send()
            conv_copy(chunk, target, me).wait_send()
            conv_scale_copy(chunk, target, me).wait_send()


def one_kernel(tables, query_in, key_in, value_in, short_filter, skip_bias, filter_spectrum):
    tok_rows, width = query_in.shape
    parties = lax.axis_size("ctx")
    group_count = filter_spectrum.shape[4]
    lanes = 128
    chunks = width // parties // lanes
    vmem = pl.BlockSpec(memory_space=pltpu.VMEM)
    hbm = pl.BlockSpec(memory_space=pltpu.HBM)
    f32, bf16 = jnp.float32, jnp.bfloat16
    dma = pltpu.SemaphoreType.DMA
    return pl.pallas_call(
        functools.partial(hyena_kernel, parties),
        out_shape=pltpu.VMEM((tok_rows, width), bf16),
        in_specs=[hbm] * 10,
        out_specs=vmem,
        scratch_shapes=[
            *[pltpu.VMEM((tok_rows, width), bf16)] * 3,
            pltpu.VMEM(short_filter.shape, f32),
            pltpu.VMEM((1, width), f32),
            pltpu.VMEM(filter_spectrum.shape, f32),
            *[pltpu.VMEM((parties, 2 * tok_rows, 2 * tok_rows), bf16)] * 4,
            pltpu.VMEM((3, 16, width), bf16),
            pltpu.VMEM((4, width), bf16),
            pltpu.VMEM((2, width), bf16),
            pltpu.VMEM((4, width), bf16),
            pltpu.VMEM((2, width), bf16),
            *[pltpu.VMEM((parties, chunks, 2, lanes), f32)] * 2,
            *[pltpu.VMEM((2, parties, group_count // parties, tok_rows), bf16)] * 2,
            pltpu.VMEM((1, lanes), f32),
            pltpu.VMEM((parties, 1, lanes), f32),
            pltpu.VMEM((chunks, parties, tok_rows, lanes), f32),
            *[pltpu.VMEM((chunks, parties, tok_rows, lanes), bf16)] * 2,
            *[pltpu.VMEM((chunks, parties, 1, lanes), f32)] * 2,
            pltpu.VMEM((chunks, parties, tok_rows, lanes), f32),
            pltpu.VMEM((chunks, parties, 2, tok_rows, 2 * lanes), bf16),
            pltpu.VMEM((chunks, parties, 2, 2, tok_rows // 2, lanes), f32),
            pltpu.VMEM((chunks, parties, 2, tok_rows, lanes), f32),
            pltpu.VMEM((chunks, parties, tok_rows, lanes), f32),
            *[pltpu.VMEM((chunks, parties, tok_rows, lanes), bf16)] * 2,
            *[pltpu.VMEM((chunks, parties, 1, lanes), f32)] * 2,
            dma((9,)),
            dma((4,)),
            dma((2,)),
            dma((2,)),
            dma((parties,)),
            dma((parties,)),
            *[dma((chunks, parties))] * 4,
            *[dma((parties,))] * 6,
            *[dma((chunks, parties))] * 4,
        ],
        compiler_params=pltpu.CompilerParams(
            collective_id=0, has_side_effects=True, vmem_limit_bytes=56 * 1024 * 1024
        ),
    )(
        query_in,
        key_in,
        value_in,
        short_filter,
        skip_bias.reshape(1, width),
        filter_spectrum,
        *[jnp.asarray(table) for table in tables],
    )


def solution(mesh):
    parties = mesh.shape["ctx"]

    def per_device(*args):
        tok_rows, width = args[0].shape
        if width // parties % 128 == 0 and mesh.shape["grp"] == 2:
            return one_kernel(transform_tables(parties, tok_rows), *args)
        return on_device(*args)

    return jax.shard_map(
        per_device,
        mesh=mesh,
        in_specs=(
            P(("grp", "ctx"), "ch"),
            P(("grp", "ctx"), "ch"),
            P(("grp", "ctx"), "ch"),
            P(None, None, "ch"),
            P("ch"),
            P(None, "ctx", None, None, "ch"),
        ),
        out_specs=P(("grp", "ctx"), "ch"),
        check_vma=False,
    )
```

```python
import functools
import math

import jax
import jax.numpy as jnp
import ml_dtypes
import numpy as np
from jax import lax
from jax.experimental import pallas as pl
from jax.experimental.pallas import tpu as pltpu
from jax.sharding import PartitionSpec as P

HIGHEST = lax.Precision.HIGHEST
MESH = pl.DeviceIdType.MESH
POWER = 17
REACH = 2.0 ** (126 / POWER)


def passed_along(value, axis, steps):
    count = lax.axis_size(axis)
    leading, last = (max(0, -steps), min(count, count - steps))
    return lax.ppermute(value, axis, [(source, source + steps) for source in range(leading, last)])


def reversed_bits(number, digits):
    result = number * 0
    for bit_level in range(digits):
        result = result + (number >> bit_level & 1) * (1 << digits - 1 - bit_level)
    return result


def rotate(real_part, imag_part, cosine, sine):
    return (real_part * cosine - imag_part * sine, real_part * sine + imag_part * cosine)


def complex_product(pattern, table_real, table_imag, data_real, data_imag):
    out_real = jnp.einsum(pattern, table_real, data_real, precision=HIGHEST) - jnp.einsum(
        pattern, table_imag, data_imag, precision=HIGHEST
    )
    out_imag = jnp.einsum(pattern, table_real, data_imag, precision=HIGHEST) + jnp.einsum(
        pattern, table_imag, data_real, precision=HIGHEST
    )
    return (out_real, out_imag)


def angle_table(rows, cols, modulus):
    exponent = (
        jnp.arange(rows, dtype=jnp.int32)[:, None]
        * jnp.arange(cols, dtype=jnp.int32)[None, :]
        % modulus
    )
    angle = 2.0 * math.pi / modulus * exponent.astype(jnp.float32)
    return (jnp.cos(angle), jnp.sin(angle))


def whole_convolution(first_real, first_imag, filter_spectrum, parties, levels):
    tok_rows = first_real.shape[0]
    packed = jnp.stack((first_real, first_imag))
    spread = lax.all_to_all(packed, "ctx", split_axis=2, concat_axis=1, tiled=True)
    spectrum = lax.all_to_all(filter_spectrum, "ctx", split_axis=4, concat_axis=1, tiled=True)
    tail = spectrum.shape[2:]
    spectrum = spectrum.reshape(2, *[2] * levels, *tail)
    spectrum = spectrum.transpose(0, *range(levels, 0, -1), *range(levels + 1, levels + 4))
    spectrum = spectrum.reshape(2, parties, *tail)
    size_b = 2 * parties
    total = tok_rows * size_b
    spectrum = spectrum.reshape(2, size_b, tok_rows, spectrum.shape[4])
    columns = spread.shape[2]
    data = spread.reshape(2, size_b // 2, tok_rows, columns)
    outer_cos, outer_sin = angle_table(size_b, size_b // 2, size_b)
    twist_cos, twist_sin = angle_table(size_b, tok_rows, total)
    inner_cos, inner_sin = angle_table(tok_rows, tok_rows, tok_rows)
    section_real, section_imag = complex_product(
        "fn,nac->fac", outer_cos, -outer_sin, data[0], data[1]
    )
    section_real, section_imag = rotate(
        section_real, section_imag, twist_cos[..., None], -twist_sin[..., None]
    )
    freq_real, freq_imag = complex_product(
        "ak,fac->fkc", inner_cos, -inner_sin, section_real, section_imag
    )
    group_local = spectrum.shape[3]
    per_group = columns // group_local
    shaped_real = freq_real.reshape(size_b, tok_rows, group_local, per_group)
    shaped_imag = freq_imag.reshape(size_b, tok_rows, group_local, per_group)
    resp_real = spectrum[0][..., None]
    resp_imag = spectrum[1][..., None]
    prod_real = (shaped_real * resp_real - shaped_imag * resp_imag).reshape(
        size_b, tok_rows, columns
    )
    prod_imag = (shaped_real * resp_imag + shaped_imag * resp_real).reshape(
        size_b, tok_rows, columns
    )
    back_real, back_imag = complex_product(
        "ak,fkc->fac", inner_cos, inner_sin, prod_real, prod_imag
    )
    back_real, back_imag = rotate(back_real, back_imag, twist_cos[..., None], twist_sin[..., None])
    out_real, out_imag = complex_product(
        "nf,fac->nac", outer_cos.T, outer_sin.T, back_real, back_imag
    )
    norm_factor = 1.0 / total
    result = (
        jnp.stack(
            (
                out_real.reshape(size_b // 2 * tok_rows, columns),
                out_imag.reshape(size_b // 2 * tok_rows, columns),
            )
        )
        * norm_factor
    )
    returned = lax.all_to_all(result, "ctx", split_axis=1, concat_axis=2, tiled=True)
    return (returned[0], returned[1])


def on_device(query_in, key_in, value_in, short_filter, skip_bias, filter_spectrum):
    tok_rows, chan_width = query_in.shape
    parties = lax.axis_size("ctx")
    levels = parties.bit_length() - 1
    tap_count = short_filter.shape[1]
    group_count = filter_spectrum.shape[4]
    half_group = chan_width // (2 * group_count)
    packed_width = group_count * half_group
    stacked = jnp.stack((query_in, key_in, value_in))
    earlier = passed_along(stacked[:, tok_rows - (tap_count - 1) :, :], "ctx", 1)
    extended = jnp.concatenate((earlier, stacked), axis=1).astype(jnp.float32)
    filtered = short_filter[:, 0, None, :] * extended[:, tap_count - 1 :, :]
    for tap_lag in range(1, tap_count):
        start_row = tap_count - 1 - tap_lag
        filtered = (
            filtered
            + short_filter[:, tap_lag, None, :] * extended[:, start_row : start_row + tok_rows, :]
        )
    gated = filtered[1] * filtered[2]
    halves = gated.reshape(tok_rows, group_count, 2, half_group)
    first_real = halves[:, :, 0, :].reshape(tok_rows, packed_width)
    first_imag = halves[:, :, 1, :].reshape(tok_rows, packed_width)
    conv_real, conv_imag = whole_convolution(
        first_real, first_imag, filter_spectrum, parties, levels
    )
    conv = jnp.stack(
        (
            conv_real.reshape(tok_rows, group_count, half_group),
            conv_imag.reshape(tok_rows, group_count, half_group),
        ),
        axis=2,
    ).reshape(tok_rows, chan_width)
    return (filtered[0] * (conv + skip_bias[None, :] * gated)).astype(jnp.bfloat16)


def split_terms(value):
    high = value.astype(jnp.bfloat16)
    low = (value - high.astype(jnp.float32)).astype(jnp.bfloat16)
    return high, low


def scale_of(value):
    peak = jnp.max(jnp.abs(value), axis=0, keepdims=True)
    return jnp.maximum(peak * 1.0078125, 2.0**-100)


def encode(value, scale):
    ratio = value * (REACH / scale)
    square = ratio * ratio
    fourth = square * square
    eighth = fourth * fourth
    return (ratio * (eighth * eighth)).astype(jnp.bfloat16)


def decode(block, scale):
    code = block.astype(jnp.float32)
    root = jnp.exp(jnp.log(jnp.maximum(jnp.abs(code), 2.0**-126)) * (1.0 / POWER))
    root = root * (scale * (1.0 / REACH))
    return jnp.where(code < 0, -root, jnp.where(code > 0, root, jnp.zeros_like(root)))


def place_of(rho, parties):
    if rho % parties == 0:
        return 0, rho // parties
    return (rho, 0) if rho < parties else (2 * parties - rho, 1)


def transform_tables(parties, tok_rows):
    classes, half = 2 * parties, tok_rows // 2
    total = classes * tok_rows
    time = np.arange(tok_rows)
    table = np.zeros((parties, 2, 2, half, 2, tok_rows))
    for rho in range(classes):
        pair, side = place_of(rho, parties)
        angle = 2.0 * np.pi / total * ((classes * np.arange(half)[:, None] + rho) * time % total)
        cosine, sine = np.cos(angle), np.sin(angle)
        if pair == 0:
            table[pair, side, 0, :, side] = cosine
            table[pair, side, 1, :, side] = -sine
        else:
            sign = 1.0 - 2.0 * side
            table[pair, side, 0, :, 0] = cosine
            table[pair, side, 0, :, 1] = sign * sine
            table[pair, side, 1, :, 0] = -sine
            table[pair, side, 1, :, 1] = sign * cosine
    table[0, 0, 1, 0, 0] = 1.0 - 2.0 * (time % 2)
    forward = table.reshape(parties, 2 * tok_rows, 2 * tok_rows)

    def parts(matrix):
        high = matrix.astype(ml_dtypes.bfloat16)
        low = (matrix - high.astype(np.float64)).astype(ml_dtypes.bfloat16)
        return high, low

    return parts(forward) + parts(np.ascontiguousarray(forward.transpose(0, 2, 1)))


def weighted(terms):
    result = None
    for weight, value in terms:
        if abs(weight) < 1e-12:
            continue
        if abs(abs(weight) - 1.0) > 1e-12:
            term = value * abs(weight)
        else:
            term = value
        if result is None:
            result = term if weight > 0 else -term
        else:
            result = result + term if weight > 0 else result - term
    return result


def class_signals(blocks):
    parties = len(blocks)
    middle = parties // 2
    sums = [blocks[i] + blocks[i + middle] for i in range(middle)]
    gaps = [blocks[i] - blocks[i + middle] for i in range(middle)]
    signals = []
    for pair in range(parties):
        if pair == 0:
            even = weighted([(1.0, sums[i]) for i in range(0, middle, 2)])
            odd = weighted([(1.0, sums[i]) for i in range(1, middle, 2)])
            signals.append((even + odd, even - odd))
            continue
        used = blocks if pair % 2 else (sums if pair % 4 == 0 else gaps)
        angles = [math.pi * pair * i / parties for i in range(len(used))]
        real = weighted([(math.cos(a), v) for a, v in zip(angles, used)])
        imag = weighted([(-math.sin(a), v) for a, v in zip(angles, used)])
        signals.append((real, imag))
    return signals


def block_sums(signals):
    parties = len(signals)
    middle = parties // 2
    results = [None] * parties
    for i in range(middle):
        even = {0: [], 2: []}
        for pair in range(0, parties, 2):
            angle = math.pi * pair * i / parties
            real, imag = signals[pair]
            if pair == 0:
                even[0] += [(1.0, real), (1.0 - 2.0 * (i % 2), imag)]
            else:
                even[pair % 4] += [(math.cos(angle), real), (-math.sin(angle), imag)]
        same, flipped = weighted(even[0]), weighted(even[2])
        for place, base in ((i, same + flipped), (i + middle, same - flipped)):
            odd = []
            for pair in range(1, parties, 2):
                angle = math.pi * pair * place / parties
                real, imag = signals[pair]
                odd += [(math.cos(angle), real), (-math.sin(angle), imag)]
            results[place] = base + weighted(odd)
    return results


def hyena_kernel(
    parties,
    query_hbm,
    key_hbm,
    value_hbm,
    taps_hbm,
    skip_hbm,
    spec_hbm,
    fwd_high_hbm,
    fwd_low_hbm,
    bwd_high_hbm,
    bwd_low_hbm,
    out_ref,
    query_ref,
    key_ref,
    value_ref,
    taps_ref,
    skip_ref,
    spec_ref,
    fwd_high,
    fwd_low,
    bwd_high,
    bwd_low,
    edge,
    halo_out,
    halo_query_out,
    halo_in,
    halo_query_in,
    late_out,
    late_in,
    spec_out,
    spec_in,
    spec_scale_out,
    spec_scale_in,
    gated,
    data_out,
    data_in,
    data_scale_out,
    data_scale_in,
    data,
    classes,
    response,
    inverse,
    conv,
    conv_out,
    conv_in,
    conv_scale_out,
    conv_scale_in,
    input_sem,
    table_sem,
    halo_send,
    halo_recv,
    spec_send,
    spec_recv,
    data_send,
    data_recv,
    conv_send,
    conv_recv,
    late_send,
    late_recv,
    relay_send,
    relay_recv,
    spec_scale_send,
    spec_scale_recv,
    data_scale_send,
    data_scale_recv,
    conv_scale_send,
    conv_scale_recv,
):
    me = lax.axis_index("ctx")
    plane = lax.axis_index("grp")
    tok_rows, width = query_ref.shape
    owned = width // parties
    chunks, lanes = data_out.shape[0], gated.shape[3]
    group_count = spec_ref.shape[4]
    group_owned = group_count // parties
    group_chunk = group_owned // chunks
    half = tok_rows // 2
    rows = 2 * tok_rows

    barrier = pltpu.get_barrier_semaphore()

    @pl.loop(1, parties)
    def _(step):
        pl.semaphore_signal(
            barrier, inc=1, device_id={"ctx": lax.rem(me + step, parties)}, device_id_type=MESH
        )

    pl.semaphore_signal(barrier, inc=1, device_id={"grp": 1 - plane}, device_id_type=MESH)

    inputs = [
        pltpu.make_async_copy(source, target, input_sem.at[index])
        for index, (source, target) in enumerate(
            (
                (query_hbm.at[tok_rows - 16 :, :], edge.at[0]),
                (key_hbm.at[tok_rows - 16 :, :], edge.at[1]),
                (value_hbm.at[tok_rows - 16 :, :], edge.at[2]),
                (spec_hbm, spec_ref),
                (key_hbm, key_ref),
                (value_hbm, value_ref),
                (taps_hbm, taps_ref),
                (query_hbm, query_ref),
                (skip_hbm, skip_ref),
            )
        )
    ]
    for copy in inputs:
        copy.start()

    for copy in inputs[:3]:
        copy.wait()
    last = edge[...].astype(jnp.float32)[:, 14:16, :]
    halo_out[...] = last[1:].reshape(4, width).astype(jnp.bfloat16)
    halo_query_out[...] = last[0].astype(jnp.bfloat16)
    def halo_copy(source, target, index):
        return pltpu.make_async_remote_copy(
            source,
            target,
            halo_send.at[index],
            halo_recv.at[index],
            device_id={"ctx": lax.rem(me + 1, parties)},
            device_id_type=MESH,
        )

    halo = halo_copy(halo_out, halo_in, 0)
    halo_query = halo_copy(halo_query_out, halo_query_in, 1)

    def spec_copy(target, slot):
        return pltpu.make_async_remote_copy(
            spec_out.at[plane, target],
            spec_in.at[plane, slot],
            spec_send.at[target],
            spec_recv.at[slot],
            device_id={"ctx": target},
            device_id_type=MESH,
        )

    def relay_copy(part, source):
        return pltpu.make_async_remote_copy(
            spec_in.at[part, source],
            spec_in.at[part, source],
            relay_send.at[source],
            relay_recv.at[source],
            device_id={"grp": 1 - plane},
            device_id_type=MESH,
        )

    def spec_scale_copy(target, slot):
        return pltpu.make_async_remote_copy(
            spec_scale_out,
            spec_scale_in.at[slot],
            spec_scale_send.at[target],
            spec_scale_recv.at[slot],
            device_id={"ctx": target},
            device_id_type=MESH,
        )

    def data_scale_copy(chunk, target, slot):
        return pltpu.make_async_remote_copy(
            data_scale_out.at[chunk, target],
            data_scale_in.at[chunk, slot],
            data_scale_send.at[chunk, target],
            data_scale_recv.at[chunk, slot],
            device_id={"ctx": target},
            device_id_type=MESH,
        )

    def conv_scale_copy(chunk, target, slot):
        return pltpu.make_async_remote_copy(
            conv_scale_out.at[chunk, target],
            conv_scale_in.at[chunk, slot],
            conv_scale_send.at[chunk, target],
            conv_scale_recv.at[chunk, slot],
            device_id={"ctx": target},
            device_id_type=MESH,
        )

    def data_copy(chunk, target, slot):
        return pltpu.make_async_remote_copy(
            data_out.at[chunk, target],
            data_in.at[chunk, slot],
            data_send.at[chunk, target],
            data_recv.at[chunk, slot],
            device_id={"ctx": target},
            device_id_type=MESH,
        )

    def conv_copy(chunk, target, slot):
        return pltpu.make_async_remote_copy(
            conv_out.at[chunk, target],
            conv_in.at[chunk, slot],
            conv_send.at[chunk, target],
            conv_recv.at[chunk, slot],
            device_id={"ctx": target},
            device_id_type=MESH,
        )

    token = lax.broadcasted_iota(jnp.int32, (tok_rows, lanes), 0)

    def columns_of(target, chunk):
        return pl.ds(pl.multiple_of(target * owned + chunk * lanes, lanes), lanes)

    def rotated(step):
        return lax.rem(me + step + 1, parties)

    def late_copy(target, slot):
        return pltpu.make_async_remote_copy(
            late_out.at[target],
            late_in.at[slot],
            late_send.at[target],
            late_recv.at[slot],
            device_id={"ctx": target},
            device_id_type=MESH,
        )

    def filtered(ref, index, columns, shifted, twice, current):
        taps = taps_ref[index, :, columns]
        return taps[0:1, :] * current + taps[1:2, :] * shifted + taps[2:3, :] * twice

    def inside(ref, index, columns):
        current = ref[:, columns].astype(jnp.float32)
        return filtered(
            ref, index, columns, pltpu.roll(current, 1, 0), pltpu.roll(current, 2, 0), current
        )

    def leading(ref, index, columns, before):
        current = ref[0:16, columns].astype(jnp.float32)[0:2]
        before = before[:, columns].astype(jnp.float32)[2 * index - 2 : 2 * index]
        shifted = jnp.concatenate((before[1:2], current[0:1]), axis=0)
        return filtered(ref, index, columns, shifted, before, current)

    def gate(chunk, target):
        columns = columns_of(target, chunk)
        product = inside(key_ref, 1, columns) * inside(value_ref, 2, columns)
        product = jnp.where(token < 2, jnp.zeros_like(product), product)
        gated[chunk, target] = product
        return product

    for copy in inputs[4:7]:
        copy.wait()

    for chunk in range(chunks):

        @pl.loop(0, parties - 1)
        def _(step, chunk=chunk):
            target = rotated(step)
            product = gate(chunk, target)
            scale = scale_of(product)
            data_scale_out[chunk, target] = scale
            data_out[chunk, target] = encode(product, scale)

        data[chunk, me] = gate(chunk, me)

    inputs[3].wait()
    packed = jnp.concatenate(
        [spec_ref[part, 0, parity, :half, :] for part in range(2) for parity in range(2)], axis=0
    )
    row_index = lax.broadcasted_iota(jnp.int32, packed.shape, 0)
    highest = spec_ref[0, 0, 0, half : half + 1, :]
    packed = jnp.where((row_index == tok_rows) & (me == 0), highest, packed)
    spec_scale = jnp.max(scale_of(packed), axis=1, keepdims=True)
    spec_scale_out[...] = jnp.broadcast_to(spec_scale, (1, lanes))
    codes = packed.T
    codes = encode(codes, spec_scale)
    for part in range(2):
        columns = codes[:, part * tok_rows : (part + 1) * tok_rows]
        spec_out[part] = columns.reshape(spec_out.shape[1:])
        spec_in[part, me] = spec_out[part, me]
    spec_scale_in[me] = spec_scale_out[...]

    pl.semaphore_wait(barrier, parties)


    @pl.when(me < parties - 1)
    def _():
        halo.start()
        halo_query.start()

    @pl.loop(0, parties - 1)
    def _(step):
        target = rotated(step)
        spec_copy(target, me).start()
        spec_scale_copy(target, me).start()

    @pl.loop(0, parties - 1)
    def _(step):
        target = rotated(step)
        data_copy(0, target, me).start()
        data_scale_copy(0, target, me).start()

    tables = [
        pltpu.make_async_copy(source, target, table_sem.at[index])
        for index, (source, target) in enumerate(
            (
                (fwd_high_hbm, fwd_high),
                (fwd_low_hbm, fwd_low),
                (bwd_high_hbm, bwd_high),
                (bwd_low_hbm, bwd_low),
            )
        )
    ]
    for table in tables:
        table.start()


    @pl.when(me > 0)
    def _():
        halo.wait_recv()

    @pl.when(me == 0)
    def _():
        halo_in[...] = jnp.zeros_like(halo_in)
        halo_query_in[...] = jnp.zeros_like(halo_query_in)

    def late(chunk, target):
        columns = columns_of(target, chunk)
        rows = leading(key_ref, 1, columns, halo_in) * leading(value_ref, 2, columns, halo_in)
        gated[chunk, target, 0:2, :] = rows
        return rows

    for chunk in range(chunks):
        data[chunk, me, 0:2, :] = late(chunk, me)

    @pl.loop(0, parties - 1)
    def _(step):
        target = rotated(step)
        for chunk in range(chunks):
            late_out[target, chunk] = late(chunk, target)
        late_copy(target, me).start()

    @pl.when(lax.axis_index("ch") != 1)
    def _():
        for chunk in range(1, chunks):

            @pl.loop(0, parties - 1)
            def _(step, chunk=chunk):
                target = rotated(step)
                data_copy(chunk, target, me).start()
                data_scale_copy(chunk, target, me).start()

    lane_group = lax.broadcasted_iota(jnp.int32, (3 * group_chunk, lanes), 1) // (
        lanes // group_chunk
    )
    slot_group = lax.broadcasted_iota(jnp.int32, (3 * group_chunk, lanes), 0) % group_chunk
    spread = (lane_group == slot_group).astype(jnp.float32).astype(jnp.bfloat16)

    @pl.loop(1, parties)
    def _(step):
        source = lax.rem(me + parties - step, parties)
        spec_copy(me, source).wait_recv()
        relay_copy(plane, source).start()
        spec_scale_copy(me, source).wait_recv()

    @pl.loop(1, parties)
    def _(step):
        relay_copy(1 - plane, lax.rem(me + parties - step, parties)).wait_recv()

    levels = parties.bit_length() - 1
    row = lax.broadcasted_iota(jnp.int32, (rows, lanes), 0)
    for party in range(parties):
        codes = jnp.concatenate((spec_in[0, party], spec_in[1, party]), axis=1)
        decoded = decode(codes, spec_scale_in[party, :, :1])
        for chunk in range(chunks):
            exact = decoded[chunk * group_chunk : (chunk + 1) * group_chunk]
            high = exact.astype(jnp.bfloat16).astype(jnp.float32)
            middle = (exact - high).astype(jnp.bfloat16).astype(jnp.float32)
            low = exact - high - middle
            terms = jnp.concatenate((high, middle, low), axis=0).astype(jnp.bfloat16)
            wide = lax.dot_general(
                terms, spread, (((0,), (0,)), ((), ())), preferred_element_type=jnp.float32
            )
            if party == 0:
                ends = lax.rem(row, tok_rows) == 0
                wide = wide * jnp.where(ends, 0.5 / (parties * tok_rows), 1.0 / (parties * tok_rows))
            else:
                wide = wide * (1.0 / (parties * tok_rows))
            for parity in range(2):
                pair, side = place_of(2 * reversed_bits(party, levels) + parity, parties)
                for part in range(2):
                    start = part * tok_rows + parity * half
                    response[chunk, pair, side, part] = wide[start : start + half]

    for table in tables:
        table.wait()

    first = lax.broadcasted_iota(jnp.int32, (half, lanes), 0) == 0
    slab = 16

    for chunk in range(chunks):

        @pl.loop(1, parties)
        def _(step, chunk=chunk):
            source = lax.rem(me + parties - step, parties)
            data_scale_copy(chunk, me, source).wait_recv()
            data_copy(chunk, me, source).wait_recv()
            data[chunk, source] = decode(data_in[chunk, source], data_scale_in[chunk, source])
            if chunk == 0:
                late_copy(me, source).wait_recv()
            data[chunk, source, 0:2, :] = late_in[source, chunk]

        if chunk + 1 < chunks:

            @pl.when(lax.axis_index("ch") == 1)
            def _(chunk=chunk):

                @pl.loop(0, parties - 1)
                def _(step, chunk=chunk):
                    target = rotated(step)
                    data_copy(chunk + 1, target, me).start()
                    data_scale_copy(chunk + 1, target, me).start()

        @pl.loop(0, tok_rows // slab)
        def _(step, chunk=chunk):
            here = pl.ds(pl.multiple_of(step * slab, slab), slab)
            blocks = [data[chunk, party, here, :] for party in range(parties)]
            for pair, signals in enumerate(class_signals(blocks)):
                for side, signal in enumerate(signals):
                    classes[chunk, pair, side, here, :] = jnp.concatenate(
                        split_terms(signal), axis=1
                    )

        @pl.loop(0, parties, unroll=8)
        def _(pair, chunk=chunk):
            signal = classes[chunk, pair].reshape(rows, 2 * lanes)
            both = jnp.concatenate((fwd_high[pair], fwd_low[pair]), axis=0)
            every = jnp.dot(both, signal, preferred_element_type=jnp.float32)
            wide, rest = every[:rows], every[rows:, :lanes]
            spectrum = wide[:, :lanes] + wide[:, lanes:] + rest
            products = []
            for side in range(2):
                data_re = spectrum[side * tok_rows : side * tok_rows + half]
                data_im = spectrum[side * tok_rows + half : (side + 1) * tok_rows]
                resp_re, resp_im = response[chunk, pair, side, 0], response[chunk, pair, side, 1]
                both_re, both_im = data_re * resp_re, data_im * resp_im
                cross = data_re * resp_im + data_im * resp_re
                if side == 0:
                    alone = first & (pair == 0)
                    products.append(both_re - jnp.where(alone, jnp.zeros_like(both_im), both_im))
                    products.append(jnp.where(alone, both_im, cross))
                else:
                    products += [both_re - both_im, cross]
            product = jnp.concatenate(split_terms(jnp.concatenate(products, axis=0)), axis=1)
            both = jnp.concatenate((bwd_high[pair], bwd_low[pair]), axis=0)
            every = jnp.dot(both, product, preferred_element_type=jnp.float32)
            wide, rest = every[:rows], every[rows:, :lanes]
            result = wide[:, :lanes] + wide[:, lanes:] + rest
            inverse[chunk, pair] = result.reshape(2, tok_rows, lanes)

        @pl.loop(0, tok_rows // slab)
        def _(step, chunk=chunk):
            here = pl.ds(pl.multiple_of(step * slab, slab), slab)
            signals = [
                (inverse[chunk, pair, 0, here, :], inverse[chunk, pair, 1, here, :])
                for pair in range(parties)
            ]
            for party, result in enumerate(block_sums(signals)):
                conv[chunk, party, here, :] = result

        @pl.loop(0, parties - 1)
        def _(step, chunk=chunk):
            target = rotated(step)
            result = conv[chunk, target]
            scale = scale_of(result)
            conv_scale_out[chunk, target] = scale
            conv_out[chunk, target] = encode(result, scale)
            conv_copy(chunk, target, me).start()
            conv_scale_copy(chunk, target, me).start()

    @pl.when(me > 0)
    def _():
        halo_query.wait_recv()

    for copy in inputs[7:]:
        copy.wait()

    def short(ref, index, columns):
        current = ref[:, columns].astype(jnp.float32)
        before = halo_query_in[:, columns].astype(jnp.float32)
        shifted = jnp.where(token == 0, before[1:2, :], pltpu.roll(current, 1, 0))
        twice = jnp.where(token == 0, before[0:1, :], pltpu.roll(current, 2, 0))
        twice = jnp.where(token == 1, before[1:2, :], twice)
        taps = taps_ref[index, :, columns]
        return taps[0:1, :] * current + taps[1:2, :] * shifted + taps[2:3, :] * twice

    def finish(chunk, source, conv):
        columns = columns_of(source, chunk)
        mixed = conv + skip_ref[:, columns] * gated[chunk, source]
        out_ref[:, columns] = (short(query_ref, 0, columns) * mixed).astype(jnp.bfloat16)

    for chunk in range(chunks):
        finish(chunk, me, conv[chunk, me])

        @pl.loop(1, parties)
        def _(step, chunk=chunk):
            source = lax.rem(me + parties - step, parties)
            conv_scale_copy(chunk, me, source).wait_recv()
            conv_copy(chunk, me, source).wait_recv()
            finish(chunk, source, decode(conv_in[chunk, source], conv_scale_in[chunk, source]))

    @pl.when(me < parties - 1)
    def _():
        halo.wait_send()
        halo_query.wait_send()

    @pl.loop(1, parties)
    def _(step):
        target = lax.rem(me + step, parties)
        late_copy(target, me).wait_send()
        spec_copy(target, me).wait_send()
        relay_copy(plane, target).wait_send()
        spec_scale_copy(target, me).wait_send()
        for chunk in range(chunks):
            data_copy(chunk, target, me).wait_send()
            data_scale_copy(chunk, target, me).wait_send()
            conv_copy(chunk, target, me).wait_send()
            conv_scale_copy(chunk, target, me).wait_send()


def one_kernel(tables, query_in, key_in, value_in, short_filter, skip_bias, filter_spectrum):
    tok_rows, width = query_in.shape
    parties = lax.axis_size("ctx")
    group_count = filter_spectrum.shape[4]
    lanes = 128
    chunks = width // parties // lanes
    vmem = pl.BlockSpec(memory_space=pltpu.VMEM)
    hbm = pl.BlockSpec(memory_space=pltpu.HBM)
    f32, bf16 = jnp.float32, jnp.bfloat16
    dma = pltpu.SemaphoreType.DMA
    return pl.pallas_call(
        functools.partial(hyena_kernel, parties),
        out_shape=pltpu.VMEM((tok_rows, width), bf16),
        in_specs=[hbm] * 10,
        out_specs=vmem,
        scratch_shapes=[
            *[pltpu.VMEM((tok_rows, width), bf16)] * 3,
            pltpu.VMEM(short_filter.shape, f32),
            pltpu.VMEM((1, width), f32),
            pltpu.VMEM(filter_spectrum.shape, f32),
            *[pltpu.VMEM((parties, 2 * tok_rows, 2 * tok_rows), bf16)] * 4,
            pltpu.VMEM((3, 16, width), bf16),
            pltpu.VMEM((4, width), bf16),
            pltpu.VMEM((2, width), bf16),
            pltpu.VMEM((4, width), bf16),
            pltpu.VMEM((2, width), bf16),
            *[pltpu.VMEM((parties, chunks, 2, lanes), f32)] * 2,
            *[pltpu.VMEM((2, parties, group_count // parties, tok_rows), bf16)] * 2,
            pltpu.VMEM((1, lanes), f32),
            pltpu.VMEM((parties, 1, lanes), f32),
            pltpu.VMEM((chunks, parties, tok_rows, lanes), f32),
            *[pltpu.VMEM((chunks, parties, tok_rows, lanes), bf16)] * 2,
            *[pltpu.VMEM((chunks, parties, 1, lanes), f32)] * 2,
            pltpu.VMEM((chunks, parties, tok_rows, lanes), f32),
            pltpu.VMEM((chunks, parties, 2, tok_rows, 2 * lanes), bf16),
            pltpu.VMEM((chunks, parties, 2, 2, tok_rows // 2, lanes), f32),
            pltpu.VMEM((chunks, parties, 2, tok_rows, lanes), f32),
            pltpu.VMEM((chunks, parties, tok_rows, lanes), f32),
            *[pltpu.VMEM((chunks, parties, tok_rows, lanes), bf16)] * 2,
            *[pltpu.VMEM((chunks, parties, 1, lanes), f32)] * 2,
            dma((9,)),
            dma((4,)),
            dma((2,)),
            dma((2,)),
            dma((parties,)),
            dma((parties,)),
            *[dma((chunks, parties))] * 4,
            *[dma((parties,))] * 6,
            *[dma((chunks, parties))] * 4,
        ],
        compiler_params=pltpu.CompilerParams(
            collective_id=0, has_side_effects=True, vmem_limit_bytes=56 * 1024 * 1024
        ),
    )(
        query_in,
        key_in,
        value_in,
        short_filter,
        skip_bias.reshape(1, width),
        filter_spectrum,
        *[jnp.asarray(table) for table in tables],
    )


def solution(mesh):
    parties = mesh.shape["ctx"]

    def per_device(*args):
        tok_rows, width = args[0].shape
        if width // parties % 128 == 0 and mesh.shape["grp"] == 2:
            return one_kernel(transform_tables(parties, tok_rows), *args)
        return on_device(*args)

    return jax.shard_map(
        per_device,
        mesh=mesh,
        in_specs=(
            P(("grp", "ctx"), "ch"),
            P(("grp", "ctx"), "ch"),
            P(("grp", "ctx"), "ch"),
            P(None, None, "ch"),
            P("ch"),
            P(None, "ctx", None, None, "ch"),
        ),
        out_specs=P(("grp", "ctx"), "ch"),
        check_vma=False,
    )
```

```python
import functools
import math

import jax
import jax.numpy as jnp
import ml_dtypes
import numpy as np
from jax import lax
from jax.experimental import pallas as pl
from jax.experimental.pallas import tpu as pltpu
from jax.sharding import PartitionSpec as P

HIGHEST = lax.Precision.HIGHEST
MESH = pl.DeviceIdType.MESH
POWER = 17
REACH = 2.0 ** (126 / POWER)


def passed_along(value, axis, steps):
    count = lax.axis_size(axis)
    leading, last = (max(0, -steps), min(count, count - steps))
    return lax.ppermute(value, axis, [(source, source + steps) for source in range(leading, last)])


def reversed_bits(number, digits):
    result = number * 0
    for bit_level in range(digits):
        result = result + (number >> bit_level & 1) * (1 << digits - 1 - bit_level)
    return result


def rotate(real_part, imag_part, cosine, sine):
    return (real_part * cosine - imag_part * sine, real_part * sine + imag_part * cosine)


def complex_product(pattern, table_real, table_imag, data_real, data_imag):
    out_real = jnp.einsum(pattern, table_real, data_real, precision=HIGHEST) - jnp.einsum(
        pattern, table_imag, data_imag, precision=HIGHEST
    )
    out_imag = jnp.einsum(pattern, table_real, data_imag, precision=HIGHEST) + jnp.einsum(
        pattern, table_imag, data_real, precision=HIGHEST
    )
    return (out_real, out_imag)


def angle_table(rows, cols, modulus):
    exponent = (
        jnp.arange(rows, dtype=jnp.int32)[:, None]
        * jnp.arange(cols, dtype=jnp.int32)[None, :]
        % modulus
    )
    angle = 2.0 * math.pi / modulus * exponent.astype(jnp.float32)
    return (jnp.cos(angle), jnp.sin(angle))


def whole_convolution(first_real, first_imag, filter_spectrum, parties, levels):
    tok_rows = first_real.shape[0]
    packed = jnp.stack((first_real, first_imag))
    spread = lax.all_to_all(packed, "ctx", split_axis=2, concat_axis=1, tiled=True)
    spectrum = lax.all_to_all(filter_spectrum, "ctx", split_axis=4, concat_axis=1, tiled=True)
    tail = spectrum.shape[2:]
    spectrum = spectrum.reshape(2, *[2] * levels, *tail)
    spectrum = spectrum.transpose(0, *range(levels, 0, -1), *range(levels + 1, levels + 4))
    spectrum = spectrum.reshape(2, parties, *tail)
    size_b = 2 * parties
    total = tok_rows * size_b
    spectrum = spectrum.reshape(2, size_b, tok_rows, spectrum.shape[4])
    columns = spread.shape[2]
    data = spread.reshape(2, size_b // 2, tok_rows, columns)
    outer_cos, outer_sin = angle_table(size_b, size_b // 2, size_b)
    twist_cos, twist_sin = angle_table(size_b, tok_rows, total)
    inner_cos, inner_sin = angle_table(tok_rows, tok_rows, tok_rows)
    section_real, section_imag = complex_product(
        "fn,nac->fac", outer_cos, -outer_sin, data[0], data[1]
    )
    section_real, section_imag = rotate(
        section_real, section_imag, twist_cos[..., None], -twist_sin[..., None]
    )
    freq_real, freq_imag = complex_product(
        "ak,fac->fkc", inner_cos, -inner_sin, section_real, section_imag
    )
    group_local = spectrum.shape[3]
    per_group = columns // group_local
    shaped_real = freq_real.reshape(size_b, tok_rows, group_local, per_group)
    shaped_imag = freq_imag.reshape(size_b, tok_rows, group_local, per_group)
    resp_real = spectrum[0][..., None]
    resp_imag = spectrum[1][..., None]
    prod_real = (shaped_real * resp_real - shaped_imag * resp_imag).reshape(
        size_b, tok_rows, columns
    )
    prod_imag = (shaped_real * resp_imag + shaped_imag * resp_real).reshape(
        size_b, tok_rows, columns
    )
    back_real, back_imag = complex_product(
        "ak,fkc->fac", inner_cos, inner_sin, prod_real, prod_imag
    )
    back_real, back_imag = rotate(back_real, back_imag, twist_cos[..., None], twist_sin[..., None])
    out_real, out_imag = complex_product(
        "nf,fac->nac", outer_cos.T, outer_sin.T, back_real, back_imag
    )
    norm_factor = 1.0 / total
    result = (
        jnp.stack(
            (
                out_real.reshape(size_b // 2 * tok_rows, columns),
                out_imag.reshape(size_b // 2 * tok_rows, columns),
            )
        )
        * norm_factor
    )
    returned = lax.all_to_all(result, "ctx", split_axis=1, concat_axis=2, tiled=True)
    return (returned[0], returned[1])


def on_device(query_in, key_in, value_in, short_filter, skip_bias, filter_spectrum):
    tok_rows, chan_width = query_in.shape
    parties = lax.axis_size("ctx")
    levels = parties.bit_length() - 1
    tap_count = short_filter.shape[1]
    group_count = filter_spectrum.shape[4]
    half_group = chan_width // (2 * group_count)
    packed_width = group_count * half_group
    stacked = jnp.stack((query_in, key_in, value_in))
    earlier = passed_along(stacked[:, tok_rows - (tap_count - 1) :, :], "ctx", 1)
    extended = jnp.concatenate((earlier, stacked), axis=1).astype(jnp.float32)
    filtered = short_filter[:, 0, None, :] * extended[:, tap_count - 1 :, :]
    for tap_lag in range(1, tap_count):
        start_row = tap_count - 1 - tap_lag
        filtered = (
            filtered
            + short_filter[:, tap_lag, None, :] * extended[:, start_row : start_row + tok_rows, :]
        )
    gated = filtered[1] * filtered[2]
    halves = gated.reshape(tok_rows, group_count, 2, half_group)
    first_real = halves[:, :, 0, :].reshape(tok_rows, packed_width)
    first_imag = halves[:, :, 1, :].reshape(tok_rows, packed_width)
    conv_real, conv_imag = whole_convolution(
        first_real, first_imag, filter_spectrum, parties, levels
    )
    conv = jnp.stack(
        (
            conv_real.reshape(tok_rows, group_count, half_group),
            conv_imag.reshape(tok_rows, group_count, half_group),
        ),
        axis=2,
    ).reshape(tok_rows, chan_width)
    return (filtered[0] * (conv + skip_bias[None, :] * gated)).astype(jnp.bfloat16)


def split_terms(value):
    high = value.astype(jnp.bfloat16)
    low = (value - high.astype(jnp.float32)).astype(jnp.bfloat16)
    return high, low


def scale_of(value):
    peak = jnp.max(jnp.abs(value), axis=0, keepdims=True)
    return jnp.maximum(peak * 1.0078125, 2.0**-100)


def encode(value, scale):
    ratio = value * (REACH / scale)
    square = ratio * ratio
    fourth = square * square
    eighth = fourth * fourth
    return (ratio * (eighth * eighth)).astype(jnp.bfloat16)


def decode(block, scale):
    code = block.astype(jnp.float32)
    root = jnp.exp(jnp.log(jnp.maximum(jnp.abs(code), 2.0**-126)) * (1.0 / POWER))
    root = root * (scale * (1.0 / REACH))
    return jnp.where(code < 0, -root, jnp.where(code > 0, root, jnp.zeros_like(root)))


def place_of(rho, parties):
    if rho % parties == 0:
        return 0, rho // parties
    return (rho, 0) if rho < parties else (2 * parties - rho, 1)


def transform_tables(parties, tok_rows):
    classes, half = 2 * parties, tok_rows // 2
    total = classes * tok_rows
    time = np.arange(tok_rows)
    table = np.zeros((parties, 2, 2, half, 2, tok_rows))
    for rho in range(classes):
        pair, side = place_of(rho, parties)
        angle = 2.0 * np.pi / total * ((classes * np.arange(half)[:, None] + rho) * time % total)
        cosine, sine = np.cos(angle), np.sin(angle)
        if pair == 0:
            table[pair, side, 0, :, side] = cosine
            table[pair, side, 1, :, side] = -sine
        else:
            sign = 1.0 - 2.0 * side
            table[pair, side, 0, :, 0] = cosine
            table[pair, side, 0, :, 1] = sign * sine
            table[pair, side, 1, :, 0] = -sine
            table[pair, side, 1, :, 1] = sign * cosine
    table[0, 0, 1, 0, 0] = 1.0 - 2.0 * (time % 2)
    forward = table.reshape(parties, 2 * tok_rows, 2 * tok_rows)

    def parts(matrix):
        high = matrix.astype(ml_dtypes.bfloat16)
        low = (matrix - high.astype(np.float64)).astype(ml_dtypes.bfloat16)
        return high, low

    return parts(forward) + parts(np.ascontiguousarray(forward.transpose(0, 2, 1)))


def weighted(terms):
    result = None
    for weight, value in terms:
        if abs(weight) < 1e-12:
            continue
        if abs(abs(weight) - 1.0) > 1e-12:
            term = value * abs(weight)
        else:
            term = value
        if result is None:
            result = term if weight > 0 else -term
        else:
            result = result + term if weight > 0 else result - term
    return result


def class_signals(blocks):
    parties = len(blocks)
    middle = parties // 2
    sums = [blocks[i] + blocks[i + middle] for i in range(middle)]
    gaps = [blocks[i] - blocks[i + middle] for i in range(middle)]
    signals = []
    for pair in range(parties):
        if pair == 0:
            even = weighted([(1.0, sums[i]) for i in range(0, middle, 2)])
            odd = weighted([(1.0, sums[i]) for i in range(1, middle, 2)])
            signals.append((even + odd, even - odd))
            continue
        used = blocks if pair % 2 else (sums if pair % 4 == 0 else gaps)
        angles = [math.pi * pair * i / parties for i in range(len(used))]
        real = weighted([(math.cos(a), v) for a, v in zip(angles, used)])
        imag = weighted([(-math.sin(a), v) for a, v in zip(angles, used)])
        signals.append((real, imag))
    return signals


def block_sums(signals):
    parties = len(signals)
    middle = parties // 2
    results = [None] * parties
    for i in range(middle):
        even = {0: [], 2: []}
        for pair in range(0, parties, 2):
            angle = math.pi * pair * i / parties
            real, imag = signals[pair]
            if pair == 0:
                even[0] += [(1.0, real), (1.0 - 2.0 * (i % 2), imag)]
            else:
                even[pair % 4] += [(math.cos(angle), real), (-math.sin(angle), imag)]
        same, flipped = weighted(even[0]), weighted(even[2])
        for place, base in ((i, same + flipped), (i + middle, same - flipped)):
            odd = []
            for pair in range(1, parties, 2):
                angle = math.pi * pair * place / parties
                real, imag = signals[pair]
                odd += [(math.cos(angle), real), (-math.sin(angle), imag)]
            results[place] = base + weighted(odd)
    return results


def hyena_kernel(
    parties,
    query_hbm,
    key_hbm,
    value_hbm,
    taps_hbm,
    skip_hbm,
    spec_hbm,
    fwd_high_hbm,
    fwd_low_hbm,
    bwd_high_hbm,
    bwd_low_hbm,
    out_ref,
    query_ref,
    key_ref,
    value_ref,
    taps_ref,
    skip_ref,
    spec_ref,
    fwd_high,
    fwd_low,
    bwd_high,
    bwd_low,
    edge,
    halo_out,
    halo_query_out,
    halo_in,
    halo_query_in,
    late_out,
    late_in,
    spec_out,
    spec_in,
    scale_out,
    scale_in,
    gated,
    data_out,
    data_in,
    data,
    classes,
    response,
    inverse,
    conv,
    conv_out,
    conv_in,
    conv_scale_out,
    conv_scale_in,
    input_sem,
    table_sem,
    halo_send,
    halo_recv,
    spec_send,
    spec_recv,
    data_send,
    data_recv,
    conv_send,
    conv_recv,
    late_send,
    late_recv,
    relay_send,
    relay_recv,
    scale_send,
    scale_recv,
    conv_scale_send,
    conv_scale_recv,
):
    me = lax.axis_index("ctx")
    plane = lax.axis_index("grp")
    tok_rows, width = query_ref.shape
    owned = width // parties
    chunks, lanes = data_out.shape[0], gated.shape[3]
    group_count = spec_ref.shape[4]
    group_owned = group_count // parties
    group_chunk = group_owned // chunks
    half = tok_rows // 2
    rows = 2 * tok_rows

    barrier = pltpu.get_barrier_semaphore()

    @pl.loop(1, parties)
    def _(step):
        pl.semaphore_signal(
            barrier, inc=1, device_id={"ctx": lax.rem(me + step, parties)}, device_id_type=MESH
        )

    pl.semaphore_signal(barrier, inc=1, device_id={"grp": 1 - plane}, device_id_type=MESH)

    inputs = [
        pltpu.make_async_copy(source, target, input_sem.at[index])
        for index, (source, target) in enumerate(
            (
                (query_hbm.at[tok_rows - 16 :, :], edge.at[0]),
                (key_hbm.at[tok_rows - 16 :, :], edge.at[1]),
                (value_hbm.at[tok_rows - 16 :, :], edge.at[2]),
                (spec_hbm, spec_ref),
                (key_hbm, key_ref),
                (value_hbm, value_ref),
                (taps_hbm, taps_ref),
                (query_hbm, query_ref),
                (skip_hbm, skip_ref),
            )
        )
    ]
    for copy in inputs:
        copy.start()

    for copy in inputs[:3]:
        copy.wait()
    last = edge[...].astype(jnp.float32)[:, 14:16, :]
    halo_out[...] = last[1:].reshape(4, width).astype(jnp.bfloat16)
    halo_query_out[...] = last[0].astype(jnp.bfloat16)
    def halo_copy(source, target, index):
        return pltpu.make_async_remote_copy(
            source,
            target,
            halo_send.at[index],
            halo_recv.at[index],
            device_id={"ctx": lax.rem(me + 1, parties)},
            device_id_type=MESH,
        )

    halo = halo_copy(halo_out, halo_in, 0)
    halo_query = halo_copy(halo_query_out, halo_query_in, 1)

    def spec_copy(target, slot):
        return pltpu.make_async_remote_copy(
            spec_out.at[plane, target],
            spec_in.at[plane, slot],
            spec_send.at[target],
            spec_recv.at[slot],
            device_id={"ctx": target},
            device_id_type=MESH,
        )

    def relay_copy(part, source):
        return pltpu.make_async_remote_copy(
            spec_in.at[part, source],
            spec_in.at[part, source],
            relay_send.at[source],
            relay_recv.at[source],
            device_id={"grp": 1 - plane},
            device_id_type=MESH,
        )

    def scale_copy(target, slot):
        return pltpu.make_async_remote_copy(
            scale_out.at[target],
            scale_in.at[slot],
            scale_send.at[target],
            scale_recv.at[slot],
            device_id={"ctx": target},
            device_id_type=MESH,
        )

    def conv_scale_copy(chunk, target, slot):
        return pltpu.make_async_remote_copy(
            conv_scale_out.at[chunk, target],
            conv_scale_in.at[chunk, slot],
            conv_scale_send.at[chunk, target],
            conv_scale_recv.at[chunk, slot],
            device_id={"ctx": target},
            device_id_type=MESH,
        )

    def data_copy(chunk, target, slot):
        return pltpu.make_async_remote_copy(
            data_out.at[chunk, target],
            data_in.at[chunk, slot],
            data_send.at[chunk, target],
            data_recv.at[chunk, slot],
            device_id={"ctx": target},
            device_id_type=MESH,
        )

    def conv_copy(chunk, target, slot):
        return pltpu.make_async_remote_copy(
            conv_out.at[chunk, target],
            conv_in.at[chunk, slot],
            conv_send.at[chunk, target],
            conv_recv.at[chunk, slot],
            device_id={"ctx": target},
            device_id_type=MESH,
        )

    token = lax.broadcasted_iota(jnp.int32, (tok_rows, lanes), 0)

    def columns_of(target, chunk):
        return pl.ds(pl.multiple_of(target * owned + chunk * lanes, lanes), lanes)

    def rotated(step):
        return lax.rem(me + step + 1, parties)

    def late_copy(target, slot):
        return pltpu.make_async_remote_copy(
            late_out.at[target],
            late_in.at[slot],
            late_send.at[target],
            late_recv.at[slot],
            device_id={"ctx": target},
            device_id_type=MESH,
        )

    def filtered(ref, index, columns, shifted, twice, current):
        taps = taps_ref[index, :, columns]
        return taps[0:1, :] * current + taps[1:2, :] * shifted + taps[2:3, :] * twice

    def inside(ref, index, columns):
        current = ref[:, columns].astype(jnp.float32)
        return filtered(
            ref, index, columns, pltpu.roll(current, 1, 0), pltpu.roll(current, 2, 0), current
        )

    def leading(ref, index, columns, before):
        current = ref[0:16, columns].astype(jnp.float32)[0:2]
        before = before[:, columns].astype(jnp.float32)[2 * index - 2 : 2 * index]
        shifted = jnp.concatenate((before[1:2], current[0:1]), axis=0)
        return filtered(ref, index, columns, shifted, before, current)

    def gate(chunk, target):
        columns = columns_of(target, chunk)
        product = inside(key_ref, 1, columns) * inside(value_ref, 2, columns)
        product = jnp.where(token < 2, jnp.zeros_like(product), product)
        gated[chunk, target] = product
        return product

    for copy in inputs[4:7]:
        copy.wait()

    for chunk in range(chunks):

        @pl.loop(0, parties - 1)
        def _(step, chunk=chunk):
            target = rotated(step)
            product = gate(chunk, target)
            scale = scale_of(product)
            scale_out[target, chunk] = scale
            data_out[chunk, target] = encode(product, scale)

        data[chunk, me] = gate(chunk, me)

    inputs[3].wait()
    packed = jnp.concatenate(
        [spec_ref[part, 0, parity, :half, :] for part in range(2) for parity in range(2)], axis=0
    )
    row_index = lax.broadcasted_iota(jnp.int32, packed.shape, 0)
    highest = spec_ref[0, 0, 0, half : half + 1, :]
    packed = jnp.where((row_index == tok_rows) & (me == 0), highest, packed)
    spec_scale = jnp.max(scale_of(packed), axis=1, keepdims=True)
    for target in range(parties):
        scale_out[target, chunks] = jnp.broadcast_to(spec_scale, (1, lanes))
    codes = packed.T
    codes = encode(codes, spec_scale)
    for part in range(2):
        columns = codes[:, part * tok_rows : (part + 1) * tok_rows]
        spec_out[part] = columns.reshape(spec_out.shape[1:])
        spec_in[part, me] = spec_out[part, me]
    scale_in[me, chunks] = jnp.broadcast_to(spec_scale, (1, lanes))

    pl.semaphore_wait(barrier, parties)


    @pl.when(me < parties - 1)
    def _():
        halo.start()
        halo_query.start()

    @pl.loop(0, parties - 1)
    def _(step):
        target = rotated(step)
        spec_copy(target, me).start()
        scale_copy(target, me).start()

    @pl.loop(0, parties - 1)
    def _(step):
        target = rotated(step)
        data_copy(0, target, me).start()

    tables = [
        pltpu.make_async_copy(source, target, table_sem.at[index])
        for index, (source, target) in enumerate(
            (
                (fwd_high_hbm, fwd_high),
                (fwd_low_hbm, fwd_low),
                (bwd_high_hbm, bwd_high),
                (bwd_low_hbm, bwd_low),
            )
        )
    ]
    for table in tables:
        table.start()


    @pl.when(me > 0)
    def _():
        halo.wait_recv()

    @pl.when(me == 0)
    def _():
        halo_in[...] = jnp.zeros_like(halo_in)
        halo_query_in[...] = jnp.zeros_like(halo_query_in)

    def late(chunk, target):
        columns = columns_of(target, chunk)
        rows = leading(key_ref, 1, columns, halo_in) * leading(value_ref, 2, columns, halo_in)
        gated[chunk, target, 0:2, :] = rows
        return rows

    for chunk in range(chunks):
        data[chunk, me, 0:2, :] = late(chunk, me)

    @pl.loop(0, parties - 1)
    def _(step):
        target = rotated(step)
        for chunk in range(chunks):
            late_out[target, chunk] = late(chunk, target)
        late_copy(target, me).start()

    @pl.when(lax.axis_index("ch") != 1)
    def _():
        for chunk in range(1, chunks):

            @pl.loop(0, parties - 1)
            def _(step, chunk=chunk):
                target = rotated(step)
                data_copy(chunk, target, me).start()

    lane_group = lax.broadcasted_iota(jnp.int32, (3 * group_chunk, lanes), 1) // (
        lanes // group_chunk
    )
    slot_group = lax.broadcasted_iota(jnp.int32, (3 * group_chunk, lanes), 0) % group_chunk
    spread = (lane_group == slot_group).astype(jnp.float32).astype(jnp.bfloat16)

    @pl.loop(1, parties)
    def _(step):
        source = lax.rem(me + parties - step, parties)
        spec_copy(me, source).wait_recv()
        relay_copy(plane, source).start()
        scale_copy(me, source).wait_recv()

    @pl.loop(1, parties)
    def _(step):
        relay_copy(1 - plane, lax.rem(me + parties - step, parties)).wait_recv()

    levels = parties.bit_length() - 1
    row = lax.broadcasted_iota(jnp.int32, (rows, lanes), 0)
    for party in range(parties):
        codes = jnp.concatenate((spec_in[0, party], spec_in[1, party]), axis=1)
        decoded = decode(codes, scale_in[party, chunks, :, :1])
        for chunk in range(chunks):
            exact = decoded[chunk * group_chunk : (chunk + 1) * group_chunk]
            high = exact.astype(jnp.bfloat16).astype(jnp.float32)
            middle = (exact - high).astype(jnp.bfloat16).astype(jnp.float32)
            low = exact - high - middle
            terms = jnp.concatenate((high, middle, low), axis=0).astype(jnp.bfloat16)
            wide = lax.dot_general(
                terms, spread, (((0,), (0,)), ((), ())), preferred_element_type=jnp.float32
            )
            if party == 0:
                ends = lax.rem(row, tok_rows) == 0
                wide = wide * jnp.where(ends, 0.5 / (parties * tok_rows), 1.0 / (parties * tok_rows))
            else:
                wide = wide * (1.0 / (parties * tok_rows))
            for parity in range(2):
                pair, side = place_of(2 * reversed_bits(party, levels) + parity, parties)
                for part in range(2):
                    start = part * tok_rows + parity * half
                    response[chunk, pair, side, part] = wide[start : start + half]

    for table in tables:
        table.wait()

    first = lax.broadcasted_iota(jnp.int32, (half, lanes), 0) == 0
    slab = 16

    for chunk in range(chunks):

        @pl.loop(1, parties)
        def _(step, chunk=chunk):
            source = lax.rem(me + parties - step, parties)
            data_copy(chunk, me, source).wait_recv()
            data[chunk, source] = decode(data_in[chunk, source], scale_in[source, chunk])
            if chunk == 0:
                late_copy(me, source).wait_recv()
            data[chunk, source, 0:2, :] = late_in[source, chunk]

        if chunk + 1 < chunks:

            @pl.when(lax.axis_index("ch") == 1)
            def _(chunk=chunk):

                @pl.loop(0, parties - 1)
                def _(step, chunk=chunk):
                    target = rotated(step)
                    data_copy(chunk + 1, target, me).start()

        @pl.loop(0, tok_rows // slab)
        def _(step, chunk=chunk):
            here = pl.ds(pl.multiple_of(step * slab, slab), slab)
            blocks = [data[chunk, party, here, :] for party in range(parties)]
            for pair, signals in enumerate(class_signals(blocks)):
                for side, signal in enumerate(signals):
                    classes[chunk, pair, side, here, :] = jnp.concatenate(
                        split_terms(signal), axis=1
                    )

        @pl.loop(0, parties, unroll=8)
        def _(pair, chunk=chunk):
            signal = classes[chunk, pair].reshape(rows, 2 * lanes)
            both = jnp.concatenate((fwd_high[pair], fwd_low[pair]), axis=0)
            every = jnp.dot(both, signal, preferred_element_type=jnp.float32)
            wide, rest = every[:rows], every[rows:, :lanes]
            spectrum = wide[:, :lanes] + wide[:, lanes:] + rest
            products = []
            for side in range(2):
                data_re = spectrum[side * tok_rows : side * tok_rows + half]
                data_im = spectrum[side * tok_rows + half : (side + 1) * tok_rows]
                resp_re, resp_im = response[chunk, pair, side, 0], response[chunk, pair, side, 1]
                both_re, both_im = data_re * resp_re, data_im * resp_im
                cross = data_re * resp_im + data_im * resp_re
                if side == 0:
                    alone = first & (pair == 0)
                    products.append(both_re - jnp.where(alone, jnp.zeros_like(both_im), both_im))
                    products.append(jnp.where(alone, both_im, cross))
                else:
                    products += [both_re - both_im, cross]
            product = jnp.concatenate(split_terms(jnp.concatenate(products, axis=0)), axis=1)
            both = jnp.concatenate((bwd_high[pair], bwd_low[pair]), axis=0)
            every = jnp.dot(both, product, preferred_element_type=jnp.float32)
            wide, rest = every[:rows], every[rows:, :lanes]
            result = wide[:, :lanes] + wide[:, lanes:] + rest
            inverse[chunk, pair] = result.reshape(2, tok_rows, lanes)

        @pl.loop(0, tok_rows // slab)
        def _(step, chunk=chunk):
            here = pl.ds(pl.multiple_of(step * slab, slab), slab)
            signals = [
                (inverse[chunk, pair, 0, here, :], inverse[chunk, pair, 1, here, :])
                for pair in range(parties)
            ]
            for party, result in enumerate(block_sums(signals)):
                conv[chunk, party, here, :] = result

        @pl.loop(0, parties - 1, unroll=7)
        def _(step, chunk=chunk):
            target = rotated(step)
            result = conv[chunk, target]
            scale = scale_of(result)
            conv_scale_out[chunk, target] = scale
            conv_out[chunk, target] = encode(result, scale)
            conv_copy(chunk, target, me).start()
            conv_scale_copy(chunk, target, me).start()

    @pl.when(me > 0)
    def _():
        halo_query.wait_recv()

    for copy in inputs[7:]:
        copy.wait()

    def short(ref, index, columns):
        current = ref[:, columns].astype(jnp.float32)
        before = halo_query_in[:, columns].astype(jnp.float32)
        shifted = jnp.where(token == 0, before[1:2, :], pltpu.roll(current, 1, 0))
        twice = jnp.where(token == 0, before[0:1, :], pltpu.roll(current, 2, 0))
        twice = jnp.where(token == 1, before[1:2, :], twice)
        taps = taps_ref[index, :, columns]
        return taps[0:1, :] * current + taps[1:2, :] * shifted + taps[2:3, :] * twice

    def finish(chunk, source, conv):
        columns = columns_of(source, chunk)
        mixed = conv + skip_ref[:, columns] * gated[chunk, source]
        out_ref[:, columns] = (short(query_ref, 0, columns) * mixed).astype(jnp.bfloat16)

    for chunk in range(chunks):
        finish(chunk, me, conv[chunk, me])

        @pl.loop(1, parties)
        def _(step, chunk=chunk):
            source = lax.rem(me + parties - step, parties)
            conv_scale_copy(chunk, me, source).wait_recv()
            conv_copy(chunk, me, source).wait_recv()
            finish(chunk, source, decode(conv_in[chunk, source], conv_scale_in[chunk, source]))

    @pl.when(me < parties - 1)
    def _():
        halo.wait_send()
        halo_query.wait_send()

    @pl.loop(1, parties)
    def _(step):
        target = lax.rem(me + step, parties)
        late_copy(target, me).wait_send()
        spec_copy(target, me).wait_send()
        relay_copy(plane, target).wait_send()
        scale_copy(target, me).wait_send()
        for chunk in range(chunks):
            data_copy(chunk, target, me).wait_send()
            conv_copy(chunk, target, me).wait_send()
            conv_scale_copy(chunk, target, me).wait_send()


def one_kernel(tables, query_in, key_in, value_in, short_filter, skip_bias, filter_spectrum):
    tok_rows, width = query_in.shape
    parties = lax.axis_size("ctx")
    group_count = filter_spectrum.shape[4]
    lanes = 128
    chunks = width // parties // lanes
    vmem = pl.BlockSpec(memory_space=pltpu.VMEM)
    hbm = pl.BlockSpec(memory_space=pltpu.HBM)
    f32, bf16 = jnp.float32, jnp.bfloat16
    dma = pltpu.SemaphoreType.DMA
    return pl.pallas_call(
        functools.partial(hyena_kernel, parties),
        out_shape=pltpu.VMEM((tok_rows, width), bf16),
        in_specs=[hbm] * 10,
        out_specs=vmem,
        scratch_shapes=[
            *[pltpu.VMEM((tok_rows, width), bf16)] * 3,
            pltpu.VMEM(short_filter.shape, f32),
            pltpu.VMEM((1, width), f32),
            pltpu.VMEM(filter_spectrum.shape, f32),
            *[pltpu.VMEM((parties, 2 * tok_rows, 2 * tok_rows), bf16)] * 4,
            pltpu.VMEM((3, 16, width), bf16),
            pltpu.VMEM((4, width), bf16),
            pltpu.VMEM((2, width), bf16),
            pltpu.VMEM((4, width), bf16),
            pltpu.VMEM((2, width), bf16),
            *[pltpu.VMEM((parties, chunks, 2, lanes), f32)] * 2,
            *[pltpu.VMEM((2, parties, group_count // parties, tok_rows), bf16)] * 2,
            *[pltpu.VMEM((parties, chunks + 1, 1, lanes), f32)] * 2,
            pltpu.VMEM((chunks, parties, tok_rows, lanes), f32),
            *[pltpu.VMEM((chunks, parties, tok_rows, lanes), bf16)] * 2,
            pltpu.VMEM((chunks, parties, tok_rows, lanes), f32),
            pltpu.VMEM((chunks, parties, 2, tok_rows, 2 * lanes), bf16),
            pltpu.VMEM((chunks, parties, 2, 2, tok_rows // 2, lanes), f32),
            pltpu.VMEM((chunks, parties, 2, tok_rows, lanes), f32),
            pltpu.VMEM((chunks, parties, tok_rows, lanes), f32),
            *[pltpu.VMEM((chunks, parties, tok_rows, lanes), bf16)] * 2,
            *[pltpu.VMEM((chunks, parties, 1, lanes), f32)] * 2,
            dma((9,)),
            dma((4,)),
            dma((2,)),
            dma((2,)),
            dma((parties,)),
            dma((parties,)),
            *[dma((chunks, parties))] * 4,
            *[dma((parties,))] * 6,
            *[dma((chunks, parties))] * 2,
        ],
        compiler_params=pltpu.CompilerParams(
            collective_id=0, has_side_effects=True, vmem_limit_bytes=56 * 1024 * 1024
        ),
    )(
        query_in,
        key_in,
        value_in,
        short_filter,
        skip_bias.reshape(1, width),
        filter_spectrum,
        *[jnp.asarray(table) for table in tables],
    )


def solution(mesh):
    parties = mesh.shape["ctx"]

    def per_device(*args):
        tok_rows, width = args[0].shape
        if width // parties % 128 == 0 and mesh.shape["grp"] == 2:
            return one_kernel(transform_tables(parties, tok_rows), *args)
        return on_device(*args)

    return jax.shard_map(
        per_device,
        mesh=mesh,
        in_specs=(
            P(("grp", "ctx"), "ch"),
            P(("grp", "ctx"), "ch"),
            P(("grp", "ctx"), "ch"),
            P(None, None, "ch"),
            P("ch"),
            P(None, "ctx", None, None, "ch"),
        ),
        out_specs=P(("grp", "ctx"), "ch"),
        check_vma=False,
    )
```

```python
import functools
import math

import jax
import jax.numpy as jnp
import ml_dtypes
import numpy as np
from jax import lax
from jax.experimental import pallas as pl
from jax.experimental.pallas import tpu as pltpu
from jax.sharding import PartitionSpec as P

HIGHEST = lax.Precision.HIGHEST
MESH = pl.DeviceIdType.MESH
POWER = 17
REACH = 2.0 ** (126 / POWER)


def passed_along(value, axis, steps):
    count = lax.axis_size(axis)
    leading, last = (max(0, -steps), min(count, count - steps))
    return lax.ppermute(value, axis, [(source, source + steps) for source in range(leading, last)])


def reversed_bits(number, digits):
    result = number * 0
    for bit_level in range(digits):
        result = result + (number >> bit_level & 1) * (1 << digits - 1 - bit_level)
    return result


def rotate(real_part, imag_part, cosine, sine):
    return (real_part * cosine - imag_part * sine, real_part * sine + imag_part * cosine)


def complex_product(pattern, table_real, table_imag, data_real, data_imag):
    out_real = jnp.einsum(pattern, table_real, data_real, precision=HIGHEST) - jnp.einsum(
        pattern, table_imag, data_imag, precision=HIGHEST
    )
    out_imag = jnp.einsum(pattern, table_real, data_imag, precision=HIGHEST) + jnp.einsum(
        pattern, table_imag, data_real, precision=HIGHEST
    )
    return (out_real, out_imag)


def angle_table(rows, cols, modulus):
    exponent = (
        jnp.arange(rows, dtype=jnp.int32)[:, None]
        * jnp.arange(cols, dtype=jnp.int32)[None, :]
        % modulus
    )
    angle = 2.0 * math.pi / modulus * exponent.astype(jnp.float32)
    return (jnp.cos(angle), jnp.sin(angle))


def whole_convolution(first_real, first_imag, filter_spectrum, parties, levels):
    tok_rows = first_real.shape[0]
    packed = jnp.stack((first_real, first_imag))
    spread = lax.all_to_all(packed, "ctx", split_axis=2, concat_axis=1, tiled=True)
    spectrum = lax.all_to_all(filter_spectrum, "ctx", split_axis=4, concat_axis=1, tiled=True)
    tail = spectrum.shape[2:]
    spectrum = spectrum.reshape(2, *[2] * levels, *tail)
    spectrum = spectrum.transpose(0, *range(levels, 0, -1), *range(levels + 1, levels + 4))
    spectrum = spectrum.reshape(2, parties, *tail)
    size_b = 2 * parties
    total = tok_rows * size_b
    spectrum = spectrum.reshape(2, size_b, tok_rows, spectrum.shape[4])
    columns = spread.shape[2]
    data = spread.reshape(2, size_b // 2, tok_rows, columns)
    outer_cos, outer_sin = angle_table(size_b, size_b // 2, size_b)
    twist_cos, twist_sin = angle_table(size_b, tok_rows, total)
    inner_cos, inner_sin = angle_table(tok_rows, tok_rows, tok_rows)
    section_real, section_imag = complex_product(
        "fn,nac->fac", outer_cos, -outer_sin, data[0], data[1]
    )
    section_real, section_imag = rotate(
        section_real, section_imag, twist_cos[..., None], -twist_sin[..., None]
    )
    freq_real, freq_imag = complex_product(
        "ak,fac->fkc", inner_cos, -inner_sin, section_real, section_imag
    )
    group_local = spectrum.shape[3]
    per_group = columns // group_local
    shaped_real = freq_real.reshape(size_b, tok_rows, group_local, per_group)
    shaped_imag = freq_imag.reshape(size_b, tok_rows, group_local, per_group)
    resp_real = spectrum[0][..., None]
    resp_imag = spectrum[1][..., None]
    prod_real = (shaped_real * resp_real - shaped_imag * resp_imag).reshape(
        size_b, tok_rows, columns
    )
    prod_imag = (shaped_real * resp_imag + shaped_imag * resp_real).reshape(
        size_b, tok_rows, columns
    )
    back_real, back_imag = complex_product(
        "ak,fkc->fac", inner_cos, inner_sin, prod_real, prod_imag
    )
    back_real, back_imag = rotate(back_real, back_imag, twist_cos[..., None], twist_sin[..., None])
    out_real, out_imag = complex_product(
        "nf,fac->nac", outer_cos.T, outer_sin.T, back_real, back_imag
    )
    norm_factor = 1.0 / total
    result = (
        jnp.stack(
            (
                out_real.reshape(size_b // 2 * tok_rows, columns),
                out_imag.reshape(size_b // 2 * tok_rows, columns),
            )
        )
        * norm_factor
    )
    returned = lax.all_to_all(result, "ctx", split_axis=1, concat_axis=2, tiled=True)
    return (returned[0], returned[1])


def on_device(query_in, key_in, value_in, short_filter, skip_bias, filter_spectrum):
    tok_rows, chan_width = query_in.shape
    parties = lax.axis_size("ctx")
    levels = parties.bit_length() - 1
    tap_count = short_filter.shape[1]
    group_count = filter_spectrum.shape[4]
    half_group = chan_width // (2 * group_count)
    packed_width = group_count * half_group
    stacked = jnp.stack((query_in, key_in, value_in))
    earlier = passed_along(stacked[:, tok_rows - (tap_count - 1) :, :], "ctx", 1)
    extended = jnp.concatenate((earlier, stacked), axis=1).astype(jnp.float32)
    filtered = short_filter[:, 0, None, :] * extended[:, tap_count - 1 :, :]
    for tap_lag in range(1, tap_count):
        start_row = tap_count - 1 - tap_lag
        filtered = (
            filtered
            + short_filter[:, tap_lag, None, :] * extended[:, start_row : start_row + tok_rows, :]
        )
    gated = filtered[1] * filtered[2]
    halves = gated.reshape(tok_rows, group_count, 2, half_group)
    first_real = halves[:, :, 0, :].reshape(tok_rows, packed_width)
    first_imag = halves[:, :, 1, :].reshape(tok_rows, packed_width)
    conv_real, conv_imag = whole_convolution(
        first_real, first_imag, filter_spectrum, parties, levels
    )
    conv = jnp.stack(
        (
            conv_real.reshape(tok_rows, group_count, half_group),
            conv_imag.reshape(tok_rows, group_count, half_group),
        ),
        axis=2,
    ).reshape(tok_rows, chan_width)
    return (filtered[0] * (conv + skip_bias[None, :] * gated)).astype(jnp.bfloat16)


def split_terms(value):
    high = value.astype(jnp.bfloat16)
    low = (value - high.astype(jnp.float32)).astype(jnp.bfloat16)
    return high, low


def scale_of(value):
    peak = jnp.max(jnp.abs(value), axis=0, keepdims=True)
    return jnp.maximum(peak * 1.0078125, 2.0**-100)


def encode(value, scale):
    ratio = value * (REACH / scale)
    square = ratio * ratio
    fourth = square * square
    eighth = fourth * fourth
    return (ratio * (eighth * eighth)).astype(jnp.bfloat16)


def decode(block, scale):
    code = block.astype(jnp.float32)
    root = jnp.exp(jnp.log(jnp.maximum(jnp.abs(code), 2.0**-126)) * (1.0 / POWER))
    root = root * (scale * (1.0 / REACH))
    return jnp.where(code < 0, -root, jnp.where(code > 0, root, jnp.zeros_like(root)))


def place_of(rho, parties):
    if rho % parties == 0:
        return 0, rho // parties
    return (rho, 0) if rho < parties else (2 * parties - rho, 1)


def transform_tables(parties, tok_rows):
    classes, half = 2 * parties, tok_rows // 2
    total = classes * tok_rows
    time = np.arange(tok_rows)
    table = np.zeros((parties, 2, 2, half, 2, tok_rows))
    for rho in range(classes):
        pair, side = place_of(rho, parties)
        angle = 2.0 * np.pi / total * ((classes * np.arange(half)[:, None] + rho) * time % total)
        cosine, sine = np.cos(angle), np.sin(angle)
        if pair == 0:
            table[pair, side, 0, :, side] = cosine
            table[pair, side, 1, :, side] = -sine
        else:
            sign = 1.0 - 2.0 * side
            table[pair, side, 0, :, 0] = cosine
            table[pair, side, 0, :, 1] = sign * sine
            table[pair, side, 1, :, 0] = -sine
            table[pair, side, 1, :, 1] = sign * cosine
    table[0, 0, 1, 0, 0] = 1.0 - 2.0 * (time % 2)
    forward = table.reshape(parties, 2 * tok_rows, 2 * tok_rows)

    def parts(matrix):
        high = matrix.astype(ml_dtypes.bfloat16)
        low = (matrix - high.astype(np.float64)).astype(ml_dtypes.bfloat16)
        return high, low

    return parts(forward) + parts(np.ascontiguousarray(forward.transpose(0, 2, 1)))


def weighted(terms):
    result = None
    for weight, value in terms:
        if abs(weight) < 1e-12:
            continue
        if abs(abs(weight) - 1.0) > 1e-12:
            term = value * abs(weight)
        else:
            term = value
        if result is None:
            result = term if weight > 0 else -term
        else:
            result = result + term if weight > 0 else result - term
    return result


def class_signals(blocks):
    parties = len(blocks)
    middle = parties // 2
    sums = [blocks[i] + blocks[i + middle] for i in range(middle)]
    gaps = [blocks[i] - blocks[i + middle] for i in range(middle)]
    signals = []
    for pair in range(parties):
        if pair == 0:
            even = weighted([(1.0, sums[i]) for i in range(0, middle, 2)])
            odd = weighted([(1.0, sums[i]) for i in range(1, middle, 2)])
            signals.append((even + odd, even - odd))
            continue
        used = blocks if pair % 2 else (sums if pair % 4 == 0 else gaps)
        angles = [math.pi * pair * i / parties for i in range(len(used))]
        real = weighted([(math.cos(a), v) for a, v in zip(angles, used)])
        imag = weighted([(-math.sin(a), v) for a, v in zip(angles, used)])
        signals.append((real, imag))
    return signals


def block_sums(signals):
    parties = len(signals)
    middle = parties // 2
    results = [None] * parties
    for i in range(middle):
        even = {0: [], 2: []}
        for pair in range(0, parties, 2):
            angle = math.pi * pair * i / parties
            real, imag = signals[pair]
            if pair == 0:
                even[0] += [(1.0, real), (1.0 - 2.0 * (i % 2), imag)]
            else:
                even[pair % 4] += [(math.cos(angle), real), (-math.sin(angle), imag)]
        same, flipped = weighted(even[0]), weighted(even[2])
        for place, base in ((i, same + flipped), (i + middle, same - flipped)):
            odd = []
            for pair in range(1, parties, 2):
                angle = math.pi * pair * place / parties
                real, imag = signals[pair]
                odd += [(math.cos(angle), real), (-math.sin(angle), imag)]
            results[place] = base + weighted(odd)
    return results


def hyena_kernel(
    parties,
    query_hbm,
    key_hbm,
    value_hbm,
    taps_hbm,
    skip_hbm,
    spec_hbm,
    fwd_high_hbm,
    fwd_low_hbm,
    bwd_high_hbm,
    bwd_low_hbm,
    out_ref,
    query_ref,
    key_ref,
    value_ref,
    taps_ref,
    skip_ref,
    spec_ref,
    fwd_high,
    fwd_low,
    bwd_high,
    bwd_low,
    edge,
    halo_out,
    halo_query_out,
    halo_in,
    halo_query_in,
    late_out,
    late_in,
    spec_out,
    spec_in,
    scale_out,
    scale_in,
    gated,
    data_out,
    data_in,
    data,
    classes,
    response,
    inverse,
    conv,
    conv_out,
    conv_in,
    conv_scale_out,
    conv_scale_in,
    input_sem,
    table_sem,
    halo_send,
    halo_recv,
    spec_send,
    spec_recv,
    data_send,
    data_recv,
    conv_send,
    conv_recv,
    late_send,
    late_recv,
    relay_send,
    relay_recv,
    scale_send,
    scale_recv,
    conv_scale_send,
    conv_scale_recv,
):
    me = lax.axis_index("ctx")
    plane = lax.axis_index("grp")
    tok_rows, width = query_ref.shape
    owned = width // parties
    chunks, lanes = data_out.shape[0], gated.shape[3]
    group_count = spec_ref.shape[4]
    group_owned = group_count // parties
    group_chunk = group_owned // chunks
    half = tok_rows // 2
    rows = 2 * tok_rows

    barrier = pltpu.get_barrier_semaphore()

    @pl.loop(1, parties)
    def _(step):
        pl.semaphore_signal(
            barrier, inc=1, device_id={"ctx": lax.rem(me + step, parties)}, device_id_type=MESH
        )

    pl.semaphore_signal(barrier, inc=1, device_id={"grp": 1 - plane}, device_id_type=MESH)

    inputs = [
        pltpu.make_async_copy(source, target, input_sem.at[index])
        for index, (source, target) in enumerate(
            (
                (query_hbm.at[tok_rows - 16 :, :], edge.at[0]),
                (key_hbm.at[tok_rows - 16 :, :], edge.at[1]),
                (value_hbm.at[tok_rows - 16 :, :], edge.at[2]),
                (spec_hbm, spec_ref),
                (key_hbm, key_ref),
                (value_hbm, value_ref),
                (taps_hbm, taps_ref),
                (query_hbm, query_ref),
                (skip_hbm, skip_ref),
            )
        )
    ]
    for copy in inputs:
        copy.start()

    for copy in inputs[:3]:
        copy.wait()
    last = edge[...].astype(jnp.float32)[:, 14:16, :]
    halo_out[...] = last[1:].reshape(4, width).astype(jnp.bfloat16)
    halo_query_out[...] = last[0].astype(jnp.bfloat16)
    def halo_copy(source, target, index):
        return pltpu.make_async_remote_copy(
            source,
            target,
            halo_send.at[index],
            halo_recv.at[index],
            device_id={"ctx": lax.rem(me + 1, parties)},
            device_id_type=MESH,
        )

    halo = halo_copy(halo_out, halo_in, 0)
    halo_query = halo_copy(halo_query_out, halo_query_in, 1)

    def spec_copy(target, slot):
        return pltpu.make_async_remote_copy(
            spec_out.at[plane, target],
            spec_in.at[plane, slot],
            spec_send.at[target],
            spec_recv.at[slot],
            device_id={"ctx": target},
            device_id_type=MESH,
        )

    def relay_copy(part, source):
        return pltpu.make_async_remote_copy(
            spec_in.at[part, source],
            spec_in.at[part, source],
            relay_send.at[source],
            relay_recv.at[source],
            device_id={"grp": 1 - plane},
            device_id_type=MESH,
        )

    def scale_copy(target, slot):
        return pltpu.make_async_remote_copy(
            scale_out.at[target],
            scale_in.at[slot],
            scale_send.at[target],
            scale_recv.at[slot],
            device_id={"ctx": target},
            device_id_type=MESH,
        )

    def conv_scale_copy(chunk, target, slot):
        return pltpu.make_async_remote_copy(
            conv_scale_out.at[chunk, target],
            conv_scale_in.at[chunk, slot],
            conv_scale_send.at[chunk, target],
            conv_scale_recv.at[chunk, slot],
            device_id={"ctx": target},
            device_id_type=MESH,
        )

    def data_copy(chunk, target, slot):
        return pltpu.make_async_remote_copy(
            data_out.at[chunk, target],
            data_in.at[chunk, slot],
            data_send.at[chunk, target],
            data_recv.at[chunk, slot],
            device_id={"ctx": target},
            device_id_type=MESH,
        )

    def conv_copy(chunk, target, slot):
        return pltpu.make_async_remote_copy(
            conv_out.at[chunk, target],
            conv_in.at[chunk, slot],
            conv_send.at[chunk, target],
            conv_recv.at[chunk, slot],
            device_id={"ctx": target},
            device_id_type=MESH,
        )

    token = lax.broadcasted_iota(jnp.int32, (tok_rows, lanes), 0)

    def columns_of(target, chunk):
        return pl.ds(pl.multiple_of(target * owned + chunk * lanes, lanes), lanes)

    def rotated(step):
        return lax.rem(me + step + 1, parties)

    def late_copy(target, slot):
        return pltpu.make_async_remote_copy(
            late_out.at[target],
            late_in.at[slot],
            late_send.at[target],
            late_recv.at[slot],
            device_id={"ctx": target},
            device_id_type=MESH,
        )

    def filtered(ref, index, columns, shifted, twice, current):
        taps = taps_ref[index, :, columns]
        return taps[0:1, :] * current + taps[1:2, :] * shifted + taps[2:3, :] * twice

    def inside(ref, index, columns):
        current = ref[:, columns].astype(jnp.float32)
        return filtered(
            ref, index, columns, pltpu.roll(current, 1, 0), pltpu.roll(current, 2, 0), current
        )

    def leading(ref, index, columns, before):
        current = ref[0:16, columns].astype(jnp.float32)[0:2]
        before = before[:, columns].astype(jnp.float32)[2 * index - 2 : 2 * index]
        shifted = jnp.concatenate((before[1:2], current[0:1]), axis=0)
        return filtered(ref, index, columns, shifted, before, current)

    def gate(chunk, target):
        columns = columns_of(target, chunk)
        product = inside(key_ref, 1, columns) * inside(value_ref, 2, columns)
        product = jnp.where(token < 2, jnp.zeros_like(product), product)
        gated[chunk, target] = product
        return product

    for copy in inputs[4:7]:
        copy.wait()

    for chunk in range(chunks):

        @pl.loop(0, parties - 1)
        def _(step, chunk=chunk):
            target = rotated(step)
            product = gate(chunk, target)
            scale = scale_of(product)
            scale_out[target, chunk] = scale
            data_out[chunk, target] = encode(product, scale)

        data[chunk, me] = gate(chunk, me)

    inputs[3].wait()
    packed = jnp.concatenate(
        [spec_ref[part, 0, parity, :half, :] for part in range(2) for parity in range(2)], axis=0
    )
    row_index = lax.broadcasted_iota(jnp.int32, packed.shape, 0)
    highest = spec_ref[0, 0, 0, half : half + 1, :]
    packed = jnp.where((row_index == tok_rows) & (me == 0), highest, packed)
    spec_scale = jnp.max(scale_of(packed), axis=1, keepdims=True)
    for target in range(parties):
        scale_out[target, chunks] = jnp.broadcast_to(spec_scale, (1, lanes))
    codes = packed.T
    codes = encode(codes, spec_scale)
    for part in range(2):
        columns = codes[:, part * tok_rows : (part + 1) * tok_rows]
        spec_out[part] = columns.reshape(spec_out.shape[1:])
        spec_in[part, me] = spec_out[part, me]
    scale_in[me, chunks] = jnp.broadcast_to(spec_scale, (1, lanes))

    pl.semaphore_wait(barrier, parties)


    @pl.when(me < parties - 1)
    def _():
        halo.start()

    @pl.loop(0, parties - 1)
    def _(step):
        target = rotated(step)
        spec_copy(target, me).start()
        scale_copy(target, me).start()

    @pl.loop(0, parties - 1)
    def _(step):
        target = rotated(step)
        data_copy(0, target, me).start()

    tables = [
        pltpu.make_async_copy(source, target, table_sem.at[index])
        for index, (source, target) in enumerate(
            (
                (fwd_high_hbm, fwd_high),
                (fwd_low_hbm, fwd_low),
                (bwd_high_hbm, bwd_high),
                (bwd_low_hbm, bwd_low),
            )
        )
    ]
    for table in tables:
        table.start()


    @pl.when(me > 0)
    def _():
        halo.wait_recv()

    @pl.when(me == 0)
    def _():
        halo_in[...] = jnp.zeros_like(halo_in)
        halo_query_in[...] = jnp.zeros_like(halo_query_in)

    def late(chunk, target):
        columns = columns_of(target, chunk)
        rows = leading(key_ref, 1, columns, halo_in) * leading(value_ref, 2, columns, halo_in)
        gated[chunk, target, 0:2, :] = rows
        return rows

    for chunk in range(chunks):
        data[chunk, me, 0:2, :] = late(chunk, me)

    @pl.loop(0, parties - 1)
    def _(step):
        target = rotated(step)
        for chunk in range(chunks):
            late_out[target, chunk] = late(chunk, target)
        late_copy(target, me).start()

    @pl.when(lax.axis_index("ch") != 1)
    def _():
        for chunk in range(1, chunks):

            @pl.loop(0, parties - 1)
            def _(step, chunk=chunk):
                target = rotated(step)
                data_copy(chunk, target, me).start()

    @pl.when(me < parties - 1)
    def _():
        halo_query.start()

    lane_group = lax.broadcasted_iota(jnp.int32, (3 * group_chunk, lanes), 1) // (
        lanes // group_chunk
    )
    slot_group = lax.broadcasted_iota(jnp.int32, (3 * group_chunk, lanes), 0) % group_chunk
    spread = (lane_group == slot_group).astype(jnp.float32).astype(jnp.bfloat16)

    @pl.loop(1, parties)
    def _(step):
        source = lax.rem(me + parties - step, parties)
        spec_copy(me, source).wait_recv()
        relay_copy(plane, source).start()
        scale_copy(me, source).wait_recv()

    @pl.loop(1, parties)
    def _(step):
        relay_copy(1 - plane, lax.rem(me + parties - step, parties)).wait_recv()

    levels = parties.bit_length() - 1
    row = lax.broadcasted_iota(jnp.int32, (rows, lanes), 0)
    for party in range(parties):
        codes = jnp.concatenate((spec_in[0, party], spec_in[1, party]), axis=1)
        decoded = decode(codes, scale_in[party, chunks, :, :1])
        for chunk in range(chunks):
            exact = decoded[chunk * group_chunk : (chunk + 1) * group_chunk]
            high = exact.astype(jnp.bfloat16).astype(jnp.float32)
            middle = (exact - high).astype(jnp.bfloat16).astype(jnp.float32)
            low = exact - high - middle
            terms = jnp.concatenate((high, middle, low), axis=0).astype(jnp.bfloat16)
            wide = lax.dot_general(
                terms, spread, (((0,), (0,)), ((), ())), preferred_element_type=jnp.float32
            )
            if party == 0:
                ends = lax.rem(row, tok_rows) == 0
                wide = wide * jnp.where(ends, 0.5 / (parties * tok_rows), 1.0 / (parties * tok_rows))
            else:
                wide = wide * (1.0 / (parties * tok_rows))
            for parity in range(2):
                pair, side = place_of(2 * reversed_bits(party, levels) + parity, parties)
                for part in range(2):
                    start = part * tok_rows + parity * half
                    response[chunk, pair, side, part] = wide[start : start + half]

    for table in tables:
        table.wait()

    first = lax.broadcasted_iota(jnp.int32, (half, lanes), 0) == 0
    slab = 16

    for chunk in range(chunks):

        @pl.loop(1, parties)
        def _(step, chunk=chunk):
            source = lax.rem(me + parties - step, parties)
            data_copy(chunk, me, source).wait_recv()
            data[chunk, source] = decode(data_in[chunk, source], scale_in[source, chunk])
            if chunk == 0:
                late_copy(me, source).wait_recv()
            data[chunk, source, 0:2, :] = late_in[source, chunk]

        if chunk + 1 < chunks:

            @pl.when(lax.axis_index("ch") == 1)
            def _(chunk=chunk):

                @pl.loop(0, parties - 1)
                def _(step, chunk=chunk):
                    target = rotated(step)
                    data_copy(chunk + 1, target, me).start()

        @pl.loop(0, tok_rows // slab, unroll=4)
        def _(step, chunk=chunk):
            here = pl.ds(pl.multiple_of(step * slab, slab), slab)
            blocks = [data[chunk, party, here, :] for party in range(parties)]
            for pair, signals in enumerate(class_signals(blocks)):
                for side, signal in enumerate(signals):
                    classes[chunk, pair, side, here, :] = jnp.concatenate(
                        split_terms(signal), axis=1
                    )

        @pl.loop(0, parties, unroll=8)
        def _(pair, chunk=chunk):
            signal = classes[chunk, pair].reshape(rows, 2 * lanes)
            both = jnp.concatenate((fwd_high[pair], fwd_low[pair]), axis=0)
            every = jnp.dot(both, signal, preferred_element_type=jnp.float32)
            wide, rest = every[:rows], every[rows:, :lanes]
            spectrum = wide[:, :lanes] + wide[:, lanes:] + rest
            products = []
            for side in range(2):
                data_re = spectrum[side * tok_rows : side * tok_rows + half]
                data_im = spectrum[side * tok_rows + half : (side + 1) * tok_rows]
                resp_re, resp_im = response[chunk, pair, side, 0], response[chunk, pair, side, 1]
                both_re, both_im = data_re * resp_re, data_im * resp_im
                cross = data_re * resp_im + data_im * resp_re
                if side == 0:
                    alone = first & (pair == 0)
                    products.append(both_re - jnp.where(alone, jnp.zeros_like(both_im), both_im))
                    products.append(jnp.where(alone, both_im, cross))
                else:
                    products += [both_re - both_im, cross]
            product = jnp.concatenate(split_terms(jnp.concatenate(products, axis=0)), axis=1)
            both = jnp.concatenate((bwd_high[pair], bwd_low[pair]), axis=0)
            every = jnp.dot(both, product, preferred_element_type=jnp.float32)
            wide, rest = every[:rows], every[rows:, :lanes]
            result = wide[:, :lanes] + wide[:, lanes:] + rest
            inverse[chunk, pair] = result.reshape(2, tok_rows, lanes)

        @pl.loop(0, tok_rows // slab, unroll=4)
        def _(step, chunk=chunk):
            here = pl.ds(pl.multiple_of(step * slab, slab), slab)
            signals = [
                (inverse[chunk, pair, 0, here, :], inverse[chunk, pair, 1, here, :])
                for pair in range(parties)
            ]
            for party, result in enumerate(block_sums(signals)):
                conv[chunk, party, here, :] = result

        @pl.loop(0, parties - 1, unroll=7)
        def _(step, chunk=chunk):
            target = rotated(step)
            result = conv[chunk, target]
            scale = scale_of(result)
            conv_scale_out[chunk, target] = scale
            conv_out[chunk, target] = encode(result, scale)
            conv_copy(chunk, target, me).start()
            conv_scale_copy(chunk, target, me).start()

    @pl.when(me > 0)
    def _():
        halo_query.wait_recv()

    for copy in inputs[7:]:
        copy.wait()

    def short(ref, index, columns):
        current = ref[:, columns].astype(jnp.float32)
        before = halo_query_in[:, columns].astype(jnp.float32)
        shifted = jnp.where(token == 0, before[1:2, :], pltpu.roll(current, 1, 0))
        twice = jnp.where(token == 0, before[0:1, :], pltpu.roll(current, 2, 0))
        twice = jnp.where(token == 1, before[1:2, :], twice)
        taps = taps_ref[index, :, columns]
        return taps[0:1, :] * current + taps[1:2, :] * shifted + taps[2:3, :] * twice

    def finish(chunk, source, conv):
        columns = columns_of(source, chunk)
        mixed = conv + skip_ref[:, columns] * gated[chunk, source]
        out_ref[:, columns] = (short(query_ref, 0, columns) * mixed).astype(jnp.bfloat16)

    for chunk in range(chunks):
        finish(chunk, me, conv[chunk, me])

        @pl.loop(1, parties)
        def _(step, chunk=chunk):
            source = lax.rem(me + parties - step, parties)
            conv_scale_copy(chunk, me, source).wait_recv()
            conv_copy(chunk, me, source).wait_recv()
            finish(chunk, source, decode(conv_in[chunk, source], conv_scale_in[chunk, source]))

    @pl.when(me < parties - 1)
    def _():
        halo.wait_send()
        halo_query.wait_send()

    @pl.loop(1, parties)
    def _(step):
        target = lax.rem(me + step, parties)
        late_copy(target, me).wait_send()
        spec_copy(target, me).wait_send()
        relay_copy(plane, target).wait_send()
        scale_copy(target, me).wait_send()
        for chunk in range(chunks):
            data_copy(chunk, target, me).wait_send()
            conv_copy(chunk, target, me).wait_send()
            conv_scale_copy(chunk, target, me).wait_send()


def one_kernel(tables, query_in, key_in, value_in, short_filter, skip_bias, filter_spectrum):
    tok_rows, width = query_in.shape
    parties = lax.axis_size("ctx")
    group_count = filter_spectrum.shape[4]
    lanes = 128
    chunks = width // parties // lanes
    vmem = pl.BlockSpec(memory_space=pltpu.VMEM)
    hbm = pl.BlockSpec(memory_space=pltpu.HBM)
    f32, bf16 = jnp.float32, jnp.bfloat16
    dma = pltpu.SemaphoreType.DMA
    return pl.pallas_call(
        functools.partial(hyena_kernel, parties),
        out_shape=pltpu.VMEM((tok_rows, width), bf16),
        in_specs=[hbm] * 10,
        out_specs=vmem,
        scratch_shapes=[
            *[pltpu.VMEM((tok_rows, width), bf16)] * 3,
            pltpu.VMEM(short_filter.shape, f32),
            pltpu.VMEM((1, width), f32),
            pltpu.VMEM(filter_spectrum.shape, f32),
            *[pltpu.VMEM((parties, 2 * tok_rows, 2 * tok_rows), bf16)] * 4,
            pltpu.VMEM((3, 16, width), bf16),
            pltpu.VMEM((4, width), bf16),
            pltpu.VMEM((2, width), bf16),
            pltpu.VMEM((4, width), bf16),
            pltpu.VMEM((2, width), bf16),
            *[pltpu.VMEM((parties, chunks, 2, lanes), f32)] * 2,
            *[pltpu.VMEM((2, parties, group_count // parties, tok_rows), bf16)] * 2,
            *[pltpu.VMEM((parties, chunks + 1, 1, lanes), f32)] * 2,
            pltpu.VMEM((chunks, parties, tok_rows, lanes), f32),
            *[pltpu.VMEM((chunks, parties, tok_rows, lanes), bf16)] * 2,
            pltpu.VMEM((chunks, parties, tok_rows, lanes), f32),
            pltpu.VMEM((chunks, parties, 2, tok_rows, 2 * lanes), bf16),
            pltpu.VMEM((chunks, parties, 2, 2, tok_rows // 2, lanes), f32),
            pltpu.VMEM((chunks, parties, 2, tok_rows, lanes), f32),
            pltpu.VMEM((chunks, parties, tok_rows, lanes), f32),
            *[pltpu.VMEM((chunks, parties, tok_rows, lanes), bf16)] * 2,
            *[pltpu.VMEM((chunks, parties, 1, lanes), f32)] * 2,
            dma((9,)),
            dma((4,)),
            dma((2,)),
            dma((2,)),
            dma((parties,)),
            dma((parties,)),
            *[dma((chunks, parties))] * 4,
            *[dma((parties,))] * 6,
            *[dma((chunks, parties))] * 2,
        ],
        compiler_params=pltpu.CompilerParams(
            collective_id=0, has_side_effects=True, vmem_limit_bytes=56 * 1024 * 1024
        ),
    )(
        query_in,
        key_in,
        value_in,
        short_filter,
        skip_bias.reshape(1, width),
        filter_spectrum,
        *[jnp.asarray(table) for table in tables],
    )


def solution(mesh):
    parties = mesh.shape["ctx"]

    def per_device(*args):
        tok_rows, width = args[0].shape
        if width // parties % 128 == 0 and mesh.shape["grp"] == 2:
            return one_kernel(transform_tables(parties, tok_rows), *args)
        return on_device(*args)

    return jax.shard_map(
        per_device,
        mesh=mesh,
        in_specs=(
            P(("grp", "ctx"), "ch"),
            P(("grp", "ctx"), "ch"),
            P(("grp", "ctx"), "ch"),
            P(None, None, "ch"),
            P("ch"),
            P(None, "ctx", None, None, "ch"),
        ),
        out_specs=P(("grp", "ctx"), "ch"),
        check_vma=False,
    )
```

```python
import functools
import math

import jax
import jax.numpy as jnp
import ml_dtypes
import numpy as np
from jax import lax
from jax.experimental import pallas as pl
from jax.experimental.pallas import tpu as pltpu
from jax.sharding import PartitionSpec as P

HIGHEST = lax.Precision.HIGHEST
MESH = pl.DeviceIdType.MESH
POWER = 17
REACH = 2.0 ** (126 / POWER)


def passed_along(value, axis, steps):
    count = lax.axis_size(axis)
    leading, last = (max(0, -steps), min(count, count - steps))
    return lax.ppermute(value, axis, [(source, source + steps) for source in range(leading, last)])


def reversed_bits(number, digits):
    result = number * 0
    for bit_level in range(digits):
        result = result + (number >> bit_level & 1) * (1 << digits - 1 - bit_level)
    return result


def rotate(real_part, imag_part, cosine, sine):
    return (real_part * cosine - imag_part * sine, real_part * sine + imag_part * cosine)


def complex_product(pattern, table_real, table_imag, data_real, data_imag):
    out_real = jnp.einsum(pattern, table_real, data_real, precision=HIGHEST) - jnp.einsum(
        pattern, table_imag, data_imag, precision=HIGHEST
    )
    out_imag = jnp.einsum(pattern, table_real, data_imag, precision=HIGHEST) + jnp.einsum(
        pattern, table_imag, data_real, precision=HIGHEST
    )
    return (out_real, out_imag)


def angle_table(rows, cols, modulus):
    exponent = (
        jnp.arange(rows, dtype=jnp.int32)[:, None]
        * jnp.arange(cols, dtype=jnp.int32)[None, :]
        % modulus
    )
    angle = 2.0 * math.pi / modulus * exponent.astype(jnp.float32)
    return (jnp.cos(angle), jnp.sin(angle))


def whole_convolution(first_real, first_imag, filter_spectrum, parties, levels):
    tok_rows = first_real.shape[0]
    packed = jnp.stack((first_real, first_imag))
    spread = lax.all_to_all(packed, "ctx", split_axis=2, concat_axis=1, tiled=True)
    spectrum = lax.all_to_all(filter_spectrum, "ctx", split_axis=4, concat_axis=1, tiled=True)
    tail = spectrum.shape[2:]
    spectrum = spectrum.reshape(2, *[2] * levels, *tail)
    spectrum = spectrum.transpose(0, *range(levels, 0, -1), *range(levels + 1, levels + 4))
    spectrum = spectrum.reshape(2, parties, *tail)
    size_b = 2 * parties
    total = tok_rows * size_b
    spectrum = spectrum.reshape(2, size_b, tok_rows, spectrum.shape[4])
    columns = spread.shape[2]
    data = spread.reshape(2, size_b // 2, tok_rows, columns)
    outer_cos, outer_sin = angle_table(size_b, size_b // 2, size_b)
    twist_cos, twist_sin = angle_table(size_b, tok_rows, total)
    inner_cos, inner_sin = angle_table(tok_rows, tok_rows, tok_rows)
    section_real, section_imag = complex_product(
        "fn,nac->fac", outer_cos, -outer_sin, data[0], data[1]
    )
    section_real, section_imag = rotate(
        section_real, section_imag, twist_cos[..., None], -twist_sin[..., None]
    )
    freq_real, freq_imag = complex_product(
        "ak,fac->fkc", inner_cos, -inner_sin, section_real, section_imag
    )
    group_local = spectrum.shape[3]
    per_group = columns // group_local
    shaped_real = freq_real.reshape(size_b, tok_rows, group_local, per_group)
    shaped_imag = freq_imag.reshape(size_b, tok_rows, group_local, per_group)
    resp_real = spectrum[0][..., None]
    resp_imag = spectrum[1][..., None]
    prod_real = (shaped_real * resp_real - shaped_imag * resp_imag).reshape(
        size_b, tok_rows, columns
    )
    prod_imag = (shaped_real * resp_imag + shaped_imag * resp_real).reshape(
        size_b, tok_rows, columns
    )
    back_real, back_imag = complex_product(
        "ak,fkc->fac", inner_cos, inner_sin, prod_real, prod_imag
    )
    back_real, back_imag = rotate(back_real, back_imag, twist_cos[..., None], twist_sin[..., None])
    out_real, out_imag = complex_product(
        "nf,fac->nac", outer_cos.T, outer_sin.T, back_real, back_imag
    )
    norm_factor = 1.0 / total
    result = (
        jnp.stack(
            (
                out_real.reshape(size_b // 2 * tok_rows, columns),
                out_imag.reshape(size_b // 2 * tok_rows, columns),
            )
        )
        * norm_factor
    )
    returned = lax.all_to_all(result, "ctx", split_axis=1, concat_axis=2, tiled=True)
    return (returned[0], returned[1])


def on_device(query_in, key_in, value_in, short_filter, skip_bias, filter_spectrum):
    tok_rows, chan_width = query_in.shape
    parties = lax.axis_size("ctx")
    levels = parties.bit_length() - 1
    tap_count = short_filter.shape[1]
    group_count = filter_spectrum.shape[4]
    half_group = chan_width // (2 * group_count)
    packed_width = group_count * half_group
    stacked = jnp.stack((query_in, key_in, value_in))
    earlier = passed_along(stacked[:, tok_rows - (tap_count - 1) :, :], "ctx", 1)
    extended = jnp.concatenate((earlier, stacked), axis=1).astype(jnp.float32)
    filtered = short_filter[:, 0, None, :] * extended[:, tap_count - 1 :, :]
    for tap_lag in range(1, tap_count):
        start_row = tap_count - 1 - tap_lag
        filtered = (
            filtered
            + short_filter[:, tap_lag, None, :] * extended[:, start_row : start_row + tok_rows, :]
        )
    gated = filtered[1] * filtered[2]
    halves = gated.reshape(tok_rows, group_count, 2, half_group)
    first_real = halves[:, :, 0, :].reshape(tok_rows, packed_width)
    first_imag = halves[:, :, 1, :].reshape(tok_rows, packed_width)
    conv_real, conv_imag = whole_convolution(
        first_real, first_imag, filter_spectrum, parties, levels
    )
    conv = jnp.stack(
        (
            conv_real.reshape(tok_rows, group_count, half_group),
            conv_imag.reshape(tok_rows, group_count, half_group),
        ),
        axis=2,
    ).reshape(tok_rows, chan_width)
    return (filtered[0] * (conv + skip_bias[None, :] * gated)).astype(jnp.bfloat16)


def split_terms(value):
    high = value.astype(jnp.bfloat16)
    low = (value - high.astype(jnp.float32)).astype(jnp.bfloat16)
    return high, low


def scale_of(value):
    peak = jnp.max(jnp.abs(value), axis=0, keepdims=True)
    return jnp.maximum(peak * 1.0078125, 2.0**-100)


def encode(value, scale):
    ratio = value * (REACH / scale)
    square = ratio * ratio
    fourth = square * square
    eighth = fourth * fourth
    return (ratio * (eighth * eighth)).astype(jnp.bfloat16)


def decode(block, scale):
    code = block.astype(jnp.float32)
    root = jnp.exp(jnp.log(jnp.maximum(jnp.abs(code), 2.0**-126)) * (1.0 / POWER))
    root = root * (scale * (1.0 / REACH))
    return jnp.where(code < 0, -root, jnp.where(code > 0, root, jnp.zeros_like(root)))


def place_of(rho, parties):
    if rho % parties == 0:
        return 0, rho // parties
    return (rho, 0) if rho < parties else (2 * parties - rho, 1)


def transform_tables(parties, tok_rows):
    classes, half = 2 * parties, tok_rows // 2
    total = classes * tok_rows
    time = np.arange(tok_rows)
    table = np.zeros((parties, 2, 2, half, 2, tok_rows))
    for rho in range(classes):
        pair, side = place_of(rho, parties)
        angle = 2.0 * np.pi / total * ((classes * np.arange(half)[:, None] + rho) * time % total)
        cosine, sine = np.cos(angle), np.sin(angle)
        if pair == 0:
            table[pair, side, 0, :, side] = cosine
            table[pair, side, 1, :, side] = -sine
        else:
            sign = 1.0 - 2.0 * side
            table[pair, side, 0, :, 0] = cosine
            table[pair, side, 0, :, 1] = sign * sine
            table[pair, side, 1, :, 0] = -sine
            table[pair, side, 1, :, 1] = sign * cosine
    table[0, 0, 1, 0, 0] = 1.0 - 2.0 * (time % 2)
    forward = table.reshape(parties, 2 * tok_rows, 2 * tok_rows)

    def parts(matrix):
        high = matrix.astype(ml_dtypes.bfloat16)
        low = (matrix - high.astype(np.float64)).astype(ml_dtypes.bfloat16)
        return high, low

    return parts(forward) + parts(np.ascontiguousarray(forward.transpose(0, 2, 1)))


def weighted(terms):
    result = None
    for weight, value in terms:
        if abs(weight) < 1e-12:
            continue
        if abs(abs(weight) - 1.0) > 1e-12:
            term = value * abs(weight)
        else:
            term = value
        if result is None:
            result = term if weight > 0 else -term
        else:
            result = result + term if weight > 0 else result - term
    return result


def class_signals(blocks):
    parties = len(blocks)
    middle = parties // 2
    sums = [blocks[i] + blocks[i + middle] for i in range(middle)]
    gaps = [blocks[i] - blocks[i + middle] for i in range(middle)]
    signals = []
    for pair in range(parties):
        if pair == 0:
            even = weighted([(1.0, sums[i]) for i in range(0, middle, 2)])
            odd = weighted([(1.0, sums[i]) for i in range(1, middle, 2)])
            signals.append((even + odd, even - odd))
            continue
        used = blocks if pair % 2 else (sums if pair % 4 == 0 else gaps)
        angles = [math.pi * pair * i / parties for i in range(len(used))]
        real = weighted([(math.cos(a), v) for a, v in zip(angles, used)])
        imag = weighted([(-math.sin(a), v) for a, v in zip(angles, used)])
        signals.append((real, imag))
    return signals


def block_sums(signals):
    parties = len(signals)
    middle = parties // 2
    results = [None] * parties
    for i in range(middle):
        even = {0: [], 2: []}
        for pair in range(0, parties, 2):
            angle = math.pi * pair * i / parties
            real, imag = signals[pair]
            if pair == 0:
                even[0] += [(1.0, real), (1.0 - 2.0 * (i % 2), imag)]
            else:
                even[pair % 4] += [(math.cos(angle), real), (-math.sin(angle), imag)]
        same, flipped = weighted(even[0]), weighted(even[2])
        for place, base in ((i, same + flipped), (i + middle, same - flipped)):
            odd = []
            for pair in range(1, parties, 2):
                angle = math.pi * pair * place / parties
                real, imag = signals[pair]
                odd += [(math.cos(angle), real), (-math.sin(angle), imag)]
            results[place] = base + weighted(odd)
    return results


def hyena_kernel(
    parties,
    query_hbm,
    key_hbm,
    value_hbm,
    taps_hbm,
    skip_hbm,
    spec_hbm,
    fwd_high_hbm,
    fwd_low_hbm,
    bwd_high_hbm,
    bwd_low_hbm,
    out_ref,
    query_ref,
    key_ref,
    value_ref,
    taps_ref,
    skip_ref,
    spec_ref,
    fwd_high,
    fwd_low,
    bwd_high,
    bwd_low,
    edge,
    halo_out,
    halo_query_out,
    halo_in,
    halo_query_in,
    late_out,
    late_in,
    spec_out,
    spec_in,
    scale_out,
    scale_in,
    gated,
    data_out,
    data_in,
    data,
    classes,
    response,
    inverse,
    conv,
    conv_out,
    conv_in,
    conv_scale_out,
    conv_scale_in,
    input_sem,
    table_sem,
    halo_send,
    halo_recv,
    spec_send,
    spec_recv,
    data_send,
    data_recv,
    conv_send,
    conv_recv,
    late_send,
    late_recv,
    relay_send,
    relay_recv,
    scale_send,
    scale_recv,
    conv_scale_send,
    conv_scale_recv,
):
    me = lax.axis_index("ctx")
    plane = lax.axis_index("grp")
    tok_rows, width = query_ref.shape
    owned = width // parties
    chunks, lanes = data_out.shape[0], gated.shape[3]
    group_count = spec_ref.shape[4]
    group_owned = group_count // parties
    group_chunk = group_owned // chunks
    half = tok_rows // 2
    rows = 2 * tok_rows

    barrier = pltpu.get_barrier_semaphore()

    @pl.loop(1, parties)
    def _(step):
        pl.semaphore_signal(
            barrier, inc=1, device_id={"ctx": lax.rem(me + step, parties)}, device_id_type=MESH
        )

    pl.semaphore_signal(barrier, inc=1, device_id={"grp": 1 - plane}, device_id_type=MESH)

    inputs = [
        pltpu.make_async_copy(source, target, input_sem.at[index])
        for index, (source, target) in enumerate(
            (
                (query_hbm.at[tok_rows - 16 :, :], edge.at[0]),
                (key_hbm.at[tok_rows - 16 :, :], edge.at[1]),
                (value_hbm.at[tok_rows - 16 :, :], edge.at[2]),
                (spec_hbm, spec_ref),
                (key_hbm, key_ref),
                (value_hbm, value_ref),
                (taps_hbm, taps_ref),
                (query_hbm, query_ref),
                (skip_hbm, skip_ref),
            )
        )
    ]
    for copy in inputs:
        copy.start()

    for copy in inputs[:3]:
        copy.wait()
    last = edge[...].astype(jnp.float32)[:, 14:16, :]
    halo_out[...] = last[1:].reshape(4, width).astype(jnp.bfloat16)
    halo_query_out[...] = last[0].astype(jnp.bfloat16)
    def halo_copy(source, target, index):
        return pltpu.make_async_remote_copy(
            source,
            target,
            halo_send.at[index],
            halo_recv.at[index],
            device_id={"ctx": lax.rem(me + 1, parties)},
            device_id_type=MESH,
        )

    halo = halo_copy(halo_out, halo_in, 0)
    halo_query = halo_copy(halo_query_out, halo_query_in, 1)

    def spec_copy(target, slot):
        return pltpu.make_async_remote_copy(
            spec_out.at[plane, target],
            spec_in.at[plane, slot],
            spec_send.at[target],
            spec_recv.at[slot],
            device_id={"ctx": target},
            device_id_type=MESH,
        )

    def relay_copy(part, source):
        return pltpu.make_async_remote_copy(
            spec_in.at[part, source],
            spec_in.at[part, source],
            relay_send.at[source],
            relay_recv.at[source],
            device_id={"grp": 1 - plane},
            device_id_type=MESH,
        )

    def scale_copy(target, slot):
        return pltpu.make_async_remote_copy(
            scale_out.at[target],
            scale_in.at[slot],
            scale_send.at[target],
            scale_recv.at[slot],
            device_id={"ctx": target},
            device_id_type=MESH,
        )

    def conv_scale_copy(chunk, target, slot):
        return pltpu.make_async_remote_copy(
            conv_scale_out.at[chunk, target],
            conv_scale_in.at[chunk, slot],
            conv_scale_send.at[chunk, target],
            conv_scale_recv.at[chunk, slot],
            device_id={"ctx": target},
            device_id_type=MESH,
        )

    def data_copy(chunk, target, slot):
        return pltpu.make_async_remote_copy(
            data_out.at[chunk, target],
            data_in.at[chunk, slot],
            data_send.at[chunk, target],
            data_recv.at[chunk, slot],
            device_id={"ctx": target},
            device_id_type=MESH,
        )

    def conv_copy(chunk, target, slot):
        return pltpu.make_async_remote_copy(
            conv_out.at[chunk, target],
            conv_in.at[chunk, slot],
            conv_send.at[chunk, target],
            conv_recv.at[chunk, slot],
            device_id={"ctx": target},
            device_id_type=MESH,
        )

    token = lax.broadcasted_iota(jnp.int32, (tok_rows, lanes), 0)

    def columns_of(target, chunk):
        return pl.ds(pl.multiple_of(target * owned + chunk * lanes, lanes), lanes)

    def rotated(step):
        return lax.rem(me + step + 1, parties)

    def late_copy(target, slot):
        return pltpu.make_async_remote_copy(
            late_out.at[target],
            late_in.at[slot],
            late_send.at[target],
            late_recv.at[slot],
            device_id={"ctx": target},
            device_id_type=MESH,
        )

    def filtered(ref, index, columns, shifted, twice, current):
        taps = taps_ref[index, :, columns]
        return taps[0:1, :] * current + taps[1:2, :] * shifted + taps[2:3, :] * twice

    def inside(ref, index, columns):
        current = ref[:, columns].astype(jnp.float32)
        return filtered(
            ref, index, columns, pltpu.roll(current, 1, 0), pltpu.roll(current, 2, 0), current
        )

    def leading(ref, index, columns, before):
        current = ref[0:16, columns].astype(jnp.float32)[0:2]
        before = before[:, columns].astype(jnp.float32)[2 * index - 2 : 2 * index]
        shifted = jnp.concatenate((before[1:2], current[0:1]), axis=0)
        return filtered(ref, index, columns, shifted, before, current)

    def gate(chunk, target):
        columns = columns_of(target, chunk)
        product = inside(key_ref, 1, columns) * inside(value_ref, 2, columns)
        product = jnp.where(token < 2, jnp.zeros_like(product), product)
        gated[chunk, target] = product
        return product

    for copy in inputs[4:7]:
        copy.wait()

    for chunk in range(chunks):

        @pl.loop(0, parties - 1)
        def _(step, chunk=chunk):
            target = rotated(step)
            product = gate(chunk, target)
            scale = scale_of(product)
            scale_out[target, chunk] = scale
            data_out[chunk, target] = encode(product, scale)

        data[chunk, me] = gate(chunk, me)

    inputs[3].wait()
    packed = jnp.concatenate(
        [spec_ref[part, 0, parity, :half, :] for part in range(2) for parity in range(2)], axis=0
    )
    row_index = lax.broadcasted_iota(jnp.int32, packed.shape, 0)
    highest = spec_ref[0, 0, 0, half : half + 1, :]
    packed = jnp.where((row_index == tok_rows) & (me == 0), highest, packed)
    spec_scale = jnp.max(scale_of(packed), axis=1, keepdims=True)
    for target in range(parties):
        scale_out[target, chunks] = jnp.broadcast_to(spec_scale, (1, lanes))
    codes = packed.T
    codes = encode(codes, spec_scale)
    for part in range(2):
        columns = codes[:, part * tok_rows : (part + 1) * tok_rows]
        spec_out[part] = columns.reshape(spec_out.shape[1:])
        spec_in[part, me] = spec_out[part, me]
    scale_in[me, chunks] = jnp.broadcast_to(spec_scale, (1, lanes))

    pl.semaphore_wait(barrier, parties)


    @pl.when(me < parties - 1)
    def _():
        halo.start()

    @pl.loop(0, parties - 1)
    def _(step):
        target = rotated(step)
        spec_copy(target, me).start()
        scale_copy(target, me).start()

    @pl.loop(0, parties - 1)
    def _(step):
        target = rotated(step)
        data_copy(0, target, me).start()

    tables = [
        pltpu.make_async_copy(source, target, table_sem.at[index])
        for index, (source, target) in enumerate(
            (
                (fwd_high_hbm, fwd_high),
                (fwd_low_hbm, fwd_low),
                (bwd_high_hbm, bwd_high),
                (bwd_low_hbm, bwd_low),
            )
        )
    ]
    for table in tables:
        table.start()


    @pl.when(me > 0)
    def _():
        halo.wait_recv()

    @pl.when(me == 0)
    def _():
        halo_in[...] = jnp.zeros_like(halo_in)
        halo_query_in[...] = jnp.zeros_like(halo_query_in)

    def late(chunk, target):
        columns = columns_of(target, chunk)
        rows = leading(key_ref, 1, columns, halo_in) * leading(value_ref, 2, columns, halo_in)
        gated[chunk, target, 0:2, :] = rows
        return rows

    for chunk in range(chunks):
        data[chunk, me, 0:2, :] = late(chunk, me)

    @pl.loop(0, parties - 1)
    def _(step):
        target = rotated(step)
        for chunk in range(chunks):
            late_out[target, chunk] = late(chunk, target)
        late_copy(target, me).start()

    @pl.when(lax.axis_index("ch") != 1)
    def _():
        for chunk in range(1, chunks):

            @pl.loop(0, parties - 1)
            def _(step, chunk=chunk):
                target = rotated(step)
                data_copy(chunk, target, me).start()

    @pl.when(me < parties - 1)
    def _():
        halo_query.start()

    lane_group = lax.broadcasted_iota(jnp.int32, (3 * group_chunk, lanes), 1) // (
        lanes // group_chunk
    )
    slot_group = lax.broadcasted_iota(jnp.int32, (3 * group_chunk, lanes), 0) % group_chunk
    spread = (lane_group == slot_group).astype(jnp.float32).astype(jnp.bfloat16)

    @pl.loop(1, parties)
    def _(step):
        source = lax.rem(me + parties - step, parties)
        spec_copy(me, source).wait_recv()
        relay_copy(plane, source).start()
        scale_copy(me, source).wait_recv()

    @pl.loop(1, parties)
    def _(step):
        relay_copy(1 - plane, lax.rem(me + parties - step, parties)).wait_recv()

    levels = parties.bit_length() - 1
    row = lax.broadcasted_iota(jnp.int32, (rows, lanes), 0)
    for party in range(parties):
        codes = jnp.concatenate((spec_in[0, party], spec_in[1, party]), axis=1)
        decoded = decode(codes, scale_in[party, chunks, :, :1])
        for chunk in range(chunks):
            exact = decoded[chunk * group_chunk : (chunk + 1) * group_chunk]
            high = exact.astype(jnp.bfloat16).astype(jnp.float32)
            middle = (exact - high).astype(jnp.bfloat16).astype(jnp.float32)
            low = exact - high - middle
            terms = jnp.concatenate((high, middle, low), axis=0).astype(jnp.bfloat16)
            wide = lax.dot_general(
                terms, spread, (((0,), (0,)), ((), ())), preferred_element_type=jnp.float32
            )
            if party == 0:
                ends = lax.rem(row, tok_rows) == 0
                wide = wide * jnp.where(ends, 0.5 / (parties * tok_rows), 1.0 / (parties * tok_rows))
            else:
                wide = wide * (1.0 / (parties * tok_rows))
            for parity in range(2):
                pair, side = place_of(2 * reversed_bits(party, levels) + parity, parties)
                for part in range(2):
                    start = part * tok_rows + parity * half
                    response[chunk, pair, side, part] = wide[start : start + half]

    for table in tables:
        table.wait()

    first = lax.broadcasted_iota(jnp.int32, (half, lanes), 0) == 0
    slab = 16

    for chunk in range(chunks):

        @pl.loop(1, parties, unroll=7)
        def _(step, chunk=chunk):
            source = lax.rem(me + parties - step, parties)
            data_copy(chunk, me, source).wait_recv()
            data[chunk, source] = decode(data_in[chunk, source], scale_in[source, chunk])
            if chunk == 0:
                late_copy(me, source).wait_recv()
            data[chunk, source, 0:2, :] = late_in[source, chunk]

        if chunk + 1 < chunks:

            @pl.when(lax.axis_index("ch") == 1)
            def _(chunk=chunk):

                @pl.loop(0, parties - 1)
                def _(step, chunk=chunk):
                    target = rotated(step)
                    data_copy(chunk + 1, target, me).start()

        @pl.loop(0, tok_rows // slab, unroll=4)
        def _(step, chunk=chunk):
            here = pl.ds(pl.multiple_of(step * slab, slab), slab)
            blocks = [data[chunk, party, here, :] for party in range(parties)]
            for pair, signals in enumerate(class_signals(blocks)):
                for side, signal in enumerate(signals):
                    classes[chunk, pair, side, here, :] = jnp.concatenate(
                        split_terms(signal), axis=1
                    )

        @pl.loop(0, parties, unroll=8)
        def _(pair, chunk=chunk):
            signal = classes[chunk, pair].reshape(rows, 2 * lanes)
            both = jnp.concatenate((fwd_high[pair], fwd_low[pair]), axis=0)
            every = jnp.dot(both, signal, preferred_element_type=jnp.float32)
            wide, rest = every[:rows], every[rows:, :lanes]
            spectrum = wide[:, :lanes] + wide[:, lanes:] + rest
            products = []
            for side in range(2):
                data_re = spectrum[side * tok_rows : side * tok_rows + half]
                data_im = spectrum[side * tok_rows + half : (side + 1) * tok_rows]
                resp_re, resp_im = response[chunk, pair, side, 0], response[chunk, pair, side, 1]
                both_re, both_im = data_re * resp_re, data_im * resp_im
                cross = data_re * resp_im + data_im * resp_re
                if side == 0:
                    alone = first & (pair == 0)
                    products.append(both_re - jnp.where(alone, jnp.zeros_like(both_im), both_im))
                    products.append(jnp.where(alone, both_im, cross))
                else:
                    products += [both_re - both_im, cross]
            product = jnp.concatenate(split_terms(jnp.concatenate(products, axis=0)), axis=1)
            both = jnp.concatenate((bwd_high[pair], bwd_low[pair]), axis=0)
            every = jnp.dot(both, product, preferred_element_type=jnp.float32)
            wide, rest = every[:rows], every[rows:, :lanes]
            result = wide[:, :lanes] + wide[:, lanes:] + rest
            inverse[chunk, pair] = result.reshape(2, tok_rows, lanes)

        @pl.loop(0, tok_rows // slab, unroll=4)
        def _(step, chunk=chunk):
            here = pl.ds(pl.multiple_of(step * slab, slab), slab)
            signals = [
                (inverse[chunk, pair, 0, here, :], inverse[chunk, pair, 1, here, :])
                for pair in range(parties)
            ]
            for party, result in enumerate(block_sums(signals)):
                conv[chunk, party, here, :] = result

        @pl.loop(0, parties - 1, unroll=7)
        def _(step, chunk=chunk):
            target = rotated(step)
            result = conv[chunk, target]
            scale = scale_of(result)
            conv_scale_out[chunk, target] = scale
            conv_out[chunk, target] = encode(result, scale)
            conv_copy(chunk, target, me).start()
            conv_scale_copy(chunk, target, me).start()

    @pl.when(me > 0)
    def _():
        halo_query.wait_recv()

    for copy in inputs[7:]:
        copy.wait()

    def short(ref, index, columns):
        current = ref[:, columns].astype(jnp.float32)
        before = halo_query_in[:, columns].astype(jnp.float32)
        shifted = jnp.where(token == 0, before[1:2, :], pltpu.roll(current, 1, 0))
        twice = jnp.where(token == 0, before[0:1, :], pltpu.roll(current, 2, 0))
        twice = jnp.where(token == 1, before[1:2, :], twice)
        taps = taps_ref[index, :, columns]
        return taps[0:1, :] * current + taps[1:2, :] * shifted + taps[2:3, :] * twice

    def finish(chunk, source, conv):
        columns = columns_of(source, chunk)
        mixed = conv + skip_ref[:, columns] * gated[chunk, source]
        out_ref[:, columns] = (short(query_ref, 0, columns) * mixed).astype(jnp.bfloat16)

    for chunk in range(chunks):
        finish(chunk, me, conv[chunk, me])

        @pl.loop(1, parties, unroll=7)
        def _(step, chunk=chunk):
            source = lax.rem(me + parties - step, parties)
            conv_scale_copy(chunk, me, source).wait_recv()
            conv_copy(chunk, me, source).wait_recv()
            finish(chunk, source, decode(conv_in[chunk, source], conv_scale_in[chunk, source]))

    @pl.when(me < parties - 1)
    def _():
        halo.wait_send()
        halo_query.wait_send()

    @pl.loop(1, parties)
    def _(step):
        target = lax.rem(me + step, parties)
        late_copy(target, me).wait_send()
        spec_copy(target, me).wait_send()
        relay_copy(plane, target).wait_send()
        scale_copy(target, me).wait_send()
        for chunk in range(chunks):
            data_copy(chunk, target, me).wait_send()
            conv_copy(chunk, target, me).wait_send()
            conv_scale_copy(chunk, target, me).wait_send()


def one_kernel(tables, query_in, key_in, value_in, short_filter, skip_bias, filter_spectrum):
    tok_rows, width = query_in.shape
    parties = lax.axis_size("ctx")
    group_count = filter_spectrum.shape[4]
    lanes = 128
    chunks = width // parties // lanes
    vmem = pl.BlockSpec(memory_space=pltpu.VMEM)
    hbm = pl.BlockSpec(memory_space=pltpu.HBM)
    f32, bf16 = jnp.float32, jnp.bfloat16
    dma = pltpu.SemaphoreType.DMA
    return pl.pallas_call(
        functools.partial(hyena_kernel, parties),
        out_shape=pltpu.VMEM((tok_rows, width), bf16),
        in_specs=[hbm] * 10,
        out_specs=vmem,
        scratch_shapes=[
            *[pltpu.VMEM((tok_rows, width), bf16)] * 3,
            pltpu.VMEM(short_filter.shape, f32),
            pltpu.VMEM((1, width), f32),
            pltpu.VMEM(filter_spectrum.shape, f32),
            *[pltpu.VMEM((parties, 2 * tok_rows, 2 * tok_rows), bf16)] * 4,
            pltpu.VMEM((3, 16, width), bf16),
            pltpu.VMEM((4, width), bf16),
            pltpu.VMEM((2, width), bf16),
            pltpu.VMEM((4, width), bf16),
            pltpu.VMEM((2, width), bf16),
            *[pltpu.VMEM((parties, chunks, 2, lanes), f32)] * 2,
            *[pltpu.VMEM((2, parties, group_count // parties, tok_rows), bf16)] * 2,
            *[pltpu.VMEM((parties, chunks + 1, 1, lanes), f32)] * 2,
            pltpu.VMEM((chunks, parties, tok_rows, lanes), f32),
            *[pltpu.VMEM((chunks, parties, tok_rows, lanes), bf16)] * 2,
            pltpu.VMEM((chunks, parties, tok_rows, lanes), f32),
            pltpu.VMEM((chunks, parties, 2, tok_rows, 2 * lanes), bf16),
            pltpu.VMEM((chunks, parties, 2, 2, tok_rows // 2, lanes), f32),
            pltpu.VMEM((chunks, parties, 2, tok_rows, lanes), f32),
            pltpu.VMEM((chunks, parties, tok_rows, lanes), f32),
            *[pltpu.VMEM((chunks, parties, tok_rows, lanes), bf16)] * 2,
            *[pltpu.VMEM((chunks, parties, 1, lanes), f32)] * 2,
            dma((9,)),
            dma((4,)),
            dma((2,)),
            dma((2,)),
            dma((parties,)),
            dma((parties,)),
            *[dma((chunks, parties))] * 4,
            *[dma((parties,))] * 6,
            *[dma((chunks, parties))] * 2,
        ],
        compiler_params=pltpu.CompilerParams(
            collective_id=0, has_side_effects=True, vmem_limit_bytes=56 * 1024 * 1024
        ),
    )(
        query_in,
        key_in,
        value_in,
        short_filter,
        skip_bias.reshape(1, width),
        filter_spectrum,
        *[jnp.asarray(table) for table in tables],
    )


def solution(mesh):
    parties = mesh.shape["ctx"]

    def per_device(*args):
        tok_rows, width = args[0].shape
        if width // parties % 128 == 0 and mesh.shape["grp"] == 2:
            return one_kernel(transform_tables(parties, tok_rows), *args)
        return on_device(*args)

    return jax.shard_map(
        per_device,
        mesh=mesh,
        in_specs=(
            P(("grp", "ctx"), "ch"),
            P(("grp", "ctx"), "ch"),
            P(("grp", "ctx"), "ch"),
            P(None, None, "ch"),
            P("ch"),
            P(None, "ctx", None, None, "ch"),
        ),
        out_specs=P(("grp", "ctx"), "ch"),
        check_vma=False,
    )
```

```python
import functools
import math

import jax
import jax.numpy as jnp
import ml_dtypes
import numpy as np
from jax import lax
from jax.experimental import pallas as pl
from jax.experimental.pallas import tpu as pltpu
from jax.sharding import PartitionSpec as P

HIGHEST = lax.Precision.HIGHEST
MESH = pl.DeviceIdType.MESH
POWER = 17
REACH = 2.0 ** (126 / POWER)


def passed_along(value, axis, steps):
    count = lax.axis_size(axis)
    leading, last = (max(0, -steps), min(count, count - steps))
    return lax.ppermute(value, axis, [(source, source + steps) for source in range(leading, last)])


def reversed_bits(number, digits):
    result = number * 0
    for bit_level in range(digits):
        result = result + (number >> bit_level & 1) * (1 << digits - 1 - bit_level)
    return result


def rotate(real_part, imag_part, cosine, sine):
    return (real_part * cosine - imag_part * sine, real_part * sine + imag_part * cosine)


def complex_product(pattern, table_real, table_imag, data_real, data_imag):
    out_real = jnp.einsum(pattern, table_real, data_real, precision=HIGHEST) - jnp.einsum(
        pattern, table_imag, data_imag, precision=HIGHEST
    )
    out_imag = jnp.einsum(pattern, table_real, data_imag, precision=HIGHEST) + jnp.einsum(
        pattern, table_imag, data_real, precision=HIGHEST
    )
    return (out_real, out_imag)


def angle_table(rows, cols, modulus):
    exponent = (
        jnp.arange(rows, dtype=jnp.int32)[:, None]
        * jnp.arange(cols, dtype=jnp.int32)[None, :]
        % modulus
    )
    angle = 2.0 * math.pi / modulus * exponent.astype(jnp.float32)
    return (jnp.cos(angle), jnp.sin(angle))


def whole_convolution(first_real, first_imag, filter_spectrum, parties, levels):
    tok_rows = first_real.shape[0]
    packed = jnp.stack((first_real, first_imag))
    spread = lax.all_to_all(packed, "ctx", split_axis=2, concat_axis=1, tiled=True)
    spectrum = lax.all_to_all(filter_spectrum, "ctx", split_axis=4, concat_axis=1, tiled=True)
    tail = spectrum.shape[2:]
    spectrum = spectrum.reshape(2, *[2] * levels, *tail)
    spectrum = spectrum.transpose(0, *range(levels, 0, -1), *range(levels + 1, levels + 4))
    spectrum = spectrum.reshape(2, parties, *tail)
    size_b = 2 * parties
    total = tok_rows * size_b
    spectrum = spectrum.reshape(2, size_b, tok_rows, spectrum.shape[4])
    columns = spread.shape[2]
    data = spread.reshape(2, size_b // 2, tok_rows, columns)
    outer_cos, outer_sin = angle_table(size_b, size_b // 2, size_b)
    twist_cos, twist_sin = angle_table(size_b, tok_rows, total)
    inner_cos, inner_sin = angle_table(tok_rows, tok_rows, tok_rows)
    section_real, section_imag = complex_product(
        "fn,nac->fac", outer_cos, -outer_sin, data[0], data[1]
    )
    section_real, section_imag = rotate(
        section_real, section_imag, twist_cos[..., None], -twist_sin[..., None]
    )
    freq_real, freq_imag = complex_product(
        "ak,fac->fkc", inner_cos, -inner_sin, section_real, section_imag
    )
    group_local = spectrum.shape[3]
    per_group = columns // group_local
    shaped_real = freq_real.reshape(size_b, tok_rows, group_local, per_group)
    shaped_imag = freq_imag.reshape(size_b, tok_rows, group_local, per_group)
    resp_real = spectrum[0][..., None]
    resp_imag = spectrum[1][..., None]
    prod_real = (shaped_real * resp_real - shaped_imag * resp_imag).reshape(
        size_b, tok_rows, columns
    )
    prod_imag = (shaped_real * resp_imag + shaped_imag * resp_real).reshape(
        size_b, tok_rows, columns
    )
    back_real, back_imag = complex_product(
        "ak,fkc->fac", inner_cos, inner_sin, prod_real, prod_imag
    )
    back_real, back_imag = rotate(back_real, back_imag, twist_cos[..., None], twist_sin[..., None])
    out_real, out_imag = complex_product(
        "nf,fac->nac", outer_cos.T, outer_sin.T, back_real, back_imag
    )
    norm_factor = 1.0 / total
    result = (
        jnp.stack(
            (
                out_real.reshape(size_b // 2 * tok_rows, columns),
                out_imag.reshape(size_b // 2 * tok_rows, columns),
            )
        )
        * norm_factor
    )
    returned = lax.all_to_all(result, "ctx", split_axis=1, concat_axis=2, tiled=True)
    return (returned[0], returned[1])


def on_device(query_in, key_in, value_in, short_filter, skip_bias, filter_spectrum):
    tok_rows, chan_width = query_in.shape
    parties = lax.axis_size("ctx")
    levels = parties.bit_length() - 1
    tap_count = short_filter.shape[1]
    group_count = filter_spectrum.shape[4]
    half_group = chan_width // (2 * group_count)
    packed_width = group_count * half_group
    stacked = jnp.stack((query_in, key_in, value_in))
    earlier = passed_along(stacked[:, tok_rows - (tap_count - 1) :, :], "ctx", 1)
    extended = jnp.concatenate((earlier, stacked), axis=1).astype(jnp.float32)
    filtered = short_filter[:, 0, None, :] * extended[:, tap_count - 1 :, :]
    for tap_lag in range(1, tap_count):
        start_row = tap_count - 1 - tap_lag
        filtered = (
            filtered
            + short_filter[:, tap_lag, None, :] * extended[:, start_row : start_row + tok_rows, :]
        )
    gated = filtered[1] * filtered[2]
    halves = gated.reshape(tok_rows, group_count, 2, half_group)
    first_real = halves[:, :, 0, :].reshape(tok_rows, packed_width)
    first_imag = halves[:, :, 1, :].reshape(tok_rows, packed_width)
    conv_real, conv_imag = whole_convolution(
        first_real, first_imag, filter_spectrum, parties, levels
    )
    conv = jnp.stack(
        (
            conv_real.reshape(tok_rows, group_count, half_group),
            conv_imag.reshape(tok_rows, group_count, half_group),
        ),
        axis=2,
    ).reshape(tok_rows, chan_width)
    return (filtered[0] * (conv + skip_bias[None, :] * gated)).astype(jnp.bfloat16)


def split_terms(value):
    high = value.astype(jnp.bfloat16)
    low = (value - high.astype(jnp.float32)).astype(jnp.bfloat16)
    return high, low


def scale_of(value):
    peak = jnp.max(jnp.abs(value), axis=0, keepdims=True)
    return jnp.maximum(peak * 1.0078125, 2.0**-100)


def encode(value, scale):
    ratio = value * (REACH / scale)
    square = ratio * ratio
    fourth = square * square
    eighth = fourth * fourth
    return (ratio * (eighth * eighth)).astype(jnp.bfloat16)


def decode(block, scale):
    code = block.astype(jnp.float32)
    root = jnp.exp(jnp.log(jnp.maximum(jnp.abs(code), 2.0**-126)) * (1.0 / POWER))
    root = root * (scale * (1.0 / REACH))
    return jnp.where(code < 0, -root, jnp.where(code > 0, root, jnp.zeros_like(root)))


def place_of(rho, parties):
    if rho % parties == 0:
        return 0, rho // parties
    return (rho, 0) if rho < parties else (2 * parties - rho, 1)


def transform_tables(parties, tok_rows):
    classes, half = 2 * parties, tok_rows // 2
    total = classes * tok_rows
    time = np.arange(tok_rows)
    table = np.zeros((parties, 2, 2, half, 2, tok_rows))
    for rho in range(classes):
        pair, side = place_of(rho, parties)
        angle = 2.0 * np.pi / total * ((classes * np.arange(half)[:, None] + rho) * time % total)
        cosine, sine = np.cos(angle), np.sin(angle)
        if pair == 0:
            table[pair, side, 0, :, side] = cosine
            table[pair, side, 1, :, side] = -sine
        else:
            sign = 1.0 - 2.0 * side
            table[pair, side, 0, :, 0] = cosine
            table[pair, side, 0, :, 1] = sign * sine
            table[pair, side, 1, :, 0] = -sine
            table[pair, side, 1, :, 1] = sign * cosine
    table[0, 0, 1, 0, 0] = 1.0 - 2.0 * (time % 2)
    forward = table.reshape(parties, 2 * tok_rows, 2 * tok_rows)

    def parts(matrix):
        high = matrix.astype(ml_dtypes.bfloat16)
        low = (matrix - high.astype(np.float64)).astype(ml_dtypes.bfloat16)
        return high, low

    return parts(forward) + parts(np.ascontiguousarray(forward.transpose(0, 2, 1)))


def weighted(terms):
    result = None
    for weight, value in terms:
        if abs(weight) < 1e-12:
            continue
        if abs(abs(weight) - 1.0) > 1e-12:
            term = value * abs(weight)
        else:
            term = value
        if result is None:
            result = term if weight > 0 else -term
        else:
            result = result + term if weight > 0 else result - term
    return result


def class_signals(blocks):
    parties = len(blocks)
    middle = parties // 2
    sums = [blocks[i] + blocks[i + middle] for i in range(middle)]
    gaps = [blocks[i] - blocks[i + middle] for i in range(middle)]
    signals = []
    for pair in range(parties):
        if pair == 0:
            even = weighted([(1.0, sums[i]) for i in range(0, middle, 2)])
            odd = weighted([(1.0, sums[i]) for i in range(1, middle, 2)])
            signals.append((even + odd, even - odd))
            continue
        used = blocks if pair % 2 else (sums if pair % 4 == 0 else gaps)
        angles = [math.pi * pair * i / parties for i in range(len(used))]
        real = weighted([(math.cos(a), v) for a, v in zip(angles, used)])
        imag = weighted([(-math.sin(a), v) for a, v in zip(angles, used)])
        signals.append((real, imag))
    return signals


def block_sums(signals):
    parties = len(signals)
    middle = parties // 2
    results = [None] * parties
    for i in range(middle):
        even = {0: [], 2: []}
        for pair in range(0, parties, 2):
            angle = math.pi * pair * i / parties
            real, imag = signals[pair]
            if pair == 0:
                even[0] += [(1.0, real), (1.0 - 2.0 * (i % 2), imag)]
            else:
                even[pair % 4] += [(math.cos(angle), real), (-math.sin(angle), imag)]
        same, flipped = weighted(even[0]), weighted(even[2])
        for place, base in ((i, same + flipped), (i + middle, same - flipped)):
            odd = []
            for pair in range(1, parties, 2):
                angle = math.pi * pair * place / parties
                real, imag = signals[pair]
                odd += [(math.cos(angle), real), (-math.sin(angle), imag)]
            results[place] = base + weighted(odd)
    return results


def hyena_kernel(
    parties,
    query_hbm,
    key_hbm,
    value_hbm,
    taps_hbm,
    skip_hbm,
    spec_hbm,
    fwd_high_hbm,
    fwd_low_hbm,
    bwd_high_hbm,
    bwd_low_hbm,
    out_ref,
    query_ref,
    key_ref,
    value_ref,
    taps_ref,
    skip_ref,
    spec_ref,
    fwd_high,
    fwd_low,
    bwd_high,
    bwd_low,
    edge,
    halo_out,
    halo_query_out,
    halo_in,
    halo_query_in,
    late_out,
    late_in,
    spec_out,
    spec_in,
    scale_out,
    scale_in,
    gated,
    data_out,
    data_in,
    data,
    classes,
    response,
    inverse,
    conv,
    conv_out,
    conv_in,
    conv_scale_out,
    conv_scale_in,
    input_sem,
    table_sem,
    halo_send,
    halo_recv,
    spec_send,
    spec_recv,
    data_send,
    data_recv,
    conv_send,
    conv_recv,
    late_send,
    late_recv,
    relay_send,
    relay_recv,
    scale_send,
    scale_recv,
    conv_scale_send,
    conv_scale_recv,
):
    me = lax.axis_index("ctx")
    plane = lax.axis_index("grp")
    tok_rows, width = query_ref.shape
    owned = width // parties
    chunks, lanes = data_out.shape[0], gated.shape[3]
    group_count = spec_ref.shape[4]
    group_owned = group_count // parties
    group_chunk = group_owned // chunks
    half = tok_rows // 2
    rows = 2 * tok_rows

    barrier = pltpu.get_barrier_semaphore()

    @pl.loop(1, parties)
    def _(step):
        pl.semaphore_signal(
            barrier, inc=1, device_id={"ctx": lax.rem(me + step, parties)}, device_id_type=MESH
        )

    pl.semaphore_signal(barrier, inc=1, device_id={"grp": 1 - plane}, device_id_type=MESH)

    inputs = [
        pltpu.make_async_copy(source, target, input_sem.at[index])
        for index, (source, target) in enumerate(
            (
                (query_hbm.at[tok_rows - 16 :, :], edge.at[0]),
                (key_hbm.at[tok_rows - 16 :, :], edge.at[1]),
                (value_hbm.at[tok_rows - 16 :, :], edge.at[2]),
                (spec_hbm, spec_ref),
                (key_hbm, key_ref),
                (value_hbm, value_ref),
                (taps_hbm, taps_ref),
                (query_hbm, query_ref),
                (skip_hbm, skip_ref),
            )
        )
    ]
    for copy in inputs:
        copy.start()

    for copy in inputs[:3]:
        copy.wait()
    last = edge[...].astype(jnp.float32)[:, 14:16, :]
    halo_out[...] = last[1:].reshape(4, width).astype(jnp.bfloat16)
    halo_query_out[...] = last[0].astype(jnp.bfloat16)
    def halo_copy(source, target, index):
        return pltpu.make_async_remote_copy(
            source,
            target,
            halo_send.at[index],
            halo_recv.at[index],
            device_id={"ctx": lax.rem(me + 1, parties)},
            device_id_type=MESH,
        )

    halo = halo_copy(halo_out, halo_in, 0)
    halo_query = halo_copy(halo_query_out, halo_query_in, 1)

    def spec_copy(target, slot):
        return pltpu.make_async_remote_copy(
            spec_out.at[plane, target],
            spec_in.at[plane, slot],
            spec_send.at[target],
            spec_recv.at[slot],
            device_id={"ctx": target},
            device_id_type=MESH,
        )

    def relay_copy(part, source):
        return pltpu.make_async_remote_copy(
            spec_in.at[part, source],
            spec_in.at[part, source],
            relay_send.at[source],
            relay_recv.at[source],
            device_id={"grp": 1 - plane},
            device_id_type=MESH,
        )

    def scale_copy(target, slot):
        return pltpu.make_async_remote_copy(
            scale_out.at[target],
            scale_in.at[slot],
            scale_send.at[target],
            scale_recv.at[slot],
            device_id={"ctx": target},
            device_id_type=MESH,
        )

    def conv_scale_copy(chunk, target, slot):
        return pltpu.make_async_remote_copy(
            conv_scale_out.at[chunk, target],
            conv_scale_in.at[chunk, slot],
            conv_scale_send.at[chunk, target],
            conv_scale_recv.at[chunk, slot],
            device_id={"ctx": target},
            device_id_type=MESH,
        )

    def data_copy(chunk, target, slot):
        return pltpu.make_async_remote_copy(
            data_out.at[chunk, target],
            data_in.at[chunk, slot],
            data_send.at[chunk, target],
            data_recv.at[chunk, slot],
            device_id={"ctx": target},
            device_id_type=MESH,
        )

    def conv_copy(chunk, target, slot):
        return pltpu.make_async_remote_copy(
            conv_out.at[chunk, target],
            conv_in.at[chunk, slot],
            conv_send.at[chunk, target],
            conv_recv.at[chunk, slot],
            device_id={"ctx": target},
            device_id_type=MESH,
        )

    token = lax.broadcasted_iota(jnp.int32, (tok_rows, lanes), 0)

    def columns_of(target, chunk):
        return pl.ds(pl.multiple_of(target * owned + chunk * lanes, lanes), lanes)

    def rotated(step):
        return lax.rem(me + step + 1, parties)

    def early_first(step):
        place = me + step
        place = place - (parties - 1) * jnp.int32(place >= parties)
        place = place * jnp.int32(step > 0)
        lead = jnp.int32(me == 0)
        return lead * (step + 1) + (1 - lead) * place

    def late_copy(target, slot):
        return pltpu.make_async_remote_copy(
            late_out.at[target],
            late_in.at[slot],
            late_send.at[target],
            late_recv.at[slot],
            device_id={"ctx": target},
            device_id_type=MESH,
        )

    def filtered(ref, index, columns, shifted, twice, current):
        taps = taps_ref[index, :, columns]
        return taps[0:1, :] * current + taps[1:2, :] * shifted + taps[2:3, :] * twice

    def inside(ref, index, columns):
        current = ref[:, columns].astype(jnp.float32)
        return filtered(
            ref, index, columns, pltpu.roll(current, 1, 0), pltpu.roll(current, 2, 0), current
        )

    def leading(ref, index, columns, before):
        current = ref[0:16, columns].astype(jnp.float32)[0:2]
        before = before[:, columns].astype(jnp.float32)[2 * index - 2 : 2 * index]
        shifted = jnp.concatenate((before[1:2], current[0:1]), axis=0)
        return filtered(ref, index, columns, shifted, before, current)

    def gate(chunk, target):
        columns = columns_of(target, chunk)
        product = inside(key_ref, 1, columns) * inside(value_ref, 2, columns)
        product = jnp.where(token < 2, jnp.zeros_like(product), product)
        gated[chunk, target] = product
        return product

    for copy in inputs[4:7]:
        copy.wait()

    for chunk in range(chunks):

        @pl.loop(0, parties - 1)
        def _(step, chunk=chunk):
            target = rotated(step)
            product = gate(chunk, target)
            scale = scale_of(product)
            scale_out[target, chunk] = scale
            data_out[chunk, target] = encode(product, scale)

        data[chunk, me] = gate(chunk, me)

    inputs[3].wait()
    packed = jnp.concatenate(
        [spec_ref[part, 0, parity, :half, :] for part in range(2) for parity in range(2)], axis=0
    )
    row_index = lax.broadcasted_iota(jnp.int32, packed.shape, 0)
    highest = spec_ref[0, 0, 0, half : half + 1, :]
    packed = jnp.where((row_index == tok_rows) & (me == 0), highest, packed)
    spec_scale = jnp.max(scale_of(packed), axis=1, keepdims=True)
    for target in range(parties):
        scale_out[target, chunks] = jnp.broadcast_to(spec_scale, (1, lanes))
    codes = packed.T
    codes = encode(codes, spec_scale)
    for part in range(2):
        columns = codes[:, part * tok_rows : (part + 1) * tok_rows]
        spec_out[part] = columns.reshape(spec_out.shape[1:])
        spec_in[part, me] = spec_out[part, me]
    scale_in[me, chunks] = jnp.broadcast_to(spec_scale, (1, lanes))

    pl.semaphore_wait(barrier, parties)


    @pl.when(me < parties - 1)
    def _():
        halo.start()

    @pl.loop(0, parties - 1)
    def _(step):
        target = rotated(step)
        spec_copy(target, me).start()
        scale_copy(target, me).start()

    @pl.loop(0, parties - 1)
    def _(step):
        target = rotated(step)
        data_copy(0, target, me).start()

    tables = [
        pltpu.make_async_copy(source, target, table_sem.at[index])
        for index, (source, target) in enumerate(
            (
                (fwd_high_hbm, fwd_high),
                (fwd_low_hbm, fwd_low),
                (bwd_high_hbm, bwd_high),
                (bwd_low_hbm, bwd_low),
            )
        )
    ]
    for table in tables:
        table.start()


    @pl.when(me > 0)
    def _():
        halo.wait_recv()

    @pl.when(me == 0)
    def _():
        halo_in[...] = jnp.zeros_like(halo_in)
        halo_query_in[...] = jnp.zeros_like(halo_query_in)

    def late(chunk, target):
        columns = columns_of(target, chunk)
        rows = leading(key_ref, 1, columns, halo_in) * leading(value_ref, 2, columns, halo_in)
        gated[chunk, target, 0:2, :] = rows
        return rows

    for chunk in range(chunks):
        data[chunk, me, 0:2, :] = late(chunk, me)

    @pl.loop(0, parties - 1)
    def _(step):
        target = rotated(step)
        for chunk in range(chunks):
            late_out[target, chunk] = late(chunk, target)
        late_copy(target, me).start()

    @pl.when(lax.axis_index("ch") != 1)
    def _():
        for chunk in range(1, chunks):

            @pl.loop(0, parties - 1)
            def _(step, chunk=chunk):
                target = rotated(step)
                data_copy(chunk, target, me).start()

    @pl.when(me < parties - 1)
    def _():
        halo_query.start()

    lane_group = lax.broadcasted_iota(jnp.int32, (3 * group_chunk, lanes), 1) // (
        lanes // group_chunk
    )
    slot_group = lax.broadcasted_iota(jnp.int32, (3 * group_chunk, lanes), 0) % group_chunk
    spread = (lane_group == slot_group).astype(jnp.float32).astype(jnp.bfloat16)

    @pl.loop(1, parties)
    def _(step):
        source = lax.rem(me + parties - step, parties)
        spec_copy(me, source).wait_recv()
        relay_copy(plane, source).start()
        scale_copy(me, source).wait_recv()

    @pl.loop(1, parties)
    def _(step):
        relay_copy(1 - plane, lax.rem(me + parties - step, parties)).wait_recv()

    levels = parties.bit_length() - 1
    row = lax.broadcasted_iota(jnp.int32, (rows, lanes), 0)
    for party in range(parties):
        codes = jnp.concatenate((spec_in[0, party], spec_in[1, party]), axis=1)
        decoded = decode(codes, scale_in[party, chunks, :, :1])
        for chunk in range(chunks):
            exact = decoded[chunk * group_chunk : (chunk + 1) * group_chunk]
            high = exact.astype(jnp.bfloat16).astype(jnp.float32)
            middle = (exact - high).astype(jnp.bfloat16).astype(jnp.float32)
            low = exact - high - middle
            terms = jnp.concatenate((high, middle, low), axis=0).astype(jnp.bfloat16)
            wide = lax.dot_general(
                terms, spread, (((0,), (0,)), ((), ())), preferred_element_type=jnp.float32
            )
            if party == 0:
                ends = lax.rem(row, tok_rows) == 0
                wide = wide * jnp.where(ends, 0.5 / (parties * tok_rows), 1.0 / (parties * tok_rows))
            else:
                wide = wide * (1.0 / (parties * tok_rows))
            for parity in range(2):
                pair, side = place_of(2 * reversed_bits(party, levels) + parity, parties)
                for part in range(2):
                    start = part * tok_rows + parity * half
                    response[chunk, pair, side, part] = wide[start : start + half]

    for table in tables:
        table.wait()

    first = lax.broadcasted_iota(jnp.int32, (half, lanes), 0) == 0
    slab = 16

    for chunk in range(chunks):

        @pl.loop(1, parties, unroll=7)
        def _(step, chunk=chunk):
            source = lax.rem(me + parties - step, parties)
            data_copy(chunk, me, source).wait_recv()
            data[chunk, source] = decode(data_in[chunk, source], scale_in[source, chunk])
            if chunk == 0:
                late_copy(me, source).wait_recv()
            data[chunk, source, 0:2, :] = late_in[source, chunk]

        if chunk + 1 < chunks:

            @pl.when(lax.axis_index("ch") == 1)
            def _(chunk=chunk):

                @pl.loop(0, parties - 1)
                def _(step, chunk=chunk):
                    target = rotated(step)
                    data_copy(chunk + 1, target, me).start()

        @pl.loop(0, tok_rows // slab, unroll=4)
        def _(step, chunk=chunk):
            here = pl.ds(pl.multiple_of(step * slab, slab), slab)
            blocks = [data[chunk, party, here, :] for party in range(parties)]
            for pair, signals in enumerate(class_signals(blocks)):
                for side, signal in enumerate(signals):
                    classes[chunk, pair, side, here, :] = jnp.concatenate(
                        split_terms(signal), axis=1
                    )

        @pl.loop(0, parties, unroll=8)
        def _(pair, chunk=chunk):
            signal = classes[chunk, pair].reshape(rows, 2 * lanes)
            both = jnp.concatenate((fwd_high[pair], fwd_low[pair]), axis=0)
            every = jnp.dot(both, signal, preferred_element_type=jnp.float32)
            wide, rest = every[:rows], every[rows:, :lanes]
            spectrum = wide[:, :lanes] + wide[:, lanes:] + rest
            products = []
            for side in range(2):
                data_re = spectrum[side * tok_rows : side * tok_rows + half]
                data_im = spectrum[side * tok_rows + half : (side + 1) * tok_rows]
                resp_re, resp_im = response[chunk, pair, side, 0], response[chunk, pair, side, 1]
                both_re, both_im = data_re * resp_re, data_im * resp_im
                cross = data_re * resp_im + data_im * resp_re
                if side == 0:
                    alone = first & (pair == 0)
                    products.append(both_re - jnp.where(alone, jnp.zeros_like(both_im), both_im))
                    products.append(jnp.where(alone, both_im, cross))
                else:
                    products += [both_re - both_im, cross]
            product = jnp.concatenate(split_terms(jnp.concatenate(products, axis=0)), axis=1)
            both = jnp.concatenate((bwd_high[pair], bwd_low[pair]), axis=0)
            every = jnp.dot(both, product, preferred_element_type=jnp.float32)
            wide, rest = every[:rows], every[rows:, :lanes]
            result = wide[:, :lanes] + wide[:, lanes:] + rest
            inverse[chunk, pair] = result.reshape(2, tok_rows, lanes)

        @pl.loop(0, tok_rows // slab, unroll=4)
        def _(step, chunk=chunk):
            here = pl.ds(pl.multiple_of(step * slab, slab), slab)
            signals = [
                (inverse[chunk, pair, 0, here, :], inverse[chunk, pair, 1, here, :])
                for pair in range(parties)
            ]
            for party, result in enumerate(block_sums(signals)):
                conv[chunk, party, here, :] = result

        @pl.loop(0, parties - 1, unroll=7)
        def _(step, chunk=chunk):
            target = early_first(step)
            result = conv[chunk, target]
            scale = scale_of(result)
            conv_scale_out[chunk, target] = scale
            conv_out[chunk, target] = encode(result, scale)
            conv_copy(chunk, target, me).start()
            conv_scale_copy(chunk, target, me).start()

    @pl.when(me > 0)
    def _():
        halo_query.wait_recv()

    for copy in inputs[7:]:
        copy.wait()

    def short(ref, index, columns):
        current = ref[:, columns].astype(jnp.float32)
        before = halo_query_in[:, columns].astype(jnp.float32)
        shifted = jnp.where(token == 0, before[1:2, :], pltpu.roll(current, 1, 0))
        twice = jnp.where(token == 0, before[0:1, :], pltpu.roll(current, 2, 0))
        twice = jnp.where(token == 1, before[1:2, :], twice)
        taps = taps_ref[index, :, columns]
        return taps[0:1, :] * current + taps[1:2, :] * shifted + taps[2:3, :] * twice

    def finish(chunk, source, conv):
        columns = columns_of(source, chunk)
        mixed = conv + skip_ref[:, columns] * gated[chunk, source]
        out_ref[:, columns] = (short(query_ref, 0, columns) * mixed).astype(jnp.bfloat16)

    for chunk in range(chunks):
        finish(chunk, me, conv[chunk, me])

        @pl.loop(1, parties, unroll=7)
        def _(step, chunk=chunk):
            source = lax.rem(me + parties - step, parties)
            conv_scale_copy(chunk, me, source).wait_recv()
            conv_copy(chunk, me, source).wait_recv()
            finish(chunk, source, decode(conv_in[chunk, source], conv_scale_in[chunk, source]))

    @pl.when(me < parties - 1)
    def _():
        halo.wait_send()
        halo_query.wait_send()

    @pl.loop(1, parties)
    def _(step):
        target = lax.rem(me + step, parties)
        late_copy(target, me).wait_send()
        spec_copy(target, me).wait_send()
        relay_copy(plane, target).wait_send()
        scale_copy(target, me).wait_send()
        for chunk in range(chunks):
            data_copy(chunk, target, me).wait_send()
            conv_copy(chunk, target, me).wait_send()
            conv_scale_copy(chunk, target, me).wait_send()


def one_kernel(tables, query_in, key_in, value_in, short_filter, skip_bias, filter_spectrum):
    tok_rows, width = query_in.shape
    parties = lax.axis_size("ctx")
    group_count = filter_spectrum.shape[4]
    lanes = 128
    chunks = width // parties // lanes
    vmem = pl.BlockSpec(memory_space=pltpu.VMEM)
    hbm = pl.BlockSpec(memory_space=pltpu.HBM)
    f32, bf16 = jnp.float32, jnp.bfloat16
    dma = pltpu.SemaphoreType.DMA
    return pl.pallas_call(
        functools.partial(hyena_kernel, parties),
        out_shape=pltpu.VMEM((tok_rows, width), bf16),
        in_specs=[hbm] * 10,
        out_specs=vmem,
        scratch_shapes=[
            *[pltpu.VMEM((tok_rows, width), bf16)] * 3,
            pltpu.VMEM(short_filter.shape, f32),
            pltpu.VMEM((1, width), f32),
            pltpu.VMEM(filter_spectrum.shape, f32),
            *[pltpu.VMEM((parties, 2 * tok_rows, 2 * tok_rows), bf16)] * 4,
            pltpu.VMEM((3, 16, width), bf16),
            pltpu.VMEM((4, width), bf16),
            pltpu.VMEM((2, width), bf16),
            pltpu.VMEM((4, width), bf16),
            pltpu.VMEM((2, width), bf16),
            *[pltpu.VMEM((parties, chunks, 2, lanes), f32)] * 2,
            *[pltpu.VMEM((2, parties, group_count // parties, tok_rows), bf16)] * 2,
            *[pltpu.VMEM((parties, chunks + 1, 1, lanes), f32)] * 2,
            pltpu.VMEM((chunks, parties, tok_rows, lanes), f32),
            *[pltpu.VMEM((chunks, parties, tok_rows, lanes), bf16)] * 2,
            pltpu.VMEM((chunks, parties, tok_rows, lanes), f32),
            pltpu.VMEM((chunks, parties, 2, tok_rows, 2 * lanes), bf16),
            pltpu.VMEM((chunks, parties, 2, 2, tok_rows // 2, lanes), f32),
            pltpu.VMEM((chunks, parties, 2, tok_rows, lanes), f32),
            pltpu.VMEM((chunks, parties, tok_rows, lanes), f32),
            *[pltpu.VMEM((chunks, parties, tok_rows, lanes), bf16)] * 2,
            *[pltpu.VMEM((chunks, parties, 1, lanes), f32)] * 2,
            dma((9,)),
            dma((4,)),
            dma((2,)),
            dma((2,)),
            dma((parties,)),
            dma((parties,)),
            *[dma((chunks, parties))] * 4,
            *[dma((parties,))] * 6,
            *[dma((chunks, parties))] * 2,
        ],
        compiler_params=pltpu.CompilerParams(
            collective_id=0, has_side_effects=True, vmem_limit_bytes=56 * 1024 * 1024
        ),
    )(
        query_in,
        key_in,
        value_in,
        short_filter,
        skip_bias.reshape(1, width),
        filter_spectrum,
        *[jnp.asarray(table) for table in tables],
    )


def solution(mesh):
    parties = mesh.shape["ctx"]

    def per_device(*args):
        tok_rows, width = args[0].shape
        if width // parties % 128 == 0 and mesh.shape["grp"] == 2:
            return one_kernel(transform_tables(parties, tok_rows), *args)
        return on_device(*args)

    return jax.shard_map(
        per_device,
        mesh=mesh,
        in_specs=(
            P(("grp", "ctx"), "ch"),
            P(("grp", "ctx"), "ch"),
            P(("grp", "ctx"), "ch"),
            P(None, None, "ch"),
            P("ch"),
            P(None, "ctx", None, None, "ch"),
        ),
        out_specs=P(("grp", "ctx"), "ch"),
        check_vma=False,
    )
```
